32 devices in a mesh: batch: 16 (over z, y, core), head: 2 (over x).
Axes of the slice: x: 2, y: 2, z: 4, core: 2. Of those that a mesh axis runs over, the one named last changes fastest.
Arguments:
- atoms: bfloat16 [16384, 512], P(('batch', 'head')), may hold values from -6 to 6
- pair: bfloat16 [64, 64, 256, 256], P('batch', 'head'), may hold values from -6 to 6
- counts: int32 [64], P('batch'), may hold values from 64 to 256, as said below
- qkv_weight: bfloat16 [3, 512, 512], P(None, 'batch', 'head'), may hold values from -0.25 to 0.25
- out_weight: bfloat16 [512, 512], P('batch', 'head'), may hold values from -2 to 2
- ln1_gain: float32 [512], P(('batch', 'head')), may hold values from 0.5 to 1.5
- ln2_gain: float32 [512], P(('batch', 'head')), may hold values from 0.5 to 1.5
- w_in: bfloat16 [512, 2048], P(('batch', 'head')), may hold values from -0.25 to 0.25
- w_out: bfloat16 [2048, 512], P(('batch', 'head')), may hold values from -0.125 to 0.125
- out_cot: bfloat16 [16384, 512], P(('batch', 'head')), may hold values from -6 to 6
- pair_cot: bfloat16 [64, 64, 256, 256], P('batch', 'head'), may hold values from -6 to 6
Outputs:
- output: bfloat16 [16384, 512], P(('batch', 'head'))
- new_pair: bfloat16 [64, 64, 256, 256], P('batch', 'head')
- atoms_grad: bfloat16 [16384, 512], P(('batch', 'head'))
- pair_grad: bfloat16 [64, 64, 256, 256], P('batch', 'head')
- qkv_weight_grad: float32 [3, 512, 512], P(None, 'batch', 'head')
- out_weight_grad: float32 [512, 512], P('batch', 'head')
- ln1_gain_grad: float32 [512], P(('batch', 'head'))
- ln2_gain_grad: float32 [512], P(('batch', 'head'))
- w_in_grad: float32 [512, 2048], P(('batch', 'head'))
- w_out_grad: float32 [2048, 512], P(('batch', 'head'))
The draws below stay inside these ranges and needn't reach their ends.
Inputs may be any that keep to these rules, and one draw needn't show every extreme that they name: `counts`: atoms of each molecule; the first molecule has exactly 256.
All inputs are finite; a program needn't handle non-finite values.
Results may differ from the reference program's by a relative error of at most 0.03.
Values may be sent and summed in bfloat16 or wider, within the bound.
No kernel may reach another device: no remote copies, remote signals or barrier semaphores. Data moves between devices by JAX's collectives and lax.ppermute only.
A program may use at most 256 MiB of HBM per device.

```python
import jax
import jax.numpy as jnp
from jax import lax

D = 512
FF = 2048
HEADS = 64
L = 256
MOL_DEV = 4
HEAD_DIM = 8
MOLS = 64
TOKENS = 16384


def draw_counts(key, part):
    split_keys = jax.random.split(jax.random.fold_in(key, 7), 3)
    hydrogen = jax.random.randint(split_keys[0], (MOLS,), 0, 2)
    heavy_only = jax.random.randint(split_keys[1], (MOLS,), L // 4, L // 2 + 1)
    with_hydrogen = jax.random.randint(split_keys[2], (MOLS,), L // 2, L + 1)
    atom_counts = jnp.where(hydrogen == 1, with_hydrogen, heavy_only)
    return atom_counts.at[0].set(L).astype(jnp.int32)


def level_of(own_key, dims, pieces, least, top_value):
    loudness, own = 1.0, jax.random.fold_in(own_key, 6)
    for dim, blocks in pieces:
        draws = jnp.exp(jax.random.uniform(jax.random.fold_in(own, dim), (blocks,), jnp.float32, least / len(pieces), top_value / len(pieces)))
        loudness = loudness * jnp.repeat(draws, dims[dim] // blocks).reshape([-1 if axis == dim else 1 for axis in range(len(dims))])
    return loudness


def centred(key, extent, scale, reach, shards=(), held_as=jnp.bfloat16):
    level = level_of(key, extent, shards, -0.22, 0.18) if shards else 1.0
    values = jax.random.normal(key, extent, jnp.float32) * scale * level
    return jnp.minimum(jnp.maximum(values, -reach), reach).astype(held_as)


def setup_inputs(seed: int = 0) -> dict:
    key_list = jax.random.split(jax.random.key(seed), 12)
    atoms = centred(key_list[0], (TOKENS, D), 1.0, 6.0, ((0, 32),))
    pair = centred(key_list[1], (MOLS, HEADS, L, L), 1.0, 6.0, ((0, 16), (1, 2)))
    counts = draw_counts(jax.random.fold_in(key_list[11], 71), 0)
    qkv_weight = centred(key_list[3], (3, D, D), D ** -0.5, 0.25, ((1, 16), (2, 2)))
    out_weight = centred(key_list[4], (D, D), (D // 48) ** -0.5, 2.0, ((0, 16), (1, 2)))
    ln1_gain = jnp.clip(1.0 + 0.1 * jax.random.normal(key_list[5], (D,), jnp.float32), 0.5, 1.5)
    ln2_gain = jnp.clip(1.0 + 0.1 * jax.random.normal(key_list[6], (D,), jnp.float32), 0.5, 1.5)
    w_in = centred(key_list[7], (D, FF), D ** -0.5, 0.25, ((0, 32),))
    w_out = centred(key_list[8], (FF, D), FF ** -0.5, 0.125, ((0, 32),))
    out_cot = centred(key_list[9], (TOKENS, D), 1.0, 6.0, ((0, 32),))
    pair_cot = centred(key_list[10], (MOLS, HEADS, L, L), 1.0, 6.0, ((0, 16), (1, 2)))
    return {"atoms": atoms, "pair": pair, "counts": counts, "qkv_weight": qkv_weight, "out_weight": out_weight, "ln1_gain": ln1_gain, "ln2_gain": ln2_gain, "w_in": w_in, "w_out": w_out, "out_cot": out_cot, "pair_cot": pair_cot}


@jax.custom_vjp
def low(v):
    return lax.optimization_barrier(v.astype(jnp.bfloat16)).astype(jnp.float32)

@jax.custom_vjp
def low_back(v):
    return v

def low_keep(v):
    return (low(v), None)

def low_pass(kept, grad):
    return (grad,)

def back_keep(v):
    return (v, None)

def back_low(kept, grad):
    return (low(grad),)
low.defvjp(low_keep, low_pass)
low_back.defvjp(back_keep, back_low)

def layer_norm(values):
    center = values - lax.optimization_barrier(jnp.mean(values, -1, keepdims=True))
    return center * lax.rsqrt(lax.optimization_barrier(jnp.mean(center * center, -1, keepdims=True)) + 1e-05)

def product(left, right):
    return jnp.dot(left, right, precision=lax.Precision.HIGHEST)

def attend(inputs):
    query_part, key_part, value_part, pair_part, count_part = inputs
    positions = jnp.arange(L, dtype=jnp.int32)
    valid_rows = positions[None, :] < count_part[:, None]
    both_valid = valid_rows[:, None, :, None] & valid_rows[:, None, None, :]
    logits = jnp.einsum('mqhd,mkhd->mhqk', query_part, key_part, precision=lax.Precision.HIGHEST) * HEAD_DIM ** (-0.5) + pair_part
    logits = low_back(logits)
    new_pair = jnp.where(both_valid, logits, 0.0)
    masked = jnp.where(valid_rows[:, None, None, :], logits, -1e+30)
    probs = jax.nn.softmax(masked, axis=-1)
    mixed = jnp.einsum('mhqk,mkhd->mqhd', low(probs), value_part, precision=lax.Precision.HIGHEST)
    mixed = jnp.where(valid_rows[:, :, None, None], mixed, 0.0)
    return (new_pair, mixed)

def forward(atoms_f, pair_f, counts, qkv_f, out_f, gain_one, gain_two, inner_f, outer_f):
    hidden_one = low(layer_norm(atoms_f) * gain_one)
    projected = jnp.einsum('rd,sde->sre', hidden_one, qkv_f, precision=lax.Precision.HIGHEST)
    projected = low(low_back(projected))
    blocks = MOLS // MOL_DEV
    shaped = projected.reshape(3, blocks, MOL_DEV, L, HEADS, HEAD_DIM)
    new_pair, mixed = lax.map(jax.checkpoint(attend), (shaped[0], shaped[1], shaped[2], pair_f.reshape(blocks, MOL_DEV, HEADS, L, L), counts.reshape(blocks, MOL_DEV)))
    mixed = low(low_back(mixed.reshape(TOKENS, D)))
    attention = low_back(product(mixed, out_f.T))
    first_sum = atoms_f + attention
    hidden_two = low(layer_norm(first_sum) * gain_two)
    inner = low_back(product(hidden_two, inner_f))
    activated = low(jax.nn.gelu(inner))
    output = first_sum + low_back(product(activated, outer_f))
    return (output, new_pair.reshape(MOLS, HEADS, L, L))

def reference(atoms, pair, counts, qkv_weight, out_weight, ln1_gain, ln2_gain, w_in, w_out, out_cot, pair_cot):

    def closed(atoms_f, pair_f, qkv_f, out_f, gain_one, gain_two, inner_f, outer_f):
        return forward(atoms_f, pair_f, counts, qkv_f, out_f, gain_one, gain_two, inner_f, outer_f)
    results, pull = jax.vjp(closed, atoms.astype(jnp.float32), pair.astype(jnp.float32), qkv_weight.astype(jnp.float32), out_weight.astype(jnp.float32), ln1_gain.astype(jnp.float32), ln2_gain.astype(jnp.float32), w_in.astype(jnp.float32), w_out.astype(jnp.float32))
    grads = pull((out_cot.astype(jnp.float32), pair_cot.astype(jnp.float32)))
    return (results[0].astype(jnp.bfloat16), results[1].astype(jnp.bfloat16), grads[0].astype(jnp.bfloat16), grads[1].astype(jnp.bfloat16), grads[2], grads[3], grads[4], grads[5], grads[6], grads[7])
```

```python
from functools import partial

import jax
import jax.numpy as jnp
import numpy as np
from jax import lax
from jax.experimental import pallas as pl
from jax.experimental.pallas import tpu as pltpu
from jax.sharding import PartitionSpec as P

F32 = jnp.float32
BF16 = jnp.bfloat16
NEG = -1e30
BOTH = ("batch", "head")


def layer_stats(values):
    center = values - jnp.mean(values, -1, keepdims=True)
    inverse = lax.rsqrt(jnp.mean(center * center, -1, keepdims=True) + 1e-05)
    return (center * inverse, inverse)


def norm_back(grad_norm, normed, inverse):
    return inverse * (
        grad_norm
        - jnp.mean(grad_norm, -1, keepdims=True)
        - normed * jnp.mean(grad_norm * normed, -1, keepdims=True)
    )


def times_transposed(left, right):
    return lax.dot_general(
        left, right, (((1,), (1,)), ((), ())), preferred_element_type=jnp.float32
    )


def transposed_times(left, right):
    return lax.dot_general(
        left, right, (((0,), (0,)), ((), ())), preferred_element_type=jnp.float32
    )


def block_masks(count_part, length):
    positions = jnp.arange(length, dtype=jnp.int32)
    valid_rows = positions[None, :] < count_part[:, None]
    both_valid = valid_rows[:, None, :, None] & valid_rows[:, None, None, :]
    return (valid_rows, both_valid)


def scores_of(query_part, key_part, pair_part, score_scale):
    raw = jnp.einsum("mqhd,mkhd->mhqk", query_part, key_part, preferred_element_type=jnp.float32)
    return raw * score_scale + pair_part.astype(jnp.float32)


def attend_forward(inputs, score_scale):
    query_part, key_part, value_part, pair_part, count_part = inputs
    valid_rows, both_valid = block_masks(count_part, query_part.shape[1])
    logits = scores_of(query_part, key_part, pair_part, score_scale)
    new_pair = jnp.where(both_valid, logits, 0.0).astype(jnp.bfloat16)
    masked = jnp.where(valid_rows[:, None, None, :], logits, -1e30)
    row_max = jnp.max(masked, -1, keepdims=True)
    exponent = jnp.exp(masked - row_max)
    row_total = jnp.sum(exponent, -1, keepdims=True)
    soft_weights = (exponent / row_total).astype(jnp.bfloat16)
    mixed = jnp.einsum(
        "mhqk,mkhd->mqhd", soft_weights, value_part, preferred_element_type=jnp.float32
    )
    mixed = jnp.where(valid_rows[:, :, None, None], mixed, 0.0).astype(jnp.bfloat16)
    return (new_pair, mixed, row_max[..., 0] + jnp.log(row_total[..., 0]))


def attend_backward(inputs, score_scale):
    query_part, key_part, value_part, pair_part, count_part, grad_mixed, log_total, cot_part = (
        inputs
    )
    valid_rows, both_valid = block_masks(count_part, query_part.shape[1])
    logits = scores_of(query_part, key_part, pair_part, score_scale)
    masked = jnp.where(valid_rows[:, None, None, :], logits, -1e30)
    soft = jnp.exp(masked - log_total[..., None])
    grad_masked = jnp.where(valid_rows[:, :, None, None], grad_mixed, jnp.zeros_like(grad_mixed))
    grad_soft = jnp.einsum(
        "mqhd,mkhd->mhqk", grad_masked, value_part, preferred_element_type=jnp.float32
    )
    grad_scores = soft * (grad_soft - jnp.sum(grad_soft * soft, -1, keepdims=True))
    grad_scores = (grad_scores + jnp.where(both_valid, cot_part.astype(jnp.float32), 0.0)).astype(
        jnp.bfloat16
    )
    grad_query = (
        jnp.einsum("mhqk,mkhd->mqhd", grad_scores, key_part, preferred_element_type=jnp.float32)
        * score_scale
    ).astype(jnp.bfloat16)
    grad_key = (
        jnp.einsum("mhqk,mqhd->mkhd", grad_scores, query_part, preferred_element_type=jnp.float32)
        * score_scale
    ).astype(jnp.bfloat16)
    grad_value = jnp.einsum(
        "mhqk,mqhd->mkhd",
        soft.astype(jnp.bfloat16),
        grad_masked,
        preferred_element_type=jnp.float32,
    ).astype(jnp.bfloat16)
    return (grad_scores, grad_query, grad_key, grad_value)


def body_native(
    atoms, pair, counts, qkv_weight, out_weight, ln1_gain, ln2_gain, w_in, w_out, out_cot, pair_cot
):
    mols_here, heads_here, length = (pair.shape[0], pair.shape[1], pair.shape[2])
    qkv_full, out_full = (
        lax.all_gather(qkv_weight, "batch", axis=1, tiled=True),
        lax.all_gather(out_weight, "batch", axis=0, tiled=True),
    )
    gain_one, gain_two, inner_weight, outer_weight = (
        lax.all_gather(ln1_gain.astype(jnp.bfloat16), ("batch", "head"), axis=0, tiled=True).astype(
            ln1_gain.dtype
        ),
        lax.all_gather(ln2_gain.astype(jnp.bfloat16), ("batch", "head"), axis=0, tiled=True).astype(
            ln2_gain.dtype
        ),
        lax.all_gather(w_in, ("batch", "head"), axis=0, tiled=True),
        lax.all_gather(w_out, ("batch", "head"), axis=0, tiled=True),
    )
    width_here = qkv_full.shape[2]
    head_size = width_here // heads_here
    score_scale = head_size ** (-0.5)
    blocks = mols_here // 2
    group_total = mols_here * length
    atoms_f = atoms.astype(jnp.float32)
    normed_one, inverse_one = layer_stats(atoms_f)
    hidden_one = (normed_one * gain_one).astype(jnp.bfloat16)
    group_rows = lax.all_gather(hidden_one, "head", axis=0, tiled=True)
    projected = jnp.einsum(
        "rd,sde->sre", group_rows, qkv_full, preferred_element_type=jnp.float32
    ).astype(jnp.bfloat16)

    def to_blocks(values):
        return values.reshape(blocks, 2, length, heads_here, head_size)

    query_all, key_all, value_all = (
        to_blocks(projected[0]),
        to_blocks(projected[1]),
        to_blocks(projected[2]),
    )
    pair_blocks = pair.reshape(blocks, 2, heads_here, length, length)
    count_blocks = counts.reshape(blocks, 2)
    new_pair, mixed, log_total = lax.map(
        partial(attend_forward, score_scale=score_scale),
        (query_all, key_all, value_all, pair_blocks, count_blocks),
    )
    mixed_flat = mixed.reshape(group_total, width_here)
    slab_rows = mixed_flat
    attention = lax.psum_scatter(
        times_transposed(slab_rows, out_full).astype(jnp.bfloat16),
        "head",
        scatter_dimension=0,
        tiled=True,
    ).astype(jnp.float32)
    first_sum = atoms_f + attention
    normed_two, inverse_two = layer_stats(first_sum)
    hidden_two = (normed_two * gain_two).astype(jnp.bfloat16)
    inner = jnp.dot(hidden_two, inner_weight, preferred_element_type=jnp.float32)
    gelu_value, gelu_pull = jax.vjp(jax.nn.gelu, inner)
    activated = gelu_value.astype(jnp.bfloat16)
    output = first_sum + jnp.dot(activated, outer_weight, preferred_element_type=jnp.float32)
    grad_outer_w = transposed_times(activated, out_cot)
    grad_act = times_transposed(out_cot, outer_weight)
    grad_inner = gelu_pull(grad_act)[0].astype(jnp.bfloat16)
    grad_inner_w = transposed_times(hidden_two, grad_inner)
    grad_hidden_two = times_transposed(grad_inner, inner_weight)
    grad_gain_two = jnp.sum(grad_hidden_two * normed_two, 0)
    grad_first = out_cot.astype(jnp.float32) + norm_back(
        grad_hidden_two * gain_two, normed_two, inverse_two
    )
    grad_attention = grad_first.astype(jnp.bfloat16)
    group_grad = lax.all_gather(grad_attention, "head", axis=0, tiled=True)
    grad_out_full = transposed_times(group_grad, mixed_flat)
    grad_mixed = jnp.dot(group_grad, out_full, preferred_element_type=jnp.float32).astype(
        jnp.bfloat16
    )
    cot_blocks = pair_cot.reshape(blocks, 2, heads_here, length, length)
    grad_scores, grad_query, grad_key, grad_value = lax.map(
        partial(attend_backward, score_scale=score_scale),
        (
            query_all,
            key_all,
            value_all,
            pair_blocks,
            count_blocks,
            to_blocks(grad_mixed),
            log_total,
            cot_blocks,
        ),
    )
    grad_projected = jnp.stack(
        [
            grad_query.reshape(group_total, width_here),
            grad_key.reshape(group_total, width_here),
            grad_value.reshape(group_total, width_here),
        ]
    )
    grad_qkv_full = jnp.einsum(
        "rd,sre->sde", group_rows, grad_projected, preferred_element_type=jnp.float32
    )
    slab_rows = grad_projected
    grad_hidden_one = lax.psum_scatter(
        jnp.einsum("sre,sde->rd", slab_rows, qkv_full, preferred_element_type=jnp.float32).astype(
            jnp.bfloat16
        ),
        "head",
        scatter_dimension=0,
        tiled=True,
    ).astype(jnp.float32)
    grad_gain_one = jnp.sum(grad_hidden_one * normed_one, 0)
    atoms_grad = grad_first + norm_back(grad_hidden_one * gain_one, normed_one, inverse_one)
    qkv_grad, out_grad = (
        lax.psum_scatter(
            grad_qkv_full.astype(jnp.bfloat16), "batch", scatter_dimension=1, tiled=True
        ).astype(jnp.float32),
        lax.psum_scatter(
            grad_out_full.astype(jnp.bfloat16), "batch", scatter_dimension=0, tiled=True
        ).astype(jnp.float32),
    )
    gain_one_grad, gain_two_grad, inner_grad, outer_grad = (
        lax.psum_scatter(grad_gain_one, ("batch", "head"), scatter_dimension=0, tiled=True),
        lax.psum_scatter(grad_gain_two, ("batch", "head"), scatter_dimension=0, tiled=True),
        lax.psum_scatter(grad_inner_w, ("batch", "head"), scatter_dimension=0, tiled=True),
        lax.psum_scatter(grad_outer_w, ("batch", "head"), scatter_dimension=0, tiled=True),
    )
    return (
        output.astype(jnp.bfloat16),
        new_pair.reshape(mols_here, heads_here, length, length),
        atoms_grad.astype(jnp.bfloat16),
        grad_scores.reshape(mols_here, heads_here, length, length),
        qkv_grad,
        out_grad,
        gain_one_grad,
        gain_two_grad,
        inner_grad,
        outer_grad,
    )


def dot(left, right):
    return jnp.dot(left, right, preferred_element_type=F32)


def dot_nt(left, right):
    return lax.dot_general(left, right, (((1,), (1,)), ((), ())), preferred_element_type=F32)


def dot_tn(left, right):
    return lax.dot_general(left, right, (((0,), (0,)), ((), ())), preferred_element_type=F32)


def swap(values, axes, count, bit):
    return lax.ppermute(values, axes, [(i, i ^ bit) for i in range(count)])


def relative(position, bits):
    return sum(((position >> k) & 1) * bit for k, bit in enumerate(bits))


def whole(shape):
    return pl.BlockSpec(shape, lambda *_: (0,) * len(shape))


def prep_kernel(me_ref, near_ref, far_ref, w_ref, gains_ref, rows_s, *, bits, heads_bits, shard):
    b, h = me_ref[0], me_ref[1]
    half = near_ref.shape[0]
    rows = w_ref.shape[1] // (2 * half)
    dim = gains_ref.shape[1]
    for p in range(2 * half):
        ref, q = (near_ref, p) if p < half else (far_ref, p - half)
        at = pl.multiple_of((b ^ relative(p, bits)) * rows, rows)
        for s in range(3):
            w_ref[s, pl.ds(at, rows), :] = ref[q, s * rows : (s + 1) * rows, :]
        rows_s[p : p + 1, :] = ref[q, 3 * rows : 3 * rows + 1, :].astype(F32)
    lanes = rows_s.shape[1]
    count = 2 * half
    lane = lax.broadcasted_iota(jnp.int32, (lanes, dim), 0)
    col = lax.broadcasted_iota(jnp.int32, (lanes, dim), 1)
    block = lax.broadcasted_iota(jnp.int32, (count, dim), 1) // rows
    place = lax.broadcasted_iota(jnp.int32, (count, dim), 0)
    owner = sum(((place >> k) & 1) * bit for k, bit in enumerate(bits)) ^ b
    values = rows_s[...].astype(BF16)
    for g in range(2):
        start = (((col // shard) & 1) ^ h) * (4 * shard) + g * 2 * shard + lax.rem(col, shard)
        pick = jnp.where((lane == start) | (lane == start + shard), 1.0, 0.0).astype(BF16)
        spread = dot(values, pick)
        gains_ref[g : g + 1, :] = jnp.sum(jnp.where(owner == block, spread, 0.0), 0, keepdims=True)


def attend_forward_kernel(
    mol_ref, cnt_ref, atoms_ref, w_ref, gains_ref, mask_ref, pair_ref, *rest,
    hb, groups, scale, carried
):
    new_ref, exp_ref, hid_t_ref, qkv_ref, mixed_ref, inv_ref, q_s, kt_s, v_s, sum_s = rest[carried:]
    step = pl.program_id(1)
    length = atoms_ref.shape[0]
    lanes = w_ref.shape[2] // groups
    per_group = lanes // (8 * hb)
    count = cnt_ref[mol_ref[pl.program_id(0)]]

    @pl.when(step == 0)
    def _():
        values = atoms_ref[...].astype(F32)
        center = values - jnp.mean(values, -1, keepdims=True)
        inverse = lax.rsqrt(jnp.mean(center * center, -1, keepdims=True) + 1e-05)
        hidden = (center * inverse * gains_ref[0:1, :]).astype(BF16)
        hid_t_ref[...] = hidden.T
        query = (dot(hidden, w_ref[0]) * scale).astype(BF16)
        key = dot(hidden, w_ref[1]).astype(BF16)
        value = dot(hidden, w_ref[2]).astype(BF16)
        qkv_ref[0] = query
        qkv_ref[1] = key
        qkv_ref[2] = value
        key_t = key.T
        at = lax.broadcasted_iota(jnp.int32, (1, length), 1)
        bias = jnp.where(at < count, 0.0, NEG)
        first = lax.broadcasted_iota(jnp.int32, (lanes, length), 0) == 0
        bias_rows = jnp.where(first, bias, 0.0).astype(BF16)
        ones_lane = (lax.broadcasted_iota(jnp.int32, (length, lanes), 1) == 0).astype(F32).astype(BF16)
        for g in range(groups):
            part = slice(g * lanes, (g + 1) * lanes)
            q_s[g, :, :lanes] = query[:, part]
            q_s[g, :, lanes:] = ones_lane
            kt_s[g, :lanes, :] = key_t[part]
            kt_s[g, lanes:, :] = bias_rows
            v_s[g, :, :lanes] = value[:, part]
            v_s[g, :, lanes:] = jnp.ones((length, lanes), BF16)

    g = step // per_group
    block = lax.rem(step, per_group)
    valid = (lax.broadcasted_iota(jnp.int32, (length, length), 0) < count) & (
        lax.broadcasted_iota(jnp.int32, (length, length), 1) < count
    )
    total = jnp.zeros((length, 2 * lanes), F32)
    for i in range(hb):
        logits = dot(q_s[g] * mask_ref[0, block, i : i + 1, :], kt_s[g]) + pair_ref[0, i].astype(F32)
        new_ref[0, i] = jnp.where(valid, logits, 0.0).astype(BF16)
        exp_ref[0, i] = jnp.exp(logits - jnp.max(logits, -1, keepdims=True)).astype(BF16)
        total = total + dot(exp_ref[0, i], v_s[g] * mask_ref[1, block, i : i + 1, :])

    @pl.when(block == 0)
    def _():
        sum_s[...] = total

    @pl.when(block > 0)
    def _():
        sum_s[...] = sum_s[...] + total

    @pl.when(block == per_group - 1)
    def _():
        inverse = 1.0 / sum_s[:, lanes:]
        rows_ok = lax.broadcasted_iota(jnp.int32, (length, lanes), 0) < count
        at = pl.ds(pl.multiple_of(g * lanes, lanes), lanes)
        inv_ref[:, at] = inverse
        mixed_ref[:, at] = jnp.where(rows_ok, sum_s[:, :lanes] * inverse, 0.0).astype(BF16)


def head_masks(groups, width, hb, backward):
    lanes = width // groups
    heads = lanes // 8
    masks = np.zeros((2, heads, 2 * lanes), np.float32)
    for h in range(heads):
        own = slice(h * 8, (h + 1) * 8)
        twin = slice(lanes + h * 8, lanes + (h + 1) * 8)
        masks[0, h, own] = 1
        masks[1, h, own] = 1
        if backward:
            masks[0, h, twin] = 1
        else:
            masks[0, h, lanes] = 1
            masks[1, h, twin] = 1
    return jnp.asarray(masks.reshape(2, heads // hb, hb, 2 * lanes), BF16)


def specs_of(length, hb):
    pair = pl.BlockSpec((1, hb, length, length), lambda i, j, mol, cnt: (mol[i], j, 0, 0))
    rows = lambda cols: pl.BlockSpec((length, cols), lambda i, j, mol, cnt: (i, 0))
    three = lambda cols: pl.BlockSpec((3, length, cols), lambda i, j, mol, cnt: (0, i, 0))
    return pair, rows, three


ANY = pl.BlockSpec(memory_space=pl.ANY)


def attend_forward_call(mols, counts, atoms, weights, gains, pair, carried, hb=16):
    n, (_, heads, length, _) = mols.shape[0], pair.shape
    dim, width = atoms.shape[1], weights.shape[2]
    groups = max(1, width // 128)
    lanes = width // groups
    masks = head_masks(groups, width, hb, False)
    pair_spec, rows, three = specs_of(length, hb)
    args = [atoms, weights, gains, masks, pair, *carried]
    spec = pltpu.PrefetchScalarGridSpec(
        num_scalar_prefetch=2,
        grid=(n, heads // hb),
        in_specs=[rows(dim), whole(weights.shape), whole(gains.shape), whole(masks.shape), pair_spec]
        + [ANY] * len(carried),
        out_specs=[
            pair_spec,
            pair_spec,
            pl.BlockSpec((dim, length), lambda i, j, mol, cnt: (0, i)),
            three(width),
            rows(width),
            rows(width),
        ],
        scratch_shapes=[
            pltpu.VMEM((groups, length, 2 * lanes), BF16),
            pltpu.VMEM((groups, 2 * lanes, length), BF16),
            pltpu.VMEM((groups, length, 2 * lanes), BF16),
            pltpu.VMEM((length, 2 * lanes), F32),
        ],
    )
    shape = jax.ShapeDtypeStruct
    return pl.pallas_call(
        partial(
            attend_forward_kernel,
            hb=hb,
            groups=groups,
            scale=8**-0.5,
            carried=len(carried),
        ),
        grid_spec=spec,
        out_shape=[
            shape(pair.shape, BF16),
            shape(pair.shape, BF16),
            shape((dim, n * length), BF16),
            shape((3, n * length, width), BF16),
            shape((n * length, width), BF16),
            shape((n * length, width), F32),
        ],
        input_output_aliases={7: 0, 8: 1} if carried else {},
        compiler_params=pltpu.CompilerParams(
            dimension_semantics=("arbitrary", "arbitrary"), vmem_limit_bytes=48 << 20
        ),
        cost_estimate=pl.CostEstimate(
            flops=n * heads * 4 * length**3,
            transcendentals=n * heads * length**2,
            bytes_accessed=6 * n * heads * length**2,
        ),
        name="attend_forward",
    )(mols, counts, *args)


def attend_backward_kernel(
    mol_ref, cnt_ref, gm_ref, mixed_ref, inv_ref, qkv_ref, w_ref, mask_ref, exp_ref, cot_ref, *rest,
    hb, groups, scale, carried
):
    pg_ref, gp_ref, gh_ref, l_s, r_s, k_s, qt_s, gt_s, gq_s, gk_s, gv_s = rest[carried:]
    step, steps = pl.program_id(1), pl.num_programs(1)
    length, width = gm_ref.shape
    lanes = width // groups
    per_group = lanes // (8 * hb)
    count = cnt_ref[mol_ref[pl.program_id(0)]]

    @pl.when(step == 0)
    def _():
        rows_ok = lax.broadcasted_iota(jnp.int32, (length, width), 0) < count
        scaled = jnp.where(rows_ok, gm_ref[...].astype(F32) * inv_ref[...], 0.0).astype(BF16)
        wide = scaled.astype(F32)
        delta = (-(wide * mixed_ref[...].astype(F32))).astype(BF16)
        value_t = qkv_ref[2].T
        for g in range(groups):
            part = slice(g * lanes, (g + 1) * lanes)
            l_s[g, :, :lanes] = scaled[:, part]
            l_s[g, :, lanes:] = delta[:, part]
            r_s[g, :lanes, :] = value_t[part]
            r_s[g, lanes:, :] = jnp.ones((lanes, length), BF16)
            k_s[g] = qkv_ref[1, :, part]
        qt_s[...] = qkv_ref[0].astype(F32).T.reshape(qt_s.shape).astype(BF16)
        gt_s[...] = wide.T.reshape(gt_s.shape).astype(BF16)

    g = step // per_group
    block = lax.rem(step, per_group)
    valid = (lax.broadcasted_iota(jnp.int32, (length, length), 0) < count) & (
        lax.broadcasted_iota(jnp.int32, (length, length), 1) < count
    )
    total = jnp.zeros((length, lanes), F32)
    for i in range(hb):
        soft = dot(l_s[g] * mask_ref[0, block, i : i + 1, :], r_s[g])
        scores = exp_ref[0, i].astype(F32) * soft + jnp.where(valid, cot_ref[0, i].astype(F32), 0.0)
        pg_ref[0, i] = scores.astype(BF16)
        total = total + dot(pg_ref[0, i], k_s[g] * mask_ref[1, block, i : i + 1, :lanes])
        head = step * hb + i
        gk_s[head] = dot(qt_s[head], pg_ref[0, i])
        gv_s[head] = dot(gt_s[head], exp_ref[0, i])

    @pl.when(block == 0)
    def _():
        gq_s[g] = total

    @pl.when(block > 0)
    def _():
        gq_s[g] = gq_s[g] + total

    @pl.when(step == steps - 1)
    def _():
        for k in range(groups):
            gp_ref[0, :, k * lanes : (k + 1) * lanes] = (gq_s[k] * scale).astype(BF16)
        gp_ref[1] = gk_s[...].reshape(width, length).T.astype(BF16)
        gp_ref[2] = gv_s[...].reshape(width, length).T.astype(BF16)
        gh_ref[...] = (
            dot_nt(gp_ref[0], w_ref[0]) + dot_nt(gp_ref[1], w_ref[1]) + dot_nt(gp_ref[2], w_ref[2])
        ).astype(BF16)


def attend_backward_call(mols, counts, gm, mixed, inverse, qkv, weights, exps, cot, carried, hb=16):
    n, (_, heads, length, _) = mols.shape[0], exps.shape
    dim, width = weights.shape[1], weights.shape[2]
    groups = max(1, width // 128)
    lanes = width // groups
    masks = head_masks(groups, width, hb, True)
    pair_spec, rows, three = specs_of(length, hb)
    args = [gm, mixed, inverse, qkv, weights, masks, exps, cot, *carried]
    spec = pltpu.PrefetchScalarGridSpec(
        num_scalar_prefetch=2,
        grid=(n, heads // hb),
        in_specs=[
            rows(width), rows(width), rows(width), three(width),
            whole(weights.shape), whole(masks.shape), pair_spec, pair_spec,
        ] + [ANY] * len(carried),
        out_specs=[pair_spec, three(width), rows(dim)],
        scratch_shapes=[
            pltpu.VMEM((groups, length, 2 * lanes), BF16),
            pltpu.VMEM((groups, 2 * lanes, length), BF16),
            pltpu.VMEM((groups, length, lanes), BF16),
            pltpu.VMEM((heads, 8, length), BF16),
            pltpu.VMEM((heads, 8, length), BF16),
            pltpu.VMEM((groups, length, lanes), F32),
            pltpu.VMEM((heads, 8, length), F32),
            pltpu.VMEM((heads, 8, length), F32),
        ],
    )
    shape = jax.ShapeDtypeStruct
    return pl.pallas_call(
        partial(
            attend_backward_kernel,
            hb=hb,
            groups=groups,
            scale=8**-0.5,
            carried=len(carried),
        ),
        grid_spec=spec,
        out_shape=[
            shape(exps.shape, BF16),
            shape((3, n * length, width), BF16),
            shape((n * length, dim), BF16),
        ],
        input_output_aliases={10: 0} if carried else {},
        compiler_params=pltpu.CompilerParams(
            dimension_semantics=("arbitrary", "arbitrary"), vmem_limit_bytes=48 << 20
        ),
        cost_estimate=pl.CostEstimate(
            flops=n * heads * 6 * length**3,
            transcendentals=0,
            bytes_accessed=6 * n * heads * length**2,
        ),
        name="attend_backward",
    )(mols, counts, *args)


ROOT = (2 / np.pi) ** 0.5


def layer_kernel(
    me_ref, atoms_ref, mine_ref, other_ref, cot_ref, gains_ref, a0_ref, a1_ref, b0_ref, b1_ref,
    out_ref, first_ref, gm_mine_ref, gm_other_ref, ga0_ref, ga1_ref, gb0_ref, gb1_ref,
    win_s, wout_s, ow_s, sum_s, acc_s, gh_s, normed_s, inv_s, hid_s, hid_t_s, *, bits_a, bits_b
):
    me = me_ref[0]
    c, steps = pl.program_id(0), pl.num_programs(0)
    half = a0_ref.shape[0]
    dim = atoms_ref.shape[1]
    width = mine_ref.shape[1]
    rows = dim // (2 * half)
    ff_rows = b0_ref.shape[1]
    e_rows = dim // half

    def shards(bits, near, far):
        for p in range(2 * half):
            yield p, me ^ relative(p, bits), (near, p) if p < half else (far, p - half)

    @pl.when(c == 0)
    def _():
        for p, owner, (ref, q) in shards(bits_a, a0_ref, a1_ref):
            for k in range(4):
                win_s[k, pl.ds(pl.multiple_of(owner * rows, rows), rows), :] = ref[q, k * rows : (k + 1) * rows, :]
            at = pl.multiple_of((owner // 2) * e_rows, e_rows)
            ow_s[relative(p, bits_a) & 1, pl.ds(at, e_rows), :] = ref[q, 4 * rows : 4 * rows + e_rows, :width]
        for p, owner, (ref, q) in shards(bits_b, b0_ref, b1_ref):
            wout_s[pl.ds(pl.multiple_of(owner * ff_rows, ff_rows), ff_rows), :] = ref[q]
        first_sum = (
            atoms_ref[...].astype(F32) + dot_nt(mine_ref[...], ow_s[0]) + dot_nt(other_ref[...], ow_s[1])
        )
        sum_s[...] = first_sum
        center = first_sum - jnp.mean(first_sum, -1, keepdims=True)
        inverse = lax.rsqrt(jnp.mean(center * center, -1, keepdims=True) + 1e-05)
        normed = center * inverse
        normed_s[...] = normed
        inv_s[...] = inverse
        hidden = (normed * gains_ref[1:2, :]).astype(BF16)
        hid_s[...] = hidden
        hid_t_s[...] = hidden.T
        acc_s[...] = jnp.zeros_like(acc_s)
        gh_s[...] = jnp.zeros_like(gh_s)

    win = win_s[c]
    wout = wout_s[pl.ds(pl.multiple_of(c * dim, dim), dim), :]
    inner = dot(hid_s[...], win)
    square = inner * inner
    tanh = jnp.tanh(ROOT * inner * (1.0 + 0.044715 * square))
    activated = (0.5 * inner * (1.0 + tanh)).astype(BF16)
    slope = 0.5 * (1.0 + tanh) + (0.5 * ROOT) * inner * (1.0 - tanh * tanh) * (1.0 + (3 * 0.044715) * square)
    acc_s[...] += dot(activated, wout)
    grad_inner = (dot_nt(cot_ref[...], wout) * slope).astype(BF16)
    gh_s[...] += dot_nt(grad_inner, win)
    grad_in = dot(hid_t_s[...], grad_inner).astype(BF16)
    win_s[c] = grad_in
    grad_out = dot_tn(activated, cot_ref[...]).astype(BF16)
    wout_s[pl.ds(pl.multiple_of(c * dim, dim), dim), :] = grad_out

    @pl.when(c == steps - 1)
    def _():
        out_ref[...] = (sum_s[...] + acc_s[...]).astype(BF16)
        normed = normed_s[...]
        grad_norm = gh_s[...] * gains_ref[1:2, :]
        grad_first = cot_ref[...].astype(F32) + inv_s[...] * (
            grad_norm
            - jnp.mean(grad_norm, -1, keepdims=True)
            - normed * jnp.mean(grad_norm * normed, -1, keepdims=True)
        )
        first_ref[...] = grad_first
        grad_attention = grad_first.astype(BF16)
        gm_mine_ref[...] = dot(grad_attention, ow_s[0]).astype(BF16)
        gm_other_ref[...] = dot(grad_attention, ow_s[1]).astype(BF16)
        ow_s[0] = dot_tn(grad_attention, mine_ref[...]).astype(BF16)
        ow_s[1] = dot_tn(grad_attention, other_ref[...]).astype(BF16)
        for p, owner, (ref, q) in shards(bits_a, ga0_ref, ga1_ref):
            for k in range(4):
                ref[q, k * rows : (k + 1) * rows, :] = win_s[k, pl.ds(pl.multiple_of(owner * rows, rows), rows), :]
            at = pl.multiple_of((owner // 2) * e_rows, e_rows)
            ref[q, 4 * rows : 4 * rows + e_rows, :width] = ow_s[relative(p, bits_a) & 1, pl.ds(at, e_rows), :]
            ref[q, 4 * rows : 4 * rows + e_rows, width:] = jnp.zeros((e_rows, dim - width), BF16)
        for p, owner, (ref, q) in shards(bits_b, gb0_ref, gb1_ref):
            ref[q] = wout_s[pl.ds(pl.multiple_of(owner * ff_rows, ff_rows), ff_rows), :]


def layer_call(me, atoms, mine, other, cot, gains, a_pair, b_pair, bits_a, bits_b):
    own, dim = atoms.shape
    width = mine.shape[1]
    ff = 2 * b_pair[0].shape[0] * b_pair[0].shape[1]
    args = [atoms, mine, other, cot, gains, *a_pair, *b_pair]
    shape = jax.ShapeDtypeStruct
    outs = [
        shape((own, dim), BF16),
        shape((own, dim), F32),
        shape((own, width), BF16),
        shape((own, width), BF16),
        *[shape(x.shape, BF16) for x in (*a_pair, *b_pair)],
    ]
    spec = pltpu.PrefetchScalarGridSpec(
        num_scalar_prefetch=1,
        grid=(ff // dim,),
        in_specs=[whole(x.shape) for x in args],
        out_specs=[whole(x.shape) for x in outs],
        scratch_shapes=[
            pltpu.VMEM((ff // dim, dim, dim), BF16),
            pltpu.VMEM((ff, dim), BF16),
            pltpu.VMEM((2, dim, width), BF16),
            pltpu.VMEM((own, dim), F32),
            pltpu.VMEM((own, dim), F32),
            pltpu.VMEM((own, dim), F32),
            pltpu.VMEM((own, dim), F32),
            pltpu.VMEM((own, 1), F32),
            pltpu.VMEM((own, dim), BF16),
            pltpu.VMEM((dim, own), BF16),
        ],
    )
    return pl.pallas_call(
        partial(layer_kernel, bits_a=bits_a, bits_b=bits_b),
        grid_spec=spec,
        out_shape=outs,
        compiler_params=pltpu.CompilerParams(
            dimension_semantics=("arbitrary",), vmem_limit_bytes=60 << 20
        ),
        cost_estimate=pl.CostEstimate(
            flops=12 * own * dim * ff, transcendentals=own * ff, bytes_accessed=8 * dim * ff
        ),
        name="layer",
    )(me, *args)


def project_grad_kernel(me_ref, *refs, bits, parts):
    b = me_ref[0]
    near_ref, far_ref, full_s = refs[2 * parts :]
    half = near_ref.shape[0]
    rows = full_s.shape[1] // (2 * half)
    for s in range(3):
        full_s[s] = sum(dot(refs[k][...], refs[parts + k][s]) for k in range(parts)).astype(BF16)
    for p in range(2 * half):
        ref, q = (near_ref, p) if p < half else (far_ref, p - half)
        at = pl.multiple_of((b ^ relative(p, bits)) * rows, rows)
        for s in range(3):
            ref[q, s * rows : (s + 1) * rows, :] = full_s[s, pl.ds(at, rows), :]


def project_grad_call(me, hid_ts, gps, bits):
    dim, width = hid_ts[0].shape[0], gps[0].shape[2]
    half = 2 ** (len(bits) - 1)
    rows = dim // (2 * half)
    args = [*hid_ts, *gps]
    outs = [jax.ShapeDtypeStruct((half, 3 * rows, width), BF16)] * 2
    return pl.pallas_call(
        partial(project_grad_kernel, bits=bits, parts=len(hid_ts)),
        grid_spec=pltpu.PrefetchScalarGridSpec(
            num_scalar_prefetch=1,
            grid=(1,),
            in_specs=[whole(x.shape) for x in args],
            out_specs=[whole(x.shape) for x in outs],
            scratch_shapes=[pltpu.VMEM((3, dim, width), BF16)],
        ),
        out_shape=outs,
        compiler_params=pltpu.CompilerParams(vmem_limit_bytes=32 << 20),
        name="project_grad",
    )(me, *args)


def last_kernel(atoms_ref, gains_ref, first_ref, ga_ref, gb_ref, recv_ref, out_ref):
    values = atoms_ref[...].astype(F32)
    center = values - jnp.mean(values, -1, keepdims=True)
    inverse = lax.rsqrt(jnp.mean(center * center, -1, keepdims=True) + 1e-05)
    normed = center * inverse
    part = ga_ref.shape[0]
    grads = jnp.concatenate([ga_ref[...], gb_ref[...]], 0).astype(F32) + recv_ref[...].astype(F32)
    grad_norm = grads * gains_ref[0:1, :]
    out_ref[...] = (
        first_ref[...]
        + inverse
        * (
            grad_norm
            - jnp.mean(grad_norm, -1, keepdims=True)
            - normed * jnp.mean(grad_norm * normed, -1, keepdims=True)
        )
    ).astype(BF16)


def last_call(atoms, gains, first, gh_a, gh_b, recv):
    args = [atoms, gains, first, gh_a, gh_b, recv]
    return pl.pallas_call(
        last_kernel,
        grid=(1,),
        in_specs=[whole(x.shape) for x in args],
        out_specs=whole(atoms.shape),
        out_shape=jax.ShapeDtypeStruct(atoms.shape, BF16),
        compiler_params=pltpu.CompilerParams(vmem_limit_bytes=32 << 20),
        name="last_norm",
    )(*args)


def join(values, received):
    return jnp.concatenate([values, received], 0)


def add(kept, received):
    return (kept.astype(F32) + received.astype(F32)).astype(BF16)


def halves(values):
    half = values.shape[0] // 2
    return values[:half], values[half:]


def body_pairs(
    atoms, pair, counts, qkv_weight, out_weight, ln1_gain, ln2_gain, w_in, w_out, out_cot, pair_cot,
    batch
):
    b = lax.axis_index("batch")
    h = lax.axis_index("head")
    own, dim = atoms.shape
    length = pair.shape[2]
    width = qkv_weight.shape[2]
    shard = ln1_gain.shape[0]
    top = batch.bit_length() - 1
    far_bits = [1 << k for k in range(top - 1, 1, -1)]
    batch_bits = [*far_bits, 2, 1]
    bits_a = [2 * bit for bit in far_bits] + [4, 1, 2]
    bits_b = [2 * bit for bit in far_bits] + [1, 4, 2]
    nz = len(far_bits)
    over_batch = lambda x, bit: swap(x, "batch", batch, bit)
    over_head = lambda x: swap(x, "head", 2, 1)
    over_both = lambda x, bit: swap(x, BOTH, 2 * batch, bit)

    def split_gain(gain):
        high = gain.astype(BF16)
        return [high, (gain - high.astype(F32)).astype(BF16)]

    gain_row = jnp.concatenate(split_gain(ln1_gain) + split_gain(ln2_gain))[None]
    gain_row = jnp.concatenate([gain_row, over_head(gain_row)], 1)
    atoms_other = over_head(atoms)
    tail = jnp.pad(gain_row, ((0, 15), (0, width - gain_row.shape[1])))
    gathered = jnp.concatenate([qkv_weight.reshape(-1, width), tail], 0)[None]
    for bit in batch_bits[:-1]:
        gathered = join(gathered, over_batch(gathered, bit))
    far = over_batch(gathered, batch_bits[-1])
    me_batch = jnp.stack([b, h])
    weights, gains = pl.pallas_call(
        partial(prep_kernel, bits=batch_bits, heads_bits=1, shard=shard),
        grid_spec=pltpu.PrefetchScalarGridSpec(
            num_scalar_prefetch=1,
            grid=(1,),
            in_specs=[whole(gathered.shape)] * 2,
            out_specs=[whole((3, dim, width)), whole((2, dim))],
            scratch_shapes=[pltpu.VMEM((batch, width), F32)],
        ),
        out_shape=[jax.ShapeDtypeStruct((3, dim, width), BF16), jax.ShapeDtypeStruct((2, dim), F32)],
        name="prepare",
    )(me_batch, gathered, far)

    e_rows = out_weight.shape[0]
    blocks = w_in.shape[1] // dim
    in_rows = [w_in[:, k * dim : (k + 1) * dim] for k in range(blocks)]
    out_rows = jnp.pad(out_weight, ((0, 0), (0, dim - width)))
    bulk = jnp.concatenate([*in_rows, out_rows, w_out], 0)[None]
    cut = bulk.shape[1] - w_out.shape[0]
    for bit in bits_a[:nz]:
        bulk = join(bulk, over_both(bulk, bit))
    part_a, part_b = bulk[:, :cut], bulk[:, cut:]
    for bit_a, bit_b in zip(bits_a[nz:-1], bits_b[nz:-1]):
        part_a, part_b = join(part_a, over_both(part_a, bit_a)), join(part_b, over_both(part_b, bit_b))
    a_pair = (part_a, over_both(part_a, bits_a[-1]))
    b_pair = (part_b, over_both(part_b, bits_b[-1]))

    per = own // length
    mine, theirs = h * per, (1 - h) * per
    plan = [
        (mine[None], atoms[:length]),
        (theirs + jnp.arange(per, dtype=jnp.int32), atoms_other),
        (mine + jnp.arange(1, per, dtype=jnp.int32), atoms[length:]),
    ]
    carried = ()
    saved = []
    for mols, rows in plan:
        new_pair, exps, *rest = attend_forward_call(mols, counts, rows, weights, gains, pair, carried)
        carried = (new_pair, exps)
        saved.append(rest)
    mixed_other = over_head(saved[1][2])
    mixed_mine = jnp.concatenate([saved[0][2], saved[2][2]], 0)

    me = (2 * b + h)[None]
    output, first, gm_mine, gm_other, ga0, ga1, gb0, gb1 = layer_call(
        me, atoms, mixed_mine, mixed_other, out_cot, gains, a_pair, b_pair, bits_a, bits_b
    )
    gm_received = over_head(gm_other)
    part_a = add(ga0, over_both(ga1, bits_a[-1]))
    part_b = add(gb0, over_both(gb1, bits_b[-1]))
    for bit_a, bit_b in zip(bits_a[-2:nz - 1:-1], bits_b[-2:nz - 1:-1]):
        (keep_a, send_a), (keep_b, send_b) = halves(part_a), halves(part_b)
        part_a, part_b = add(keep_a, over_both(send_a, bit_a)), add(keep_b, over_both(send_b, bit_b))
    bulk = jnp.concatenate([part_a, part_b], 1)
    for bit in bits_a[nz - 1 :: -1]:
        keep, send = halves(bulk)
        bulk = add(keep, over_both(send, bit))
    bulk = bulk[0].astype(F32)
    shard_rows = w_in.shape[0]
    in_grad = jnp.concatenate([bulk[k * shard_rows : (k + 1) * shard_rows] for k in range(blocks)], 1)
    out_grad = bulk[blocks * shard_rows : cut, :width]
    outer_grad = bulk[cut:]
    gain_two_grad = jnp.sum(in_grad * w_in.astype(F32), 1) / ln2_gain

    gm_parts = [gm_mine[:length], gm_received, gm_mine[length:]]
    carried = ()
    grads = []
    for (mols, _), gm, (hid_t, qkv, mixed, inverse) in zip(plan, gm_parts, saved):
        pair_grad, *rest = attend_backward_call(
            mols, counts, gm, mixed, inverse, qkv, weights, exps, pair_cot, carried
        )
        carried = (pair_grad,)
        grads.append(rest)
    hidden_received = over_head(grads[1][1])
    near, far = project_grad_call(
        me_batch, [s[0] for s in saved], [g[0] for g in grads], batch_bits
    )
    near = add(near, over_batch(far, batch_bits[-1]))
    for bit in batch_bits[-2::-1]:
        keep, send = halves(near)
        near = add(keep, over_batch(send, bit))
    qkv_grad = near[0].reshape(qkv_weight.shape).astype(F32)
    gain_part = jnp.sum(qkv_grad * qkv_weight.astype(F32), (0, 2)).reshape(2, shard)
    gain_mine = lax.dynamic_index_in_dim(gain_part, h, 0, False)
    gain_other = over_head(lax.dynamic_index_in_dim(gain_part, 1 - h, 0, False))
    gain_one_grad = (gain_mine + gain_other) / ln1_gain
    atoms_grad = last_call(atoms, gains, first, grads[0][1], grads[2][1], hidden_received)
    return (
        output, new_pair, atoms_grad, pair_grad, qkv_grad, out_grad,
        gain_one_grad, gain_two_grad, in_grad, outer_grad,
    )


def solution(mesh):
    rows = P(BOTH, None)
    heads = P("batch", "head", None, None)
    batch, head = mesh.shape["batch"], mesh.shape["head"]
    body = partial(body_pairs, batch=batch) if (batch, head) == (16, 2) else body_native
    return jax.shard_map(
        body,
        mesh=mesh,
        in_specs=(
            rows, heads, P("batch"), P(None, "batch", "head"), P("batch", "head"),
            P(BOTH), P(BOTH), rows, rows, rows, heads,
        ),
        out_specs=(
            rows, heads, rows, heads, P(None, "batch", "head"), P("batch", "head"),
            P(BOTH), P(BOTH), rows, rows,
        ),
        check_vma=False,
    )
```

```python
from functools import partial

import jax
import jax.numpy as jnp
import numpy as np
from jax import lax
from jax.experimental import pallas as pl
from jax.experimental.pallas import tpu as pltpu
from jax.sharding import PartitionSpec as P

F32 = jnp.float32
BF16 = jnp.bfloat16
NEG = -1e30
BOTH = ("batch", "head")


def layer_stats(values):
    center = values - jnp.mean(values, -1, keepdims=True)
    inverse = lax.rsqrt(jnp.mean(center * center, -1, keepdims=True) + 1e-05)
    return (center * inverse, inverse)


def norm_back(grad_norm, normed, inverse):
    return inverse * (
        grad_norm
        - jnp.mean(grad_norm, -1, keepdims=True)
        - normed * jnp.mean(grad_norm * normed, -1, keepdims=True)
    )


def times_transposed(left, right):
    return lax.dot_general(
        left, right, (((1,), (1,)), ((), ())), preferred_element_type=jnp.float32
    )


def transposed_times(left, right):
    return lax.dot_general(
        left, right, (((0,), (0,)), ((), ())), preferred_element_type=jnp.float32
    )


def block_masks(count_part, length):
    positions = jnp.arange(length, dtype=jnp.int32)
    valid_rows = positions[None, :] < count_part[:, None]
    both_valid = valid_rows[:, None, :, None] & valid_rows[:, None, None, :]
    return (valid_rows, both_valid)


def scores_of(query_part, key_part, pair_part, score_scale):
    raw = jnp.einsum("mqhd,mkhd->mhqk", query_part, key_part, preferred_element_type=jnp.float32)
    return raw * score_scale + pair_part.astype(jnp.float32)


def attend_forward(inputs, score_scale):
    query_part, key_part, value_part, pair_part, count_part = inputs
    valid_rows, both_valid = block_masks(count_part, query_part.shape[1])
    logits = scores_of(query_part, key_part, pair_part, score_scale)
    new_pair = jnp.where(both_valid, logits, 0.0).astype(jnp.bfloat16)
    masked = jnp.where(valid_rows[:, None, None, :], logits, -1e30)
    row_max = jnp.max(masked, -1, keepdims=True)
    exponent = jnp.exp(masked - row_max)
    row_total = jnp.sum(exponent, -1, keepdims=True)
    soft_weights = (exponent / row_total).astype(jnp.bfloat16)
    mixed = jnp.einsum(
        "mhqk,mkhd->mqhd", soft_weights, value_part, preferred_element_type=jnp.float32
    )
    mixed = jnp.where(valid_rows[:, :, None, None], mixed, 0.0).astype(jnp.bfloat16)
    return (new_pair, mixed, row_max[..., 0] + jnp.log(row_total[..., 0]))


def attend_backward(inputs, score_scale):
    query_part, key_part, value_part, pair_part, count_part, grad_mixed, log_total, cot_part = (
        inputs
    )
    valid_rows, both_valid = block_masks(count_part, query_part.shape[1])
    logits = scores_of(query_part, key_part, pair_part, score_scale)
    masked = jnp.where(valid_rows[:, None, None, :], logits, -1e30)
    soft = jnp.exp(masked - log_total[..., None])
    grad_masked = jnp.where(valid_rows[:, :, None, None], grad_mixed, jnp.zeros_like(grad_mixed))
    grad_soft = jnp.einsum(
        "mqhd,mkhd->mhqk", grad_masked, value_part, preferred_element_type=jnp.float32
    )
    grad_scores = soft * (grad_soft - jnp.sum(grad_soft * soft, -1, keepdims=True))
    grad_scores = (grad_scores + jnp.where(both_valid, cot_part.astype(jnp.float32), 0.0)).astype(
        jnp.bfloat16
    )
    grad_query = (
        jnp.einsum("mhqk,mkhd->mqhd", grad_scores, key_part, preferred_element_type=jnp.float32)
        * score_scale
    ).astype(jnp.bfloat16)
    grad_key = (
        jnp.einsum("mhqk,mqhd->mkhd", grad_scores, query_part, preferred_element_type=jnp.float32)
        * score_scale
    ).astype(jnp.bfloat16)
    grad_value = jnp.einsum(
        "mhqk,mqhd->mkhd",
        soft.astype(jnp.bfloat16),
        grad_masked,
        preferred_element_type=jnp.float32,
    ).astype(jnp.bfloat16)
    return (grad_scores, grad_query, grad_key, grad_value)


def body_native(
    atoms, pair, counts, qkv_weight, out_weight, ln1_gain, ln2_gain, w_in, w_out, out_cot, pair_cot
):
    mols_here, heads_here, length = (pair.shape[0], pair.shape[1], pair.shape[2])
    qkv_full, out_full = (
        lax.all_gather(qkv_weight, "batch", axis=1, tiled=True),
        lax.all_gather(out_weight, "batch", axis=0, tiled=True),
    )
    gain_one, gain_two, inner_weight, outer_weight = (
        lax.all_gather(ln1_gain.astype(jnp.bfloat16), ("batch", "head"), axis=0, tiled=True).astype(
            ln1_gain.dtype
        ),
        lax.all_gather(ln2_gain.astype(jnp.bfloat16), ("batch", "head"), axis=0, tiled=True).astype(
            ln2_gain.dtype
        ),
        lax.all_gather(w_in, ("batch", "head"), axis=0, tiled=True),
        lax.all_gather(w_out, ("batch", "head"), axis=0, tiled=True),
    )
    width_here = qkv_full.shape[2]
    head_size = width_here // heads_here
    score_scale = head_size ** (-0.5)
    blocks = mols_here // 2
    group_total = mols_here * length
    atoms_f = atoms.astype(jnp.float32)
    normed_one, inverse_one = layer_stats(atoms_f)
    hidden_one = (normed_one * gain_one).astype(jnp.bfloat16)
    group_rows = lax.all_gather(hidden_one, "head", axis=0, tiled=True)
    projected = jnp.einsum(
        "rd,sde->sre", group_rows, qkv_full, preferred_element_type=jnp.float32
    ).astype(jnp.bfloat16)

    def to_blocks(values):
        return values.reshape(blocks, 2, length, heads_here, head_size)

    query_all, key_all, value_all = (
        to_blocks(projected[0]),
        to_blocks(projected[1]),
        to_blocks(projected[2]),
    )
    pair_blocks = pair.reshape(blocks, 2, heads_here, length, length)
    count_blocks = counts.reshape(blocks, 2)
    new_pair, mixed, log_total = lax.map(
        partial(attend_forward, score_scale=score_scale),
        (query_all, key_all, value_all, pair_blocks, count_blocks),
    )
    mixed_flat = mixed.reshape(group_total, width_here)
    slab_rows = mixed_flat
    attention = lax.psum_scatter(
        times_transposed(slab_rows, out_full).astype(jnp.bfloat16),
        "head",
        scatter_dimension=0,
        tiled=True,
    ).astype(jnp.float32)
    first_sum = atoms_f + attention
    normed_two, inverse_two = layer_stats(first_sum)
    hidden_two = (normed_two * gain_two).astype(jnp.bfloat16)
    inner = jnp.dot(hidden_two, inner_weight, preferred_element_type=jnp.float32)
    gelu_value, gelu_pull = jax.vjp(jax.nn.gelu, inner)
    activated = gelu_value.astype(jnp.bfloat16)
    output = first_sum + jnp.dot(activated, outer_weight, preferred_element_type=jnp.float32)
    grad_outer_w = transposed_times(activated, out_cot)
    grad_act = times_transposed(out_cot, outer_weight)
    grad_inner = gelu_pull(grad_act)[0].astype(jnp.bfloat16)
    grad_inner_w = transposed_times(hidden_two, grad_inner)
    grad_hidden_two = times_transposed(grad_inner, inner_weight)
    grad_gain_two = jnp.sum(grad_hidden_two * normed_two, 0)
    grad_first = out_cot.astype(jnp.float32) + norm_back(
        grad_hidden_two * gain_two, normed_two, inverse_two
    )
    grad_attention = grad_first.astype(jnp.bfloat16)
    group_grad = lax.all_gather(grad_attention, "head", axis=0, tiled=True)
    grad_out_full = transposed_times(group_grad, mixed_flat)
    grad_mixed = jnp.dot(group_grad, out_full, preferred_element_type=jnp.float32).astype(
        jnp.bfloat16
    )
    cot_blocks = pair_cot.reshape(blocks, 2, heads_here, length, length)
    grad_scores, grad_query, grad_key, grad_value = lax.map(
        partial(attend_backward, score_scale=score_scale),
        (
            query_all,
            key_all,
            value_all,
            pair_blocks,
            count_blocks,
            to_blocks(grad_mixed),
            log_total,
            cot_blocks,
        ),
    )
    grad_projected = jnp.stack(
        [
            grad_query.reshape(group_total, width_here),
            grad_key.reshape(group_total, width_here),
            grad_value.reshape(group_total, width_here),
        ]
    )
    grad_qkv_full = jnp.einsum(
        "rd,sre->sde", group_rows, grad_projected, preferred_element_type=jnp.float32
    )
    slab_rows = grad_projected
    grad_hidden_one = lax.psum_scatter(
        jnp.einsum("sre,sde->rd", slab_rows, qkv_full, preferred_element_type=jnp.float32).astype(
            jnp.bfloat16
        ),
        "head",
        scatter_dimension=0,
        tiled=True,
    ).astype(jnp.float32)
    grad_gain_one = jnp.sum(grad_hidden_one * normed_one, 0)
    atoms_grad = grad_first + norm_back(grad_hidden_one * gain_one, normed_one, inverse_one)
    qkv_grad, out_grad = (
        lax.psum_scatter(
            grad_qkv_full.astype(jnp.bfloat16), "batch", scatter_dimension=1, tiled=True
        ).astype(jnp.float32),
        lax.psum_scatter(
            grad_out_full.astype(jnp.bfloat16), "batch", scatter_dimension=0, tiled=True
        ).astype(jnp.float32),
    )
    gain_one_grad, gain_two_grad, inner_grad, outer_grad = (
        lax.psum_scatter(grad_gain_one, ("batch", "head"), scatter_dimension=0, tiled=True),
        lax.psum_scatter(grad_gain_two, ("batch", "head"), scatter_dimension=0, tiled=True),
        lax.psum_scatter(grad_inner_w, ("batch", "head"), scatter_dimension=0, tiled=True),
        lax.psum_scatter(grad_outer_w, ("batch", "head"), scatter_dimension=0, tiled=True),
    )
    return (
        output.astype(jnp.bfloat16),
        new_pair.reshape(mols_here, heads_here, length, length),
        atoms_grad.astype(jnp.bfloat16),
        grad_scores.reshape(mols_here, heads_here, length, length),
        qkv_grad,
        out_grad,
        gain_one_grad,
        gain_two_grad,
        inner_grad,
        outer_grad,
    )


def dot(left, right):
    return jnp.dot(left, right, preferred_element_type=F32)


def dot_nt(left, right):
    return lax.dot_general(left, right, (((1,), (1,)), ((), ())), preferred_element_type=F32)


def dot_tn(left, right):
    return lax.dot_general(left, right, (((0,), (0,)), ((), ())), preferred_element_type=F32)


def swap(values, axes, count, bit):
    return lax.ppermute(values, axes, [(i, i ^ bit) for i in range(count)])


def relative(position, bits):
    return sum(((position >> k) & 1) * bit for k, bit in enumerate(bits))


def whole(shape):
    return pl.BlockSpec(shape, lambda *_: (0,) * len(shape))


def prep_kernel(me_ref, near_ref, far_ref, w_ref, gains_ref, rows_s, *, bits, heads_bits, shard):
    b, h = me_ref[0], me_ref[1]
    half = near_ref.shape[0]
    rows = w_ref.shape[1] // (2 * half)
    dim = gains_ref.shape[1]
    for p in range(2 * half):
        ref, q = (near_ref, p) if p < half else (far_ref, p - half)
        at = pl.multiple_of((b ^ relative(p, bits)) * rows, rows)
        for s in range(3):
            w_ref[s, pl.ds(at, rows), :] = ref[q, s * rows : (s + 1) * rows, :]
        rows_s[p : p + 1, :] = ref[q, 3 * rows : 3 * rows + 1, :].astype(F32)
    lanes = rows_s.shape[1]
    count = 2 * half
    lane = lax.broadcasted_iota(jnp.int32, (lanes, dim), 0)
    col = lax.broadcasted_iota(jnp.int32, (lanes, dim), 1)
    block = lax.broadcasted_iota(jnp.int32, (count, dim), 1) // rows
    place = lax.broadcasted_iota(jnp.int32, (count, dim), 0)
    owner = sum(((place >> k) & 1) * bit for k, bit in enumerate(bits)) ^ b
    values = rows_s[...].astype(BF16)
    for g in range(2):
        start = (((col // shard) & 1) ^ h) * (4 * shard) + g * 2 * shard + lax.rem(col, shard)
        pick = jnp.where((lane == start) | (lane == start + shard), 1.0, 0.0).astype(BF16)
        spread = dot(values, pick)
        gains_ref[g : g + 1, :] = jnp.sum(jnp.where(owner == block, spread, 0.0), 0, keepdims=True)


def attend_forward_kernel(
    mol_ref, cnt_ref, atoms_ref, w_ref, gains_ref, mask_ref, pair_ref, *rest,
    hb, groups, scale, carried
):
    new_ref, exp_ref, hid_t_ref, qkv_ref, mixed_ref, inv_ref, q_s, kt_s, v_s, sum_s = rest[carried:]
    step = pl.program_id(1)
    length = atoms_ref.shape[0]
    lanes = w_ref.shape[2] // groups
    per_group = lanes // (8 * hb)
    count = cnt_ref[mol_ref[pl.program_id(0)]]

    @pl.when(step == 0)
    def _():
        values = atoms_ref[...].astype(F32)
        center = values - jnp.mean(values, -1, keepdims=True)
        inverse = lax.rsqrt(jnp.mean(center * center, -1, keepdims=True) + 1e-05)
        hidden = (center * inverse * gains_ref[0:1, :]).astype(BF16)
        hid_t_ref[...] = hidden.T
        query = (dot(hidden, w_ref[0]) * scale).astype(BF16)
        key = dot(hidden, w_ref[1]).astype(BF16)
        value = dot(hidden, w_ref[2]).astype(BF16)
        qkv_ref[0] = query
        qkv_ref[1] = key
        qkv_ref[2] = value
        key_t = key.T
        at = lax.broadcasted_iota(jnp.int32, (1, length), 1)
        bias = jnp.where(at < count, 0.0, NEG)
        first = lax.broadcasted_iota(jnp.int32, (lanes, length), 0) == 0
        bias_rows = jnp.where(first, bias, 0.0).astype(BF16)
        ones_lane = (lax.broadcasted_iota(jnp.int32, (length, lanes), 1) == 0).astype(F32).astype(BF16)
        for g in range(groups):
            part = slice(g * lanes, (g + 1) * lanes)
            q_s[g, :, :lanes] = query[:, part]
            q_s[g, :, lanes:] = ones_lane
            kt_s[g, :lanes, :] = key_t[part]
            kt_s[g, lanes:, :] = bias_rows
            v_s[g, :, :lanes] = value[:, part]
            v_s[g, :, lanes:] = jnp.ones((length, lanes), BF16)

    g = step // per_group
    block = lax.rem(step, per_group)
    valid = (lax.broadcasted_iota(jnp.int32, (length, length), 0) < count) & (
        lax.broadcasted_iota(jnp.int32, (length, length), 1) < count
    )
    total = jnp.zeros((length, 2 * lanes), F32)
    for i in range(hb):
        logits = dot(q_s[g] * mask_ref[0, block, i : i + 1, :], kt_s[g]) + pair_ref[0, i].astype(F32)
        new_ref[0, i] = jnp.where(valid, logits, 0.0).astype(BF16)
        exp_ref[0, i] = jnp.exp(logits - jnp.max(logits, -1, keepdims=True)).astype(BF16)
        total = total + dot(exp_ref[0, i], v_s[g] * mask_ref[1, block, i : i + 1, :])

    @pl.when(block == 0)
    def _():
        sum_s[...] = total

    @pl.when(block > 0)
    def _():
        sum_s[...] = sum_s[...] + total

    @pl.when(block == per_group - 1)
    def _():
        inverse = 1.0 / sum_s[:, lanes:]
        rows_ok = lax.broadcasted_iota(jnp.int32, (length, lanes), 0) < count
        at = pl.ds(pl.multiple_of(g * lanes, lanes), lanes)
        inv_ref[:, at] = inverse
        mixed_ref[:, at] = jnp.where(rows_ok, sum_s[:, :lanes] * inverse, 0.0).astype(BF16)


def head_masks(groups, width, hb, backward):
    lanes = width // groups
    heads = lanes // 8
    masks = np.zeros((2, heads, 2 * lanes), np.float32)
    for h in range(heads):
        own = slice(h * 8, (h + 1) * 8)
        twin = slice(lanes + h * 8, lanes + (h + 1) * 8)
        masks[0, h, own] = 1
        masks[1, h, own] = 1
        if backward:
            masks[0, h, twin] = 1
        else:
            masks[0, h, lanes] = 1
            masks[1, h, twin] = 1
    return jnp.asarray(masks.reshape(2, heads // hb, hb, 2 * lanes), BF16)


def specs_of(length, hb):
    pair = pl.BlockSpec((1, hb, length, length), lambda i, j, mol, cnt: (mol[i], j, 0, 0))
    rows = lambda cols: pl.BlockSpec((length, cols), lambda i, j, mol, cnt: (i, 0))
    three = lambda cols: pl.BlockSpec((3, length, cols), lambda i, j, mol, cnt: (0, i, 0))
    return pair, rows, three


ANY = pl.BlockSpec(memory_space=pl.ANY)


def attend_forward_call(mols, counts, atoms, weights, gains, pair, carried, hb=16):
    n, (_, heads, length, _) = mols.shape[0], pair.shape
    dim, width = atoms.shape[1], weights.shape[2]
    groups = max(1, width // 128)
    lanes = width // groups
    masks = head_masks(groups, width, hb, False)
    pair_spec, rows, three = specs_of(length, hb)
    args = [atoms, weights, gains, masks, pair, *carried]
    spec = pltpu.PrefetchScalarGridSpec(
        num_scalar_prefetch=2,
        grid=(n, heads // hb),
        in_specs=[rows(dim), whole(weights.shape), whole(gains.shape), whole(masks.shape), pair_spec]
        + [ANY] * len(carried),
        out_specs=[
            pair_spec,
            pair_spec,
            pl.BlockSpec((dim, length), lambda i, j, mol, cnt: (0, i)),
            three(width),
            rows(width),
            rows(width),
        ],
        scratch_shapes=[
            pltpu.VMEM((groups, length, 2 * lanes), BF16),
            pltpu.VMEM((groups, 2 * lanes, length), BF16),
            pltpu.VMEM((groups, length, 2 * lanes), BF16),
            pltpu.VMEM((length, 2 * lanes), F32),
        ],
    )
    shape = jax.ShapeDtypeStruct
    return pl.pallas_call(
        partial(
            attend_forward_kernel,
            hb=hb,
            groups=groups,
            scale=8**-0.5,
            carried=len(carried),
        ),
        grid_spec=spec,
        out_shape=[
            shape(pair.shape, BF16),
            shape(pair.shape, BF16),
            shape((dim, n * length), BF16),
            shape((3, n * length, width), BF16),
            shape((n * length, width), BF16),
            shape((n * length, width), F32),
        ],
        input_output_aliases={7: 0, 8: 1} if carried else {},
        compiler_params=pltpu.CompilerParams(
            dimension_semantics=("arbitrary", "arbitrary"), vmem_limit_bytes=48 << 20
        ),
        cost_estimate=pl.CostEstimate(
            flops=n * heads * 4 * length**3,
            transcendentals=n * heads * length**2,
            bytes_accessed=6 * n * heads * length**2,
        ),
        name="attend_forward",
    )(mols, counts, *args)


def attend_backward_kernel(
    mol_ref, cnt_ref, gm_ref, mixed_ref, inv_ref, qkv_ref, w_ref, mask_ref, exp_ref, cot_ref, *rest,
    hb, groups, scale, carried
):
    pg_ref, gp_ref, gh_ref, l_s, r_s, k_s, qt_s, gt_s, gq_s, gk_s, gv_s = rest[carried:]
    step, steps = pl.program_id(1), pl.num_programs(1)
    length, width = gm_ref.shape
    lanes = width // groups
    per_group = lanes // (8 * hb)
    count = cnt_ref[mol_ref[pl.program_id(0)]]

    @pl.when(step == 0)
    def _():
        rows_ok = lax.broadcasted_iota(jnp.int32, (length, width), 0) < count
        scaled = jnp.where(rows_ok, gm_ref[...].astype(F32) * inv_ref[...], 0.0).astype(BF16)
        wide = scaled.astype(F32)
        delta = (-(wide * mixed_ref[...].astype(F32))).astype(BF16)
        value_t = qkv_ref[2].T
        for g in range(groups):
            part = slice(g * lanes, (g + 1) * lanes)
            l_s[g, :, :lanes] = scaled[:, part]
            l_s[g, :, lanes:] = delta[:, part]
            r_s[g, :lanes, :] = value_t[part]
            r_s[g, lanes:, :] = jnp.ones((lanes, length), BF16)
            k_s[g] = qkv_ref[1, :, part]
        qt_s[...] = qkv_ref[0].astype(F32).T.reshape(qt_s.shape).astype(BF16)
        gt_s[...] = wide.T.reshape(gt_s.shape).astype(BF16)

    g = step // per_group
    block = lax.rem(step, per_group)
    valid = (lax.broadcasted_iota(jnp.int32, (length, length), 0) < count) & (
        lax.broadcasted_iota(jnp.int32, (length, length), 1) < count
    )
    total = jnp.zeros((length, lanes), F32)
    for i in range(hb):
        soft = dot(l_s[g] * mask_ref[0, block, i : i + 1, :], r_s[g])
        scores = exp_ref[0, i].astype(F32) * soft + jnp.where(valid, cot_ref[0, i].astype(F32), 0.0)
        pg_ref[0, i] = scores.astype(BF16)
        total = total + dot(pg_ref[0, i], k_s[g] * mask_ref[1, block, i : i + 1, :lanes])
        head = step * hb + i
        gk_s[head] = dot(qt_s[head], pg_ref[0, i])
        gv_s[head] = dot(gt_s[head], exp_ref[0, i])

    @pl.when(block == 0)
    def _():
        gq_s[g] = total

    @pl.when(block > 0)
    def _():
        gq_s[g] = gq_s[g] + total

    @pl.when(step == steps - 1)
    def _():
        for k in range(groups):
            gp_ref[0, :, k * lanes : (k + 1) * lanes] = (gq_s[k] * scale).astype(BF16)
        gp_ref[1] = gk_s[...].reshape(width, length).T.astype(BF16)
        gp_ref[2] = gv_s[...].reshape(width, length).T.astype(BF16)
        gh_ref[...] = (
            dot_nt(gp_ref[0], w_ref[0]) + dot_nt(gp_ref[1], w_ref[1]) + dot_nt(gp_ref[2], w_ref[2])
        ).astype(BF16)


def attend_backward_call(mols, counts, gm, mixed, inverse, qkv, weights, exps, cot, carried, hb=16):
    n, (_, heads, length, _) = mols.shape[0], exps.shape
    dim, width = weights.shape[1], weights.shape[2]
    groups = max(1, width // 128)
    lanes = width // groups
    masks = head_masks(groups, width, hb, True)
    pair_spec, rows, three = specs_of(length, hb)
    args = [gm, mixed, inverse, qkv, weights, masks, exps, cot, *carried]
    spec = pltpu.PrefetchScalarGridSpec(
        num_scalar_prefetch=2,
        grid=(n, heads // hb),
        in_specs=[
            rows(width), rows(width), rows(width), three(width),
            whole(weights.shape), whole(masks.shape), pair_spec, pair_spec,
        ] + [ANY] * len(carried),
        out_specs=[pair_spec, three(width), rows(dim)],
        scratch_shapes=[
            pltpu.VMEM((groups, length, 2 * lanes), BF16),
            pltpu.VMEM((groups, 2 * lanes, length), BF16),
            pltpu.VMEM((groups, length, lanes), BF16),
            pltpu.VMEM((heads, 8, length), BF16),
            pltpu.VMEM((heads, 8, length), BF16),
            pltpu.VMEM((groups, length, lanes), F32),
            pltpu.VMEM((heads, 8, length), F32),
            pltpu.VMEM((heads, 8, length), F32),
        ],
    )
    shape = jax.ShapeDtypeStruct
    return pl.pallas_call(
        partial(
            attend_backward_kernel,
            hb=hb,
            groups=groups,
            scale=8**-0.5,
            carried=len(carried),
        ),
        grid_spec=spec,
        out_shape=[
            shape(exps.shape, BF16),
            shape((3, n * length, width), BF16),
            shape((n * length, dim), BF16),
        ],
        input_output_aliases={10: 0} if carried else {},
        compiler_params=pltpu.CompilerParams(
            dimension_semantics=("arbitrary", "arbitrary"), vmem_limit_bytes=48 << 20
        ),
        cost_estimate=pl.CostEstimate(
            flops=n * heads * 6 * length**3,
            transcendentals=0,
            bytes_accessed=6 * n * heads * length**2,
        ),
        name="attend_backward",
    )(mols, counts, *args)


ROOT = (2 / np.pi) ** 0.5


def layer_kernel(
    me_ref, atoms_ref, mine_ref, other_ref, cot_ref, gains_ref, a0_ref, a1_ref, b0_ref, b1_ref,
    out_ref, first_ref, gm_mine_ref, gm_other_ref, ga0_ref, ga1_ref, gb0_ref, gb1_ref,
    win_s, wout_s, ow_s, sum_s, acc_s, gh_s, normed_s, inv_s, hid_s, hid_t_s, *, bits_a, bits_b
):
    me = me_ref[0]
    c, steps = pl.program_id(0), pl.num_programs(0)
    half = a0_ref.shape[0]
    dim = atoms_ref.shape[1]
    width = mine_ref.shape[1]
    rows = dim // (2 * half)
    ff_rows = b0_ref.shape[1]
    e_rows = dim // half

    def shards(bits, near, far):
        for p in range(2 * half):
            yield p, me ^ relative(p, bits), (near, p) if p < half else (far, p - half)

    @pl.when(c == 0)
    def _():
        for p, owner, (ref, q) in shards(bits_a, a0_ref, a1_ref):
            for k in range(4):
                win_s[k, pl.ds(pl.multiple_of(owner * rows, rows), rows), :] = ref[q, k * rows : (k + 1) * rows, :]
            at = pl.multiple_of((owner // 2) * e_rows, e_rows)
            for k in range(2):
                ow_s[relative(p, bits_a) & 1, pl.ds(at + k * rows, rows), :] = ref[q, 4 * rows :, k * width : (k + 1) * width]
        for p, owner, (ref, q) in shards(bits_b, b0_ref, b1_ref):
            wout_s[pl.ds(pl.multiple_of(owner * ff_rows, ff_rows), ff_rows), :] = ref[q]
        first_sum = (
            atoms_ref[...].astype(F32) + dot_nt(mine_ref[...], ow_s[0]) + dot_nt(other_ref[...], ow_s[1])
        )
        sum_s[...] = first_sum
        center = first_sum - jnp.mean(first_sum, -1, keepdims=True)
        inverse = lax.rsqrt(jnp.mean(center * center, -1, keepdims=True) + 1e-05)
        normed = center * inverse
        normed_s[...] = normed
        inv_s[...] = inverse
        hidden = (normed * gains_ref[1:2, :]).astype(BF16)
        hid_s[...] = hidden
        hid_t_s[...] = hidden.T
        acc_s[...] = jnp.zeros_like(acc_s)
        gh_s[...] = jnp.zeros_like(gh_s)

    win = win_s[c]
    wout = wout_s[pl.ds(pl.multiple_of(c * dim, dim), dim), :]
    inner = dot(hid_s[...], win)
    square = inner * inner
    tanh = jnp.tanh(ROOT * inner * (1.0 + 0.044715 * square))
    activated = (0.5 * inner * (1.0 + tanh)).astype(BF16)
    slope = 0.5 * (1.0 + tanh) + (0.5 * ROOT) * inner * (1.0 - tanh * tanh) * (1.0 + (3 * 0.044715) * square)
    acc_s[...] += dot(activated, wout)
    grad_inner = (dot_nt(cot_ref[...], wout) * slope).astype(BF16)
    gh_s[...] += dot_nt(grad_inner, win)
    grad_in = dot(hid_t_s[...], grad_inner).astype(BF16)
    win_s[c] = grad_in
    grad_out = dot_tn(activated, cot_ref[...]).astype(BF16)
    wout_s[pl.ds(pl.multiple_of(c * dim, dim), dim), :] = grad_out

    @pl.when(c == steps - 1)
    def _():
        out_ref[...] = (sum_s[...] + acc_s[...]).astype(BF16)
        normed = normed_s[...]
        grad_norm = gh_s[...] * gains_ref[1:2, :]
        grad_first = cot_ref[...].astype(F32) + inv_s[...] * (
            grad_norm
            - jnp.mean(grad_norm, -1, keepdims=True)
            - normed * jnp.mean(grad_norm * normed, -1, keepdims=True)
        )
        first_ref[...] = grad_first
        grad_attention = grad_first.astype(BF16)
        gm_mine_ref[...] = dot(grad_attention, ow_s[0]).astype(BF16)
        gm_other_ref[...] = dot(grad_attention, ow_s[1]).astype(BF16)
        ow_s[0] = dot_tn(grad_attention, mine_ref[...]).astype(BF16)
        ow_s[1] = dot_tn(grad_attention, other_ref[...]).astype(BF16)
        for p, owner, (ref, q) in shards(bits_a, ga0_ref, ga1_ref):
            for k in range(4):
                ref[q, k * rows : (k + 1) * rows, :] = win_s[k, pl.ds(pl.multiple_of(owner * rows, rows), rows), :]
            at = pl.multiple_of((owner // 2) * e_rows, e_rows)
            for k in range(2):
                ref[q, 4 * rows :, k * width : (k + 1) * width] = ow_s[relative(p, bits_a) & 1, pl.ds(at + k * rows, rows), :]
        for p, owner, (ref, q) in shards(bits_b, gb0_ref, gb1_ref):
            ref[q] = wout_s[pl.ds(pl.multiple_of(owner * ff_rows, ff_rows), ff_rows), :]


def layer_call(me, atoms, mine, other, cot, gains, a_pair, b_pair, bits_a, bits_b):
    own, dim = atoms.shape
    width = mine.shape[1]
    ff = 2 * b_pair[0].shape[0] * b_pair[0].shape[1]
    args = [atoms, mine, other, cot, gains, *a_pair, *b_pair]
    shape = jax.ShapeDtypeStruct
    outs = [
        shape((own, dim), BF16),
        shape((own, dim), F32),
        shape((own, width), BF16),
        shape((own, width), BF16),
        *[shape(x.shape, BF16) for x in (*a_pair, *b_pair)],
    ]
    spec = pltpu.PrefetchScalarGridSpec(
        num_scalar_prefetch=1,
        grid=(ff // dim,),
        in_specs=[whole(x.shape) for x in args],
        out_specs=[whole(x.shape) for x in outs],
        scratch_shapes=[
            pltpu.VMEM((ff // dim, dim, dim), BF16),
            pltpu.VMEM((ff, dim), BF16),
            pltpu.VMEM((2, dim, width), BF16),
            pltpu.VMEM((own, dim), F32),
            pltpu.VMEM((own, dim), F32),
            pltpu.VMEM((own, dim), F32),
            pltpu.VMEM((own, dim), F32),
            pltpu.VMEM((own, 1), F32),
            pltpu.VMEM((own, dim), BF16),
            pltpu.VMEM((dim, own), BF16),
        ],
    )
    return pl.pallas_call(
        partial(layer_kernel, bits_a=bits_a, bits_b=bits_b),
        grid_spec=spec,
        out_shape=outs,
        compiler_params=pltpu.CompilerParams(
            dimension_semantics=("arbitrary",), vmem_limit_bytes=60 << 20
        ),
        cost_estimate=pl.CostEstimate(
            flops=12 * own * dim * ff, transcendentals=own * ff, bytes_accessed=8 * dim * ff
        ),
        name="layer",
    )(me, *args)


def project_grad_kernel(me_ref, *refs, bits, parts):
    b = me_ref[0]
    near_ref, far_ref, full_s = refs[2 * parts :]
    half = near_ref.shape[0]
    rows = full_s.shape[1] // (2 * half)
    for s in range(3):
        full_s[s] = sum(dot(refs[k][...], refs[parts + k][s]) for k in range(parts)).astype(BF16)
    for p in range(2 * half):
        ref, q = (near_ref, p) if p < half else (far_ref, p - half)
        at = pl.multiple_of((b ^ relative(p, bits)) * rows, rows)
        for s in range(3):
            ref[q, s * rows : (s + 1) * rows, :] = full_s[s, pl.ds(at, rows), :]


def project_grad_call(me, hid_ts, gps, bits):
    dim, width = hid_ts[0].shape[0], gps[0].shape[2]
    half = 2 ** (len(bits) - 1)
    rows = dim // (2 * half)
    args = [*hid_ts, *gps]
    outs = [jax.ShapeDtypeStruct((half, 3 * rows, width), BF16)] * 2
    return pl.pallas_call(
        partial(project_grad_kernel, bits=bits, parts=len(hid_ts)),
        grid_spec=pltpu.PrefetchScalarGridSpec(
            num_scalar_prefetch=1,
            grid=(1,),
            in_specs=[whole(x.shape) for x in args],
            out_specs=[whole(x.shape) for x in outs],
            scratch_shapes=[pltpu.VMEM((3, dim, width), BF16)],
        ),
        out_shape=outs,
        compiler_params=pltpu.CompilerParams(vmem_limit_bytes=32 << 20),
        name="project_grad",
    )(me, *args)


def last_kernel(atoms_ref, gains_ref, first_ref, ga_ref, gb_ref, recv_ref, out_ref):
    values = atoms_ref[...].astype(F32)
    center = values - jnp.mean(values, -1, keepdims=True)
    inverse = lax.rsqrt(jnp.mean(center * center, -1, keepdims=True) + 1e-05)
    normed = center * inverse
    part = ga_ref.shape[0]
    grads = jnp.concatenate([ga_ref[...], gb_ref[...]], 0).astype(F32) + recv_ref[...].astype(F32)
    grad_norm = grads * gains_ref[0:1, :]
    out_ref[...] = (
        first_ref[...]
        + inverse
        * (
            grad_norm
            - jnp.mean(grad_norm, -1, keepdims=True)
            - normed * jnp.mean(grad_norm * normed, -1, keepdims=True)
        )
    ).astype(BF16)


def last_call(atoms, gains, first, gh_a, gh_b, recv):
    args = [atoms, gains, first, gh_a, gh_b, recv]
    return pl.pallas_call(
        last_kernel,
        grid=(1,),
        in_specs=[whole(x.shape) for x in args],
        out_specs=whole(atoms.shape),
        out_shape=jax.ShapeDtypeStruct(atoms.shape, BF16),
        compiler_params=pltpu.CompilerParams(vmem_limit_bytes=32 << 20),
        name="last_norm",
    )(*args)


def join(values, received):
    return jnp.concatenate([values, received], 0)


def add(kept, received):
    return (kept.astype(F32) + received.astype(F32)).astype(BF16)


def halves(values):
    half = values.shape[0] // 2
    return values[:half], values[half:]


def body_pairs(
    atoms, pair, counts, qkv_weight, out_weight, ln1_gain, ln2_gain, w_in, w_out, out_cot, pair_cot,
    batch
):
    b = lax.axis_index("batch")
    h = lax.axis_index("head")
    own, dim = atoms.shape
    length = pair.shape[2]
    width = qkv_weight.shape[2]
    shard = ln1_gain.shape[0]
    top = batch.bit_length() - 1
    far_bits = [1 << k for k in range(top - 1, 1, -1)]
    batch_bits = [*far_bits, 2, 1]
    bits_a = [2 * bit for bit in far_bits] + [4, 1, 2]
    bits_b = [2 * bit for bit in far_bits] + [1, 4, 2]
    nz = len(far_bits)
    over_batch = lambda x, bit: swap(x, "batch", batch, bit)
    over_head = lambda x: swap(x, "head", 2, 1)
    over_both = lambda x, bit: swap(x, BOTH, 2 * batch, bit)

    tie = lax.optimization_barrier

    def split_gain(gain):
        high = gain.astype(BF16)
        return [high, (gain - high.astype(F32)).astype(BF16)]

    gain_row = jnp.concatenate(split_gain(ln1_gain) + split_gain(ln2_gain))[None]
    gain_row = jnp.concatenate([gain_row, over_head(gain_row)], 1)
    tail = jnp.pad(gain_row, ((0, 15), (0, width - gain_row.shape[1])))
    gathered = jnp.concatenate([qkv_weight.reshape(-1, width), tail], 0)[None]
    for bit in far_bits:
        gathered = join(gathered, over_batch(gathered, bit))
    e_rows = out_weight.shape[0]
    blocks = w_in.shape[1] // dim
    in_rows = [w_in[:, k * dim : (k + 1) * dim] for k in range(blocks)]
    out_rows = jnp.concatenate([out_weight[: e_rows // 2], out_weight[e_rows // 2 :]], 1)
    bulk = jnp.concatenate([*in_rows, out_rows, w_out], 0)[None]
    cut = bulk.shape[1] - w_out.shape[0]
    gathered, bulk = tie((gathered, bulk))
    atoms_other = over_head(atoms)
    gathered = join(gathered, over_batch(gathered, 2))
    far = over_batch(gathered, 1)
    me_batch = jnp.stack([b, h])
    weights, gains = pl.pallas_call(
        partial(prep_kernel, bits=batch_bits, heads_bits=1, shard=shard),
        grid_spec=pltpu.PrefetchScalarGridSpec(
            num_scalar_prefetch=1,
            grid=(1,),
            in_specs=[whole(gathered.shape)] * 2,
            out_specs=[whole((3, dim, width)), whole((2, dim))],
            scratch_shapes=[pltpu.VMEM((batch, width), F32)],
        ),
        out_shape=[jax.ShapeDtypeStruct((3, dim, width), BF16), jax.ShapeDtypeStruct((2, dim), F32)],
        name="prepare",
    )(me_batch, gathered, far)

    per = own // length
    mine, theirs = h * per, (1 - h) * per
    plan = [(mine, atoms[:length])]
    plan += [(theirs + k, atoms_other[k * length : (k + 1) * length]) for k in range(per)]
    plan += [(mine + k, atoms[k * length : (k + 1) * length]) for k in range(1, per)]
    plan = [(mol[None], rows) for mol, rows in plan]
    stage_bits = [(bit, bit) for bit in bits_a[:nz]] + list(zip(bits_a[nz:], bits_b[nz:]))
    parts = (bulk,)

    def send_stage(parts, k):
        return tuple(over_both(x, bit) for x, bit in zip(parts, stage_bits[k]))

    received = send_stage(parts, 0)
    received, gains = tie((received, gains))
    cnt = counts
    carried = ()
    saved = []
    for k, (mols, rows) in enumerate(plan):
        if k < len(stage_bits) - 1:
            parts = tuple(map(join, parts, received))
            if k + 1 == nz:
                parts = (parts[0][:, :cut], parts[0][:, cut:])
            cnt, parts = tie((cnt, parts))
        if k < len(stage_bits) - 2:
            received = send_stage(parts, k + 1)
        new_pair, exps, *rest = attend_forward_call(mols, cnt, rows, weights, gains, pair, carried)
        if k < len(stage_bits) - 2:
            received, rest = tie((received, rest))
        carried = (new_pair, exps)
        saved.append(rest)
    a_pair = (parts[0], over_both(parts[0], bits_a[-1]))
    b_pair = (parts[1], over_both(parts[1], bits_b[-1]))
    mixed_theirs = jnp.concatenate([s[2] for s in saved[1 : 1 + per]], 0)
    mixed_other = over_head(mixed_theirs)
    mixed_mine = jnp.concatenate([saved[0][2], *[s[2] for s in saved[1 + per :]]], 0)

    me = (2 * b + h)[None]
    output, first, gm_mine, gm_other, ga0, ga1, gb0, gb1 = layer_call(
        me, atoms, mixed_mine, mixed_other, out_cot, gains, a_pair, b_pair, bits_a, bits_b
    )
    gm_received = over_head(gm_other)

    def scatter_stage(parts, k):
        if k == nz - 1:
            parts = (jnp.concatenate(parts, 1),)
        return tuple(
            add(keep, over_both(send, bit))
            for (keep, send), bit in zip(map(halves, parts), stage_bits[k])
        )

    parts = (add(ga0, over_both(ga1, bits_a[-1])), add(gb0, over_both(gb1, bits_b[-1])))
    gm_parts = [gm_mine[:length]]
    gm_parts += [gm_received[k * length : (k + 1) * length] for k in range(per)]
    gm_parts += [gm_mine[k * length : (k + 1) * length] for k in range(1, per)]
    carried = ()
    grads = []
    stage = len(stage_bits) - 2
    cnt = counts
    for k, ((mols, _), gm, (hid_t, qkv, mixed, inverse)) in enumerate(zip(plan, gm_parts, saved)):
        if k > 0:
            cnt, parts = tie((cnt, parts))
            parts = scatter_stage(parts, stage)
            stage -= 1
        pair_grad, *rest = attend_backward_call(
            mols, cnt, gm, mixed, inverse, qkv, weights, exps, pair_cot, carried
        )
        carried = (pair_grad,)
        grads.append(rest)
    hidden_received = over_head(jnp.concatenate([g[1] for g in grads[1 : 1 + per]], 0))
    near, far = project_grad_call(
        me_batch, [s[0] for s in saved], [g[0] for g in grads], batch_bits
    )
    near = add(near, over_batch(far, batch_bits[-1]))
    for bit in batch_bits[-2::-1]:
        keep, send = halves(near)
        near = add(keep, over_batch(send, bit))
    qkv_grad = near[0].reshape(qkv_weight.shape).astype(F32)
    gain_part = jnp.sum(qkv_grad * qkv_weight.astype(F32), (0, 2)).reshape(2, shard)
    gain_mine = lax.dynamic_index_in_dim(gain_part, h, 0, False)
    gain_other = over_head(lax.dynamic_index_in_dim(gain_part, 1 - h, 0, False))
    gain_one_grad = (gain_mine + gain_other) / ln1_gain
    atoms_grad = last_call(atoms, gains, first, grads[0][1], grads[-1][1], hidden_received)
    while stage >= 0:
        parts = scatter_stage(parts, stage)
        stage -= 1
    bulk = parts[0][0].astype(F32)
    shard_rows = w_in.shape[0]
    in_grad = jnp.concatenate([bulk[k * shard_rows : (k + 1) * shard_rows] for k in range(blocks)], 1)
    out_grad = jnp.concatenate([bulk[blocks * shard_rows : cut, k * width : (k + 1) * width] for k in range(2)], 0)
    outer_grad = bulk[cut:]
    gain_two_grad = jnp.sum(in_grad * w_in.astype(F32), 1) / ln2_gain
    return (
        output, new_pair, atoms_grad, pair_grad, qkv_grad, out_grad,
        gain_one_grad, gain_two_grad, in_grad, outer_grad,
    )


def solution(mesh):
    rows = P(BOTH, None)
    heads = P("batch", "head", None, None)
    batch, head = mesh.shape["batch"], mesh.shape["head"]
    body = partial(body_pairs, batch=batch) if (batch, head) == (16, 2) else body_native
    return jax.shard_map(
        body,
        mesh=mesh,
        in_specs=(
            rows, heads, P("batch"), P(None, "batch", "head"), P("batch", "head"),
            P(BOTH), P(BOTH), rows, rows, rows, heads,
        ),
        out_specs=(
            rows, heads, rows, heads, P(None, "batch", "head"), P("batch", "head"),
            P(BOTH), P(BOTH), rows, rows,
        ),
        check_vma=False,
    )
```

```python
from functools import partial

import jax
import jax.numpy as jnp
import numpy as np
from jax import lax
from jax.experimental import pallas as pl
from jax.experimental.pallas import tpu as pltpu
from jax.sharding import PartitionSpec as P

F32 = jnp.float32
BF16 = jnp.bfloat16
NEG = -1e30
VMEM_LIMIT = 48 << 20
BOTH = ("batch", "head")


def layer_stats(values):
    center = values - jnp.mean(values, -1, keepdims=True)
    inverse = lax.rsqrt(jnp.mean(center * center, -1, keepdims=True) + 1e-05)
    return (center * inverse, inverse)


def norm_back(grad_norm, normed, inverse):
    return inverse * (
        grad_norm
        - jnp.mean(grad_norm, -1, keepdims=True)
        - normed * jnp.mean(grad_norm * normed, -1, keepdims=True)
    )


def times_transposed(left, right):
    return lax.dot_general(
        left, right, (((1,), (1,)), ((), ())), preferred_element_type=jnp.float32
    )


def transposed_times(left, right):
    return lax.dot_general(
        left, right, (((0,), (0,)), ((), ())), preferred_element_type=jnp.float32
    )


def block_masks(count_part, length):
    positions = jnp.arange(length, dtype=jnp.int32)
    valid_rows = positions[None, :] < count_part[:, None]
    both_valid = valid_rows[:, None, :, None] & valid_rows[:, None, None, :]
    return (valid_rows, both_valid)


def scores_of(query_part, key_part, pair_part, score_scale):
    raw = jnp.einsum("mqhd,mkhd->mhqk", query_part, key_part, preferred_element_type=jnp.float32)
    return raw * score_scale + pair_part.astype(jnp.float32)


def attend_forward(inputs, score_scale):
    query_part, key_part, value_part, pair_part, count_part = inputs
    valid_rows, both_valid = block_masks(count_part, query_part.shape[1])
    logits = scores_of(query_part, key_part, pair_part, score_scale)
    new_pair = jnp.where(both_valid, logits, 0.0).astype(jnp.bfloat16)
    masked = jnp.where(valid_rows[:, None, None, :], logits, -1e30)
    row_max = jnp.max(masked, -1, keepdims=True)
    exponent = jnp.exp(masked - row_max)
    row_total = jnp.sum(exponent, -1, keepdims=True)
    soft_weights = (exponent / row_total).astype(jnp.bfloat16)
    mixed = jnp.einsum(
        "mhqk,mkhd->mqhd", soft_weights, value_part, preferred_element_type=jnp.float32
    )
    mixed = jnp.where(valid_rows[:, :, None, None], mixed, 0.0).astype(jnp.bfloat16)
    return (new_pair, mixed, row_max[..., 0] + jnp.log(row_total[..., 0]))


def attend_backward(inputs, score_scale):
    query_part, key_part, value_part, pair_part, count_part, grad_mixed, log_total, cot_part = (
        inputs
    )
    valid_rows, both_valid = block_masks(count_part, query_part.shape[1])
    logits = scores_of(query_part, key_part, pair_part, score_scale)
    masked = jnp.where(valid_rows[:, None, None, :], logits, -1e30)
    soft = jnp.exp(masked - log_total[..., None])
    grad_masked = jnp.where(valid_rows[:, :, None, None], grad_mixed, jnp.zeros_like(grad_mixed))
    grad_soft = jnp.einsum(
        "mqhd,mkhd->mhqk", grad_masked, value_part, preferred_element_type=jnp.float32
    )
    grad_scores = soft * (grad_soft - jnp.sum(grad_soft * soft, -1, keepdims=True))
    grad_scores = (grad_scores + jnp.where(both_valid, cot_part.astype(jnp.float32), 0.0)).astype(
        jnp.bfloat16
    )
    grad_query = (
        jnp.einsum("mhqk,mkhd->mqhd", grad_scores, key_part, preferred_element_type=jnp.float32)
        * score_scale
    ).astype(jnp.bfloat16)
    grad_key = (
        jnp.einsum("mhqk,mqhd->mkhd", grad_scores, query_part, preferred_element_type=jnp.float32)
        * score_scale
    ).astype(jnp.bfloat16)
    grad_value = jnp.einsum(
        "mhqk,mqhd->mkhd",
        soft.astype(jnp.bfloat16),
        grad_masked,
        preferred_element_type=jnp.float32,
    ).astype(jnp.bfloat16)
    return (grad_scores, grad_query, grad_key, grad_value)


def body_native(
    atoms, pair, counts, qkv_weight, out_weight, ln1_gain, ln2_gain, w_in, w_out, out_cot, pair_cot
):
    mols_here, heads_here, length = (pair.shape[0], pair.shape[1], pair.shape[2])
    qkv_full, out_full = (
        lax.all_gather(qkv_weight, "batch", axis=1, tiled=True),
        lax.all_gather(out_weight, "batch", axis=0, tiled=True),
    )
    gain_one, gain_two, inner_weight, outer_weight = (
        lax.all_gather(ln1_gain.astype(jnp.bfloat16), ("batch", "head"), axis=0, tiled=True).astype(
            ln1_gain.dtype
        ),
        lax.all_gather(ln2_gain.astype(jnp.bfloat16), ("batch", "head"), axis=0, tiled=True).astype(
            ln2_gain.dtype
        ),
        lax.all_gather(w_in, ("batch", "head"), axis=0, tiled=True),
        lax.all_gather(w_out, ("batch", "head"), axis=0, tiled=True),
    )
    width_here = qkv_full.shape[2]
    head_size = width_here // heads_here
    score_scale = head_size ** (-0.5)
    blocks = mols_here // 2
    group_total = mols_here * length
    atoms_f = atoms.astype(jnp.float32)
    normed_one, inverse_one = layer_stats(atoms_f)
    hidden_one = (normed_one * gain_one).astype(jnp.bfloat16)
    group_rows = lax.all_gather(hidden_one, "head", axis=0, tiled=True)
    projected = jnp.einsum(
        "rd,sde->sre", group_rows, qkv_full, preferred_element_type=jnp.float32
    ).astype(jnp.bfloat16)

    def to_blocks(values):
        return values.reshape(blocks, 2, length, heads_here, head_size)

    query_all, key_all, value_all = (
        to_blocks(projected[0]),
        to_blocks(projected[1]),
        to_blocks(projected[2]),
    )
    pair_blocks = pair.reshape(blocks, 2, heads_here, length, length)
    count_blocks = counts.reshape(blocks, 2)
    new_pair, mixed, log_total = lax.map(
        partial(attend_forward, score_scale=score_scale),
        (query_all, key_all, value_all, pair_blocks, count_blocks),
    )
    mixed_flat = mixed.reshape(group_total, width_here)
    slab_rows = mixed_flat
    attention = lax.psum_scatter(
        times_transposed(slab_rows, out_full).astype(jnp.bfloat16),
        "head",
        scatter_dimension=0,
        tiled=True,
    ).astype(jnp.float32)
    first_sum = atoms_f + attention
    normed_two, inverse_two = layer_stats(first_sum)
    hidden_two = (normed_two * gain_two).astype(jnp.bfloat16)
    inner = jnp.dot(hidden_two, inner_weight, preferred_element_type=jnp.float32)
    gelu_value, gelu_pull = jax.vjp(jax.nn.gelu, inner)
    activated = gelu_value.astype(jnp.bfloat16)
    output = first_sum + jnp.dot(activated, outer_weight, preferred_element_type=jnp.float32)
    grad_outer_w = transposed_times(activated, out_cot)
    grad_act = times_transposed(out_cot, outer_weight)
    grad_inner = gelu_pull(grad_act)[0].astype(jnp.bfloat16)
    grad_inner_w = transposed_times(hidden_two, grad_inner)
    grad_hidden_two = times_transposed(grad_inner, inner_weight)
    grad_gain_two = jnp.sum(grad_hidden_two * normed_two, 0)
    grad_first = out_cot.astype(jnp.float32) + norm_back(
        grad_hidden_two * gain_two, normed_two, inverse_two
    )
    grad_attention = grad_first.astype(jnp.bfloat16)
    group_grad = lax.all_gather(grad_attention, "head", axis=0, tiled=True)
    grad_out_full = transposed_times(group_grad, mixed_flat)
    grad_mixed = jnp.dot(group_grad, out_full, preferred_element_type=jnp.float32).astype(
        jnp.bfloat16
    )
    cot_blocks = pair_cot.reshape(blocks, 2, heads_here, length, length)
    grad_scores, grad_query, grad_key, grad_value = lax.map(
        partial(attend_backward, score_scale=score_scale),
        (
            query_all,
            key_all,
            value_all,
            pair_blocks,
            count_blocks,
            to_blocks(grad_mixed),
            log_total,
            cot_blocks,
        ),
    )
    grad_projected = jnp.stack(
        [
            grad_query.reshape(group_total, width_here),
            grad_key.reshape(group_total, width_here),
            grad_value.reshape(group_total, width_here),
        ]
    )
    grad_qkv_full = jnp.einsum(
        "rd,sre->sde", group_rows, grad_projected, preferred_element_type=jnp.float32
    )
    slab_rows = grad_projected
    grad_hidden_one = lax.psum_scatter(
        jnp.einsum("sre,sde->rd", slab_rows, qkv_full, preferred_element_type=jnp.float32).astype(
            jnp.bfloat16
        ),
        "head",
        scatter_dimension=0,
        tiled=True,
    ).astype(jnp.float32)
    grad_gain_one = jnp.sum(grad_hidden_one * normed_one, 0)
    atoms_grad = grad_first + norm_back(grad_hidden_one * gain_one, normed_one, inverse_one)
    qkv_grad, out_grad = (
        lax.psum_scatter(
            grad_qkv_full.astype(jnp.bfloat16), "batch", scatter_dimension=1, tiled=True
        ).astype(jnp.float32),
        lax.psum_scatter(
            grad_out_full.astype(jnp.bfloat16), "batch", scatter_dimension=0, tiled=True
        ).astype(jnp.float32),
    )
    gain_one_grad, gain_two_grad, inner_grad, outer_grad = (
        lax.psum_scatter(grad_gain_one, ("batch", "head"), scatter_dimension=0, tiled=True),
        lax.psum_scatter(grad_gain_two, ("batch", "head"), scatter_dimension=0, tiled=True),
        lax.psum_scatter(grad_inner_w, ("batch", "head"), scatter_dimension=0, tiled=True),
        lax.psum_scatter(grad_outer_w, ("batch", "head"), scatter_dimension=0, tiled=True),
    )
    return (
        output.astype(jnp.bfloat16),
        new_pair.reshape(mols_here, heads_here, length, length),
        atoms_grad.astype(jnp.bfloat16),
        grad_scores.reshape(mols_here, heads_here, length, length),
        qkv_grad,
        out_grad,
        gain_one_grad,
        gain_two_grad,
        inner_grad,
        outer_grad,
    )


def dot(left, right):
    return jnp.dot(left, right, preferred_element_type=F32)


def dot_nt(left, right):
    return lax.dot_general(left, right, (((1,), (1,)), ((), ())), preferred_element_type=F32)


def dot_tn(left, right):
    return lax.dot_general(left, right, (((0,), (0,)), ((), ())), preferred_element_type=F32)


def swap(values, axes, count, bit):
    return lax.ppermute(values, axes, [(i, i ^ bit) for i in range(count)])


def relative(position, bits):
    return sum(((position >> k) & 1) * bit for k, bit in enumerate(bits))


def whole(shape):
    return pl.BlockSpec(shape, lambda *_: (0,) * len(shape))


def unpack_shards(info_ref, near_ref, far_ref, w_ref, gains_ref, rows_s, bits, shard):
    b, h = info_ref[0], info_ref[1]
    half = near_ref.shape[0]
    rows = w_ref.shape[1] // (2 * half)
    dim = gains_ref.shape[1]
    for p in range(2 * half):
        ref, q = (near_ref, p) if p < half else (far_ref, p - half)
        at = pl.multiple_of((b ^ relative(p, bits)) * rows, rows)
        for s in range(3):
            w_ref[s, pl.ds(at, rows), :] = ref[q, s * rows : (s + 1) * rows, :]
        rows_s[p : p + 1, :] = ref[q, 3 * rows : 3 * rows + 1, :].astype(F32)
    lanes = rows_s.shape[1]
    count = 2 * half
    lane = lax.broadcasted_iota(jnp.int32, (lanes, dim), 0)
    col = lax.broadcasted_iota(jnp.int32, (lanes, dim), 1)
    block = lax.broadcasted_iota(jnp.int32, (count, dim), 1) // rows
    place = lax.broadcasted_iota(jnp.int32, (count, dim), 0)
    owner = sum(((place >> k) & 1) * bit for k, bit in enumerate(bits)) ^ b
    values = rows_s[...].astype(BF16)
    for g in range(2):
        start = (((col // shard) & 1) ^ h) * (4 * shard) + g * 2 * shard + lax.rem(col, shard)
        pick = jnp.where((lane == start) | (lane == start + shard), 1.0, 0.0).astype(BF16)
        spread = dot(values, pick)
        gains_ref[g : g + 1, :] = jnp.sum(jnp.where(owner == block, spread, 0.0), 0, keepdims=True)


def attend_forward_kernel(
    info_ref, cnt_ref, atoms_ref, w_ref, gains_ref, pair_ref, *rest, hb, scale, carried, mol, bits, shard
):
    rest = rest[carried:]
    new_ref, exp_ref, mixed_ref, hid_t_ref, qkv_t_ref, inv_ref = rest[:6]
    if bits:
        near_ref, far_ref, (w_ref, gains_ref) = w_ref, gains_ref, rest[6:8]
        rest = (*rest[:6], *rest[8:-1], rest[-1])
        rows_s = rest[-1]
        rest = rest[:-1]
    q_s, kz_s, va_s, valid_s, sum_s = rest[6:]
    step = pl.program_id(0)
    length = atoms_ref.shape[0]
    heads = qkv_t_ref.shape[1]
    lanes = 8 * hb
    count = cnt_ref[mol(info_ref)]

    @pl.when(step == 0)
    def _():
        kz_s[...] = jnp.zeros_like(kz_s)
        if bits:
            unpack_shards(info_ref, near_ref, far_ref, w_ref, gains_ref, rows_s, bits, shard)

    @pl.when(step == 0)
    def _():
        values = atoms_ref[...].astype(F32)
        center = values - jnp.mean(values, -1, keepdims=True)
        inverse = lax.rsqrt(jnp.mean(center * center, -1, keepdims=True) + 1e-05)
        hidden = (center * inverse * gains_ref[0:1, :]).astype(BF16)
        hid_t_ref[...] = hidden.T
        query = (dot(hidden, w_ref[0]) * scale).astype(BF16)
        key = dot(hidden, w_ref[1]).astype(BF16)
        value = dot(hidden, w_ref[2]).astype(BF16)
        qkv_t_ref[0] = query.T.reshape(heads, 8, length)
        qkv_t_ref[1] = key.T.reshape(heads, 8, length)
        value_t = value.T.reshape(heads, 8, length)
        qkv_t_ref[2] = value_t
        va_s[:, :8, :] = value_t
        top = lax.broadcasted_iota(jnp.int32, (8, length), 0) == 0
        first = jnp.where(top, 1.0, 0.0).astype(BF16)
        va_s[:, 8:, :] = jnp.broadcast_to(first[None], (heads, 8, length))
        at = lax.broadcasted_iota(jnp.int32, (8, length), 1)
        bias = jnp.where(top & (at >= count), NEG, 0.0).astype(BF16)
        kz_s[:, lanes : lanes + 8, :] = jnp.broadcast_to(bias[None], (hb, 8, length))
        first_lane = jnp.where(lax.broadcasted_iota(jnp.int32, (length, lanes), 1) == 0, 1.0, 0.0).astype(BF16)
        for g in range(heads // hb):
            q_s[g, :, :lanes] = query[:, g * lanes : (g + 1) * lanes]
            q_s[g, :, lanes:] = first_lane
        valid = (lax.broadcasted_iota(jnp.int32, (length, length), 0) < count) & (
            lax.broadcasted_iota(jnp.int32, (length, length), 1) < count
        )
        valid_s[...] = jnp.where(valid, 1.0, 0.0).astype(BF16)

    for i in range(hb):
        kz_s[i, i * 8 : (i + 1) * 8, :] = qkv_t_ref[1, step * hb + i]
    for i in range(hb):
        logits = dot(q_s[step], kz_s[i]) + pair_ref[0, i].astype(F32)
        new_ref[0, i] = logits.astype(BF16) * valid_s[...]
        soft = jnp.exp(logits - jnp.max(logits, -1, keepdims=True)).astype(BF16)
        exp_ref[0, i] = soft
        sum_s[i] = dot_nt(va_s[step * hb + i], exp_ref[0, i])
    inverse = 1.0 / sum_s[:, 8:9, :]
    rows_ok = lax.broadcasted_iota(jnp.int32, (1, 1, length), 2) < count
    mixed = jnp.where(rows_ok, sum_s[:, :8, :] * inverse, 0.0)
    at = pl.ds(pl.multiple_of(step * lanes, lanes), lanes)
    mixed_ref[:, at] = mixed.reshape(lanes, length).T.astype(BF16)
    inv_ref[:, at] = jnp.broadcast_to(inverse, (hb, 8, length)).reshape(lanes, length).T


ANY = pl.BlockSpec(memory_space=pl.ANY)


def pair_spec_of(mol, hb, length):
    return pl.BlockSpec((1, hb, length, length), lambda j, info, cnt: (mol(info), j, 0, 0))


def rows_spec(length, cols, at=0):
    return pl.BlockSpec((length, cols), lambda *_: (at, 0))


def attend_forward_call(info, mol, counts, atoms, at, weights, pair, carried, theirs, bits=(), shard=0, hb=16):
    _, heads, length, _ = pair.shape
    dim = atoms.shape[1]
    width = 8 * heads
    lanes = 8 * hb
    pair_spec = pair_spec_of(mol, hb, length)
    place, blocks = theirs
    args = [atoms, *weights, pair, *carried]
    shape = jax.ShapeDtypeStruct
    outs = [
        (shape(pair.shape, BF16), pair_spec),
        (shape(pair.shape, BF16), pair_spec),
        (shape((blocks * length, width), BF16), rows_spec(length, width, place)),
        (shape((dim, length), BF16), whole((dim, length))),
        (shape((3, heads, 8, length), BF16), whole((3, heads, 8, length))),
        (shape((length, width), F32), whole((length, width))),
    ]
    scratch = [
        pltpu.VMEM((heads // hb, length, 2 * lanes), BF16),
        pltpu.VMEM((hb, 2 * lanes, length), BF16),
        pltpu.VMEM((heads, 16, length), BF16),
        pltpu.VMEM((length, length), BF16),
        pltpu.VMEM((hb, 16, length), F32),
    ]
    if bits:
        outs += [
            (shape((3, dim, width), BF16), whole((3, dim, width))),
            (shape((2, dim), F32), whole((2, dim))),
        ]
        scratch.append(pltpu.VMEM((2 ** len(bits), width), F32))
    spec = pltpu.PrefetchScalarGridSpec(
        num_scalar_prefetch=2,
        grid=(heads // hb,),
        in_specs=[rows_spec(length, dim, at), *[whole(x.shape) for x in weights], pair_spec]
        + [ANY] * len(carried),
        out_specs=[x[1] for x in outs],
        scratch_shapes=scratch,
    )
    return pl.pallas_call(
        partial(
            attend_forward_kernel,
            hb=hb,
            scale=8**-0.5,
            carried=len(carried),
            mol=mol,
            bits=bits,
            shard=shard,
        ),
        grid_spec=spec,
        out_shape=[x[0] for x in outs],
        input_output_aliases={6 + k: k for k in range(len(carried))},
        compiler_params=pltpu.CompilerParams(
            dimension_semantics=("arbitrary",), vmem_limit_bytes=VMEM_LIMIT
        ),
        cost_estimate=pl.CostEstimate(
            flops=heads * 4 * length**3,
            transcendentals=heads * length**2,
            bytes_accessed=6 * heads * length**2,
        ),
        name="attend_forward",
    )(info, counts, *args)


def attend_backward_kernel(
    info_ref, cnt_ref, gm_ref, mixed_ref, inv_ref, qkv_t_ref, w_ref, mask_ref, exp_ref, cot_ref, *rest,
    hb, scale, carried, mol
):
    pg_ref, gh_ref, gp_ref, l_s, r_s, gt_s, valid_s, gq_s, gk_s, gv_s = rest[carried:]
    step, steps = pl.program_id(0), pl.num_programs(0)
    length, width = gm_ref.shape
    heads = qkv_t_ref.shape[1]
    lanes = 8 * hb
    count = cnt_ref[mol(info_ref)]

    @pl.when(step == 0)
    def _():
        rows_ok = lax.broadcasted_iota(jnp.int32, (length, width), 0) < count
        scaled = jnp.where(rows_ok, gm_ref[...].astype(F32) * inv_ref[...], 0.0).astype(BF16)
        delta = (-(scaled.astype(F32) * mixed_ref[...].astype(F32))).astype(BF16)
        gt_s[...] = scaled.T.reshape(gt_s.shape)
        for g in range(heads // hb):
            part = slice(g * lanes, (g + 1) * lanes)
            l_s[g, :, :lanes] = scaled[:, part]
            l_s[g, :, lanes:] = delta[:, part]
            r_s[g, :lanes, :] = qkv_t_ref[2, g * hb : (g + 1) * hb].reshape(lanes, length)
            r_s[g, lanes:, :] = jnp.ones((lanes, length), BF16)
        valid = (lax.broadcasted_iota(jnp.int32, (length, length), 0) < count) & (
            lax.broadcasted_iota(jnp.int32, (length, length), 1) < count
        )
        valid_s[...] = jnp.where(valid, 1.0, 0.0).astype(BF16)

    for i in range(0, hb, 16):
        left = [l_s[step] * mask_ref[k : k + 1, :] for k in range(i, i + 16)]
        soft = dot(jnp.concatenate(left, 0), r_s[step])
        for k in range(16):
            part = soft[k * length : (k + 1) * length]
            cot = (cot_ref[0, i + k] * valid_s[...]).astype(F32)
            scores = (exp_ref[0, i + k].astype(F32) * part + cot).astype(BF16)
            pg_ref[0, i + k] = scores
            head = step * hb + i + k
            gq_s[head] = dot_nt(qkv_t_ref[1, head], pg_ref[0, i + k])
            gk_s[head] = dot(qkv_t_ref[0, head], pg_ref[0, i + k])
            gv_s[head] = dot(gt_s[head], exp_ref[0, i + k])

    @pl.when(step == steps - 1)
    def _():
        gp_ref[0] = (gq_s[...] * scale).reshape(width, length).astype(BF16).T
        gp_ref[1] = gk_s[...].reshape(width, length).astype(BF16).T
        gp_ref[2] = gv_s[...].reshape(width, length).astype(BF16).T
        gh_ref[...] = (
            dot_nt(gp_ref[0], w_ref[0]) + dot_nt(gp_ref[1], w_ref[1]) + dot_nt(gp_ref[2], w_ref[2])
        ).astype(BF16)


def attend_backward_call(info, mol, counts, gm, at, mixed, place, saved, weights, exps, cot, carried, theirs, hb=16):
    _, heads, length, _ = exps.shape
    dim, width = weights.shape[1], weights.shape[2]
    lanes = 8 * hb
    masks = jnp.asarray(np.tile(np.repeat(np.eye(hb, dtype=np.float32), 8, 1), 2), BF16)
    pair_spec = pair_spec_of(mol, hb, length)
    qkv_t, inverse = saved
    args = [gm, mixed, inverse, qkv_t, weights, masks, exps, cot, *carried]
    block, blocks = theirs
    spec = pltpu.PrefetchScalarGridSpec(
        num_scalar_prefetch=2,
        grid=(heads // hb,),
        in_specs=[
            rows_spec(length, width, at), rows_spec(length, width, place), whole(inverse.shape),
            whole(qkv_t.shape), whole(weights.shape), whole(masks.shape), pair_spec, pair_spec,
        ] + [ANY] * len(carried),
        out_specs=[pair_spec, rows_spec(length, dim, block), whole((3, length, width))],
        scratch_shapes=[
            pltpu.VMEM((heads // hb, length, 2 * lanes), BF16),
            pltpu.VMEM((heads // hb, 2 * lanes, length), BF16),
            pltpu.VMEM((heads, 8, length), BF16),
            pltpu.VMEM((length, length), BF16),
            pltpu.VMEM((heads, 8, length), F32),
            pltpu.VMEM((heads, 8, length), F32),
            pltpu.VMEM((heads, 8, length), F32),
        ],
    )
    shape = jax.ShapeDtypeStruct
    return pl.pallas_call(
        partial(attend_backward_kernel, hb=hb, scale=8**-0.5, carried=len(carried), mol=mol),
        grid_spec=spec,
        out_shape=[
            shape(exps.shape, BF16),
            shape((blocks * length, dim), BF16),
            shape((3, length, width), BF16),
        ],
        input_output_aliases={10 + k: k for k in range(len(carried))},
        compiler_params=pltpu.CompilerParams(
            dimension_semantics=("arbitrary",), vmem_limit_bytes=VMEM_LIMIT
        ),
        cost_estimate=pl.CostEstimate(
            flops=heads * 6 * length**3,
            transcendentals=0,
            bytes_accessed=6 * heads * length**2,
        ),
        name="attend_backward",
    )(info, counts, *args)


ROOT = (2 / np.pi) ** 0.5


def layer_kernel(
    info_ref, atoms_ref, mine0_ref, mine1_ref, other_ref, cot_ref, gains_ref, *rest, bits_a, bits_b
):
    a_refs, b_refs = rest[:4], rest[4:8]
    out_ref, first_ref, gm_mine_ref, gm_other_ref = rest[8:12]
    ga_refs, gb_refs = rest[12:16], rest[16:20]
    win_s, wout_s, ow_s, sum_s, acc_s, gh_s, normed_s, inv_s, hid_s, hid_t_s, mixed_s = rest[20:]
    me = 2 * info_ref[0] + info_ref[1]
    c, steps = pl.program_id(0), pl.num_programs(0)
    part = a_refs[0].shape[0]
    dim = atoms_ref.shape[1]
    length, width = mine0_ref.shape
    rows = dim // (4 * part)
    ff_rows = b_refs[0].shape[1]
    e_rows = dim // (2 * part)

    def shards(bits, refs):
        for p in range(4 * part):
            yield p, me ^ relative(p, bits), (refs[p // part], p % part)

    @pl.when(c == 0)
    def _():
        for p, owner, (ref, q) in shards(bits_a, a_refs):
            for k in range(4):
                win_s[k, pl.ds(pl.multiple_of(owner * rows, rows), rows), :] = ref[q, k * rows : (k + 1) * rows, :]
            at = pl.multiple_of((owner // 2) * e_rows, e_rows)
            for k in range(2):
                ow_s[relative(p, bits_a) & 1, pl.ds(at + k * rows, rows), :] = ref[q, 4 * rows :, k * width : (k + 1) * width]
        for p, owner, (ref, q) in shards(bits_b, b_refs):
            wout_s[pl.ds(pl.multiple_of(owner * ff_rows, ff_rows), ff_rows), :] = ref[q]
        mixed_s[:length] = mine0_ref[...]
        mixed_s[length:] = mine1_ref[...]
        first_sum = (
            atoms_ref[...].astype(F32) + dot_nt(mixed_s[...], ow_s[0]) + dot_nt(other_ref[...], ow_s[1])
        )
        sum_s[...] = first_sum
        center = first_sum - jnp.mean(first_sum, -1, keepdims=True)
        inverse = lax.rsqrt(jnp.mean(center * center, -1, keepdims=True) + 1e-05)
        normed = center * inverse
        normed_s[...] = normed
        inv_s[...] = inverse
        hidden = (normed * gains_ref[1:2, :]).astype(BF16)
        hid_s[...] = hidden
        hid_t_s[...] = hidden.T
        acc_s[...] = jnp.zeros_like(acc_s)
        gh_s[...] = jnp.zeros_like(gh_s)

    win = win_s[c]
    wout = wout_s[pl.ds(pl.multiple_of(c * dim, dim), dim), :]
    inner = dot(hid_s[...], win)
    square = inner * inner
    tanh = jnp.tanh(ROOT * inner * (1.0 + 0.044715 * square))
    activated = (0.5 * inner * (1.0 + tanh)).astype(BF16)
    slope = 0.5 * (1.0 + tanh) + (0.5 * ROOT) * inner * (1.0 - tanh * tanh) * (1.0 + (3 * 0.044715) * square)
    acc_s[...] += dot(activated, wout)
    grad_inner = (dot_nt(cot_ref[...], wout) * slope).astype(BF16)
    gh_s[...] += dot_nt(grad_inner, win)
    grad_in = dot(hid_t_s[...], grad_inner).astype(BF16)
    win_s[c] = grad_in
    grad_out = dot_tn(activated, cot_ref[...]).astype(BF16)
    wout_s[pl.ds(pl.multiple_of(c * dim, dim), dim), :] = grad_out

    @pl.when(c == steps - 1)
    def _():
        out_ref[...] = (sum_s[...] + acc_s[...]).astype(BF16)
        normed = normed_s[...]
        grad_norm = gh_s[...] * gains_ref[1:2, :]
        grad_first = cot_ref[...].astype(F32) + inv_s[...] * (
            grad_norm
            - jnp.mean(grad_norm, -1, keepdims=True)
            - normed * jnp.mean(grad_norm * normed, -1, keepdims=True)
        )
        first_ref[...] = grad_first
        grad_attention = grad_first.astype(BF16)
        gm_mine_ref[...] = dot(grad_attention, ow_s[0]).astype(BF16)
        gm_other_ref[...] = dot(grad_attention, ow_s[1]).astype(BF16)
        ow_s[0] = dot_tn(grad_attention, mixed_s[...]).astype(BF16)
        ow_s[1] = dot_tn(grad_attention, other_ref[...]).astype(BF16)
        for p, owner, (ref, q) in shards(bits_a, ga_refs):
            for k in range(4):
                ref[q, k * rows : (k + 1) * rows, :] = win_s[k, pl.ds(pl.multiple_of(owner * rows, rows), rows), :]
            at = pl.multiple_of((owner // 2) * e_rows, e_rows)
            for k in range(2):
                ref[q, 4 * rows :, k * width : (k + 1) * width] = ow_s[relative(p, bits_a) & 1, pl.ds(at + k * rows, rows), :]
        for p, owner, (ref, q) in shards(bits_b, gb_refs):
            ref[q] = wout_s[pl.ds(pl.multiple_of(owner * ff_rows, ff_rows), ff_rows), :]


def layer_call(info, atoms, mine, other, cot, gains, a_parts, b_parts, bits_a, bits_b):
    own, dim = atoms.shape
    width = other.shape[1]
    ff = 4 * b_parts[0].shape[0] * b_parts[0].shape[1]
    args = [atoms, *mine, other, cot, gains, *a_parts, *b_parts]
    shape = jax.ShapeDtypeStruct
    outs = [
        shape((own, dim), BF16),
        shape((own, dim), F32),
        shape((own, width), BF16),
        shape((own, width), BF16),
        *[shape(x.shape, BF16) for x in (*a_parts, *b_parts)],
    ]
    spec = pltpu.PrefetchScalarGridSpec(
        num_scalar_prefetch=1,
        grid=(ff // dim,),
        in_specs=[whole(x.shape) for x in args],
        out_specs=[whole(x.shape) for x in outs],
        scratch_shapes=[
            pltpu.VMEM((ff // dim, dim, dim), BF16),
            pltpu.VMEM((ff, dim), BF16),
            pltpu.VMEM((2, dim, width), BF16),
            pltpu.VMEM((own, dim), F32),
            pltpu.VMEM((own, dim), F32),
            pltpu.VMEM((own, dim), F32),
            pltpu.VMEM((own, dim), F32),
            pltpu.VMEM((own, 1), F32),
            pltpu.VMEM((own, dim), BF16),
            pltpu.VMEM((dim, own), BF16),
            pltpu.VMEM((own, width), BF16),
        ],
    )
    return pl.pallas_call(
        partial(layer_kernel, bits_a=bits_a, bits_b=bits_b),
        grid_spec=spec,
        out_shape=outs,
        compiler_params=pltpu.CompilerParams(
            dimension_semantics=("arbitrary",), vmem_limit_bytes=VMEM_LIMIT
        ),
        cost_estimate=pl.CostEstimate(
            flops=12 * own * dim * ff, transcendentals=own * ff, bytes_accessed=8 * dim * ff
        ),
        name="layer",
    )(info, *args)


def project_grad_kernel(me_ref, *refs, bits, parts):
    b = me_ref[0]
    near_ref, far_ref, full_s = refs[2 * parts :]
    half = near_ref.shape[0]
    rows = full_s.shape[1] // (2 * half)
    for s in range(3):
        full_s[s] = sum(dot(refs[k][...], refs[parts + k][s]) for k in range(parts)).astype(BF16)
    for p in range(2 * half):
        ref, q = (near_ref, p) if p < half else (far_ref, p - half)
        at = pl.multiple_of((b ^ relative(p, bits)) * rows, rows)
        for s in range(3):
            ref[q, s * rows : (s + 1) * rows, :] = full_s[s, pl.ds(at, rows), :]


def project_grad_call(me, hid_ts, gps, bits):
    dim, width = hid_ts[0].shape[0], gps[0].shape[2]
    half = 2 ** (len(bits) - 1)
    rows = dim // (2 * half)
    args = [*hid_ts, *gps]
    outs = [jax.ShapeDtypeStruct((half, 3 * rows, width), BF16)] * 2
    return pl.pallas_call(
        partial(project_grad_kernel, bits=bits, parts=len(hid_ts)),
        grid_spec=pltpu.PrefetchScalarGridSpec(
            num_scalar_prefetch=1,
            grid=(1,),
            in_specs=[whole(x.shape) for x in args],
            out_specs=[whole(x.shape) for x in outs],
            scratch_shapes=[pltpu.VMEM((3, dim, width), BF16)],
        ),
        out_shape=outs,
        compiler_params=pltpu.CompilerParams(vmem_limit_bytes=32 << 20),
        name="project_grad",
    )(me, *args)


def last_kernel(atoms_ref, gains_ref, first_ref, ga_ref, gb_ref, recv_ref, out_ref):
    values = atoms_ref[...].astype(F32)
    center = values - jnp.mean(values, -1, keepdims=True)
    inverse = lax.rsqrt(jnp.mean(center * center, -1, keepdims=True) + 1e-05)
    normed = center * inverse
    part = ga_ref.shape[0]
    grads = jnp.concatenate([ga_ref[...], gb_ref[...]], 0).astype(F32) + recv_ref[...].astype(F32)
    grad_norm = grads * gains_ref[0:1, :]
    out_ref[...] = (
        first_ref[...]
        + inverse
        * (
            grad_norm
            - jnp.mean(grad_norm, -1, keepdims=True)
            - normed * jnp.mean(grad_norm * normed, -1, keepdims=True)
        )
    ).astype(BF16)


def last_call(atoms, gains, first, gh_a, gh_b, recv):
    args = [atoms, gains, first, gh_a, gh_b, recv]
    return pl.pallas_call(
        last_kernel,
        grid=(1,),
        in_specs=[whole(x.shape) for x in args],
        out_specs=whole(atoms.shape),
        out_shape=jax.ShapeDtypeStruct(atoms.shape, BF16),
        compiler_params=pltpu.CompilerParams(vmem_limit_bytes=32 << 20),
        name="last_norm",
    )(*args)


def join(values, received):
    return jnp.concatenate([values, received], 0)


def add(kept, received):
    return (kept.astype(F32) + received.astype(F32)).astype(BF16)


def halves(values):
    half = values.shape[0] // 2
    return values[:half], values[half:]


def body_pairs(
    atoms, pair, counts, qkv_weight, out_weight, ln1_gain, ln2_gain, w_in, w_out, out_cot, pair_cot,
    batch
):
    info = jnp.stack([lax.axis_index("batch"), lax.axis_index("head")])
    h = info[1]
    own, dim = atoms.shape
    length = pair.shape[2]
    width = qkv_weight.shape[2]
    shard = ln1_gain.shape[0]
    top = batch.bit_length() - 1
    far_bits = [1 << k for k in range(top - 1, 1, -1)]
    batch_bits = (*far_bits, 2, 1)
    bits_a = [2 * bit for bit in far_bits] + [4, 1, 2]
    bits_b = [2 * bit for bit in far_bits] + [1, 4, 2]
    nz = len(far_bits)
    over_batch = lambda x, bit: swap(x, "batch", batch, bit)
    over_head = lambda x: swap(x, "head", 2, 1)
    over_both = lambda x, bit: swap(x, BOTH, 2 * batch, bit)
    tie = lax.optimization_barrier

    def split_gain(gain):
        high = gain.astype(BF16)
        return [high, (gain - high.astype(F32)).astype(BF16)]

    gain_row = jnp.concatenate(split_gain(ln1_gain) + split_gain(ln2_gain))[None]
    gain_row = jnp.concatenate([gain_row, over_head(gain_row)], 1)
    tail = jnp.pad(gain_row, ((0, 15), (0, width - gain_row.shape[1])))
    gathered = jnp.concatenate([qkv_weight.reshape(-1, width), tail], 0)[None]
    gathered, w_in_late, w_out_late, out_late = tie((gathered, w_in, w_out, out_weight))
    for bit in far_bits:
        gathered = join(gathered, over_batch(gathered, bit))
    e_rows = out_weight.shape[0]
    blocks = w_in.shape[1] // dim
    in_rows = [w_in_late[:, k * dim : (k + 1) * dim] for k in range(blocks)]
    out_rows = jnp.concatenate([out_late[: e_rows // 2], out_late[e_rows // 2 :]], 1)
    bulk = jnp.concatenate([*in_rows, out_rows, w_out_late], 0)[None]
    cut = bulk.shape[1] - w_out.shape[0]
    gathered, bulk = tie((gathered, bulk))
    atoms_other = over_head(atoms)
    gathered = join(gathered, over_batch(gathered, 2))
    far = over_batch(gathered, 1)

    per = own // length
    mine = lambda k: lambda info: info[1] * per + k
    theirs = lambda k: lambda info: (1 - info[1]) * per + k
    plan = [(mine(0), atoms, 0, (0, 1))]
    plan += [(theirs(k), atoms_other, k, (k, per)) for k in range(per)]
    plan += [(mine(k), atoms, k, (0, 1)) for k in range(1, per)]
    stage_bits = [(bit, bit) for bit in bits_a[:nz]] + list(zip(bits_a[nz:], bits_b[nz:]))
    last = len(stage_bits) - 1
    parts = (bulk,)

    def send_stage(parts, k):
        return tuple(over_both(x, bit) for x, bit in zip(parts, stage_bits[k]))

    received = send_stage(parts, 0)
    received, far = tie((received, far))
    cnt = counts
    carried = ()
    saved = []
    for k, (mol, rows, at, place) in enumerate(plan):
        if k < last - 1:
            parts = tuple(map(join, parts, received))
            if k + 1 == nz:
                parts = (parts[0][:, :cut], parts[0][:, cut:])
            cnt, parts = tie((cnt, parts))
            received = send_stage(parts, k + 1)
        else:
            cnt, received = tie((cnt, received))
            a_parts, b_parts = (
                [x, y, over_both(x, bit), over_both(y, bit)]
                for x, y, bit in zip(parts, received, stage_bits[last])
            )
        if k == 0:
            results = attend_forward_call(
                info, mol, cnt, rows, at, (gathered, far), pair, carried, place, batch_bits, shard
            )
            weights, gains = results[6:]
        else:
            results = attend_forward_call(
                info, mol, cnt, rows, at, (weights, gains), pair, carried, place
            )
        new_pair, exps, mixed, hid_t, qkv_t, inverse = results[:6]
        if k < last - 1:
            received, inverse = tie((received, inverse))
        carried = (new_pair, exps, mixed) if place[0] + 1 < place[1] else (new_pair, exps)
        saved.append((mixed, hid_t, (qkv_t, inverse)))
    mixed_theirs = saved[per][0]
    mixed_mine = [saved[0][0], *[s[0] for s in saved[1 + per :]]]
    mixed_other = over_head(mixed_theirs)

    output, first, gm_mine, gm_other, *pieces = layer_call(
        info, atoms, mixed_mine, mixed_other, out_cot, gains, a_parts, b_parts, bits_a, bits_b
    )
    gm_received = over_head(gm_other)

    def scatter_core(piece, bit):
        low, high, far_low, far_high = piece
        return add(low, over_both(far_low, bit)), add(high, over_both(far_high, bit))

    parts = [scatter_core(p, bit) for p, bit in zip((pieces[:4], pieces[4:]), stage_bits[last])]
    send_halves = lambda parts, k: [over_both(high, bit) for (_, high), bit in zip(parts, stage_bits[k])]
    add_halves = lambda parts, received: [add(low, r) for (low, _), r in zip(parts, received)]
    carried = ()
    grads = []
    cnt = counts
    stage = last - 1
    for k, (mol, _, at, place) in enumerate(plan):
        if k == 1:
            cnt, parts = tie((cnt, parts))
            received = send_halves(parts, stage)
        elif k == len(plan) - 1:
            cnt, sums = tie((cnt, add_halves(parts, received)))
            parts = [halves(x) for x in sums]
            stage -= 1
            received = send_halves(parts, stage)
        mixed = mixed_theirs if place[1] > 1 else saved[k][0]
        gm = gm_received if place[1] > 1 else gm_mine
        pair_grad, gh, gp = attend_backward_call(
            info, mol, cnt, gm, at, mixed, place[0], saved[k][2], weights, exps, pair_cot, carried, place
        )
        carried = (pair_grad, gh) if place[0] + 1 < place[1] else (pair_grad,)
        grads.append((gh, gp))
    hidden_received = over_head(grads[per][0])
    gps, received = tie(([g[1] for g in grads], received))
    near, far = project_grad_call(info, [s[1] for s in saved], gps, batch_bits)
    near = add(near, over_batch(far, batch_bits[-1]))
    near, received = tie((near, received))
    bulk = jnp.concatenate(add_halves(parts, received), 1)
    for bit in batch_bits[-2::-1]:
        keep, send = halves(near)
        near = add(keep, over_batch(send, bit))
        if stage > 0:
            stage -= 1
            keep, send = halves(bulk)
            bulk = add(keep, over_both(send, bits_a[stage]))
    qkv_grad = near[0].reshape(qkv_weight.shape).astype(F32)
    gain_part = jnp.sum(qkv_grad * qkv_weight.astype(F32), (0, 2)).reshape(2, shard)
    gain_mine = lax.dynamic_index_in_dim(gain_part, h, 0, False)
    gain_other = over_head(lax.dynamic_index_in_dim(gain_part, 1 - h, 0, False))
    gain_one_grad = (gain_mine + gain_other) / ln1_gain
    atoms_grad = last_call(atoms, gains, first, grads[0][0], grads[-1][0], hidden_received)
    bulk = bulk[0].astype(F32)
    shard_rows = w_in.shape[0]
    in_grad = jnp.concatenate([bulk[k * shard_rows : (k + 1) * shard_rows] for k in range(blocks)], 1)
    out_grad = jnp.concatenate([bulk[blocks * shard_rows : cut, k * width : (k + 1) * width] for k in range(2)], 0)
    outer_grad = bulk[cut:]
    gain_two_grad = jnp.sum(in_grad * w_in.astype(F32), 1) / ln2_gain
    return (
        output, new_pair, atoms_grad, pair_grad, qkv_grad, out_grad,
        gain_one_grad, gain_two_grad, in_grad, outer_grad,
    )


def solution(mesh):
    rows = P(BOTH, None)
    heads = P("batch", "head", None, None)
    batch, head = mesh.shape["batch"], mesh.shape["head"]
    body = partial(body_pairs, batch=batch) if (batch, head) == (16, 2) else body_native
    return jax.shard_map(
        body,
        mesh=mesh,
        in_specs=(
            rows, heads, P("batch"), P(None, "batch", "head"), P("batch", "head"),
            P(BOTH), P(BOTH), rows, rows, rows, heads,
        ),
        out_specs=(
            rows, heads, rows, heads, P(None, "batch", "head"), P("batch", "head"),
            P(BOTH), P(BOTH), rows, rows,
        ),
        check_vma=False,
    )
```

```python
from functools import partial

import jax
import jax.numpy as jnp
import numpy as np
from jax import lax
from jax.experimental import pallas as pl
from jax.experimental.pallas import tpu as pltpu
from jax.sharding import PartitionSpec as P

F32 = jnp.float32
BF16 = jnp.bfloat16
NEG = -1e30
VMEM_LIMIT = 48 << 20
BOTH = ("batch", "head")


def layer_stats(values):
    center = values - jnp.mean(values, -1, keepdims=True)
    inverse = lax.rsqrt(jnp.mean(center * center, -1, keepdims=True) + 1e-05)
    return (center * inverse, inverse)


def norm_back(grad_norm, normed, inverse):
    return inverse * (
        grad_norm
        - jnp.mean(grad_norm, -1, keepdims=True)
        - normed * jnp.mean(grad_norm * normed, -1, keepdims=True)
    )


def times_transposed(left, right):
    return lax.dot_general(
        left, right, (((1,), (1,)), ((), ())), preferred_element_type=jnp.float32
    )


def transposed_times(left, right):
    return lax.dot_general(
        left, right, (((0,), (0,)), ((), ())), preferred_element_type=jnp.float32
    )


def block_masks(count_part, length):
    positions = jnp.arange(length, dtype=jnp.int32)
    valid_rows = positions[None, :] < count_part[:, None]
    both_valid = valid_rows[:, None, :, None] & valid_rows[:, None, None, :]
    return (valid_rows, both_valid)


def scores_of(query_part, key_part, pair_part, score_scale):
    raw = jnp.einsum("mqhd,mkhd->mhqk", query_part, key_part, preferred_element_type=jnp.float32)
    return raw * score_scale + pair_part.astype(jnp.float32)


def attend_forward(inputs, score_scale):
    query_part, key_part, value_part, pair_part, count_part = inputs
    valid_rows, both_valid = block_masks(count_part, query_part.shape[1])
    logits = scores_of(query_part, key_part, pair_part, score_scale)
    new_pair = jnp.where(both_valid, logits, 0.0).astype(jnp.bfloat16)
    masked = jnp.where(valid_rows[:, None, None, :], logits, -1e30)
    row_max = jnp.max(masked, -1, keepdims=True)
    exponent = jnp.exp(masked - row_max)
    row_total = jnp.sum(exponent, -1, keepdims=True)
    soft_weights = (exponent / row_total).astype(jnp.bfloat16)
    mixed = jnp.einsum(
        "mhqk,mkhd->mqhd", soft_weights, value_part, preferred_element_type=jnp.float32
    )
    mixed = jnp.where(valid_rows[:, :, None, None], mixed, 0.0).astype(jnp.bfloat16)
    return (new_pair, mixed, row_max[..., 0] + jnp.log(row_total[..., 0]))


def attend_backward(inputs, score_scale):
    query_part, key_part, value_part, pair_part, count_part, grad_mixed, log_total, cot_part = (
        inputs
    )
    valid_rows, both_valid = block_masks(count_part, query_part.shape[1])
    logits = scores_of(query_part, key_part, pair_part, score_scale)
    masked = jnp.where(valid_rows[:, None, None, :], logits, -1e30)
    soft = jnp.exp(masked - log_total[..., None])
    grad_masked = jnp.where(valid_rows[:, :, None, None], grad_mixed, jnp.zeros_like(grad_mixed))
    grad_soft = jnp.einsum(
        "mqhd,mkhd->mhqk", grad_masked, value_part, preferred_element_type=jnp.float32
    )
    grad_scores = soft * (grad_soft - jnp.sum(grad_soft * soft, -1, keepdims=True))
    grad_scores = (grad_scores + jnp.where(both_valid, cot_part.astype(jnp.float32), 0.0)).astype(
        jnp.bfloat16
    )
    grad_query = (
        jnp.einsum("mhqk,mkhd->mqhd", grad_scores, key_part, preferred_element_type=jnp.float32)
        * score_scale
    ).astype(jnp.bfloat16)
    grad_key = (
        jnp.einsum("mhqk,mqhd->mkhd", grad_scores, query_part, preferred_element_type=jnp.float32)
        * score_scale
    ).astype(jnp.bfloat16)
    grad_value = jnp.einsum(
        "mhqk,mqhd->mkhd",
        soft.astype(jnp.bfloat16),
        grad_masked,
        preferred_element_type=jnp.float32,
    ).astype(jnp.bfloat16)
    return (grad_scores, grad_query, grad_key, grad_value)


def body_native(
    atoms, pair, counts, qkv_weight, out_weight, ln1_gain, ln2_gain, w_in, w_out, out_cot, pair_cot
):
    mols_here, heads_here, length = (pair.shape[0], pair.shape[1], pair.shape[2])
    qkv_full, out_full = (
        lax.all_gather(qkv_weight, "batch", axis=1, tiled=True),
        lax.all_gather(out_weight, "batch", axis=0, tiled=True),
    )
    gain_one, gain_two, inner_weight, outer_weight = (
        lax.all_gather(ln1_gain.astype(jnp.bfloat16), ("batch", "head"), axis=0, tiled=True).astype(
            ln1_gain.dtype
        ),
        lax.all_gather(ln2_gain.astype(jnp.bfloat16), ("batch", "head"), axis=0, tiled=True).astype(
            ln2_gain.dtype
        ),
        lax.all_gather(w_in, ("batch", "head"), axis=0, tiled=True),
        lax.all_gather(w_out, ("batch", "head"), axis=0, tiled=True),
    )
    width_here = qkv_full.shape[2]
    head_size = width_here // heads_here
    score_scale = head_size ** (-0.5)
    blocks = mols_here // 2
    group_total = mols_here * length
    atoms_f = atoms.astype(jnp.float32)
    normed_one, inverse_one = layer_stats(atoms_f)
    hidden_one = (normed_one * gain_one).astype(jnp.bfloat16)
    group_rows = lax.all_gather(hidden_one, "head", axis=0, tiled=True)
    projected = jnp.einsum(
        "rd,sde->sre", group_rows, qkv_full, preferred_element_type=jnp.float32
    ).astype(jnp.bfloat16)

    def to_blocks(values):
        return values.reshape(blocks, 2, length, heads_here, head_size)

    query_all, key_all, value_all = (
        to_blocks(projected[0]),
        to_blocks(projected[1]),
        to_blocks(projected[2]),
    )
    pair_blocks = pair.reshape(blocks, 2, heads_here, length, length)
    count_blocks = counts.reshape(blocks, 2)
    new_pair, mixed, log_total = lax.map(
        partial(attend_forward, score_scale=score_scale),
        (query_all, key_all, value_all, pair_blocks, count_blocks),
    )
    mixed_flat = mixed.reshape(group_total, width_here)
    slab_rows = mixed_flat
    attention = lax.psum_scatter(
        times_transposed(slab_rows, out_full).astype(jnp.bfloat16),
        "head",
        scatter_dimension=0,
        tiled=True,
    ).astype(jnp.float32)
    first_sum = atoms_f + attention
    normed_two, inverse_two = layer_stats(first_sum)
    hidden_two = (normed_two * gain_two).astype(jnp.bfloat16)
    inner = jnp.dot(hidden_two, inner_weight, preferred_element_type=jnp.float32)
    gelu_value, gelu_pull = jax.vjp(jax.nn.gelu, inner)
    activated = gelu_value.astype(jnp.bfloat16)
    output = first_sum + jnp.dot(activated, outer_weight, preferred_element_type=jnp.float32)
    grad_outer_w = transposed_times(activated, out_cot)
    grad_act = times_transposed(out_cot, outer_weight)
    grad_inner = gelu_pull(grad_act)[0].astype(jnp.bfloat16)
    grad_inner_w = transposed_times(hidden_two, grad_inner)
    grad_hidden_two = times_transposed(grad_inner, inner_weight)
    grad_gain_two = jnp.sum(grad_hidden_two * normed_two, 0)
    grad_first = out_cot.astype(jnp.float32) + norm_back(
        grad_hidden_two * gain_two, normed_two, inverse_two
    )
    grad_attention = grad_first.astype(jnp.bfloat16)
    group_grad = lax.all_gather(grad_attention, "head", axis=0, tiled=True)
    grad_out_full = transposed_times(group_grad, mixed_flat)
    grad_mixed = jnp.dot(group_grad, out_full, preferred_element_type=jnp.float32).astype(
        jnp.bfloat16
    )
    cot_blocks = pair_cot.reshape(blocks, 2, heads_here, length, length)
    grad_scores, grad_query, grad_key, grad_value = lax.map(
        partial(attend_backward, score_scale=score_scale),
        (
            query_all,
            key_all,
            value_all,
            pair_blocks,
            count_blocks,
            to_blocks(grad_mixed),
            log_total,
            cot_blocks,
        ),
    )
    grad_projected = jnp.stack(
        [
            grad_query.reshape(group_total, width_here),
            grad_key.reshape(group_total, width_here),
            grad_value.reshape(group_total, width_here),
        ]
    )
    grad_qkv_full = jnp.einsum(
        "rd,sre->sde", group_rows, grad_projected, preferred_element_type=jnp.float32
    )
    slab_rows = grad_projected
    grad_hidden_one = lax.psum_scatter(
        jnp.einsum("sre,sde->rd", slab_rows, qkv_full, preferred_element_type=jnp.float32).astype(
            jnp.bfloat16
        ),
        "head",
        scatter_dimension=0,
        tiled=True,
    ).astype(jnp.float32)
    grad_gain_one = jnp.sum(grad_hidden_one * normed_one, 0)
    atoms_grad = grad_first + norm_back(grad_hidden_one * gain_one, normed_one, inverse_one)
    qkv_grad, out_grad = (
        lax.psum_scatter(
            grad_qkv_full.astype(jnp.bfloat16), "batch", scatter_dimension=1, tiled=True
        ).astype(jnp.float32),
        lax.psum_scatter(
            grad_out_full.astype(jnp.bfloat16), "batch", scatter_dimension=0, tiled=True
        ).astype(jnp.float32),
    )
    gain_one_grad, gain_two_grad, inner_grad, outer_grad = (
        lax.psum_scatter(grad_gain_one, ("batch", "head"), scatter_dimension=0, tiled=True),
        lax.psum_scatter(grad_gain_two, ("batch", "head"), scatter_dimension=0, tiled=True),
        lax.psum_scatter(grad_inner_w, ("batch", "head"), scatter_dimension=0, tiled=True),
        lax.psum_scatter(grad_outer_w, ("batch", "head"), scatter_dimension=0, tiled=True),
    )
    return (
        output.astype(jnp.bfloat16),
        new_pair.reshape(mols_here, heads_here, length, length),
        atoms_grad.astype(jnp.bfloat16),
        grad_scores.reshape(mols_here, heads_here, length, length),
        qkv_grad,
        out_grad,
        gain_one_grad,
        gain_two_grad,
        inner_grad,
        outer_grad,
    )


def dot(left, right):
    return jnp.dot(left, right, preferred_element_type=F32)


def dot_nt(left, right):
    return lax.dot_general(left, right, (((1,), (1,)), ((), ())), preferred_element_type=F32)


def dot_tn(left, right):
    return lax.dot_general(left, right, (((0,), (0,)), ((), ())), preferred_element_type=F32)


def swap(values, axes, count, bit):
    return lax.ppermute(values, axes, [(i, i ^ bit) for i in range(count)])


def relative(position, bits):
    return sum(((position >> k) & 1) * bit for k, bit in enumerate(bits))


def whole(shape):
    return pl.BlockSpec(shape, lambda *_: (0,) * len(shape))


def unpack_shards(info_ref, near_ref, far_ref, other_ref, w_ref, gains_ref, rows_s, bits, shard):
    b, h = info_ref[0], info_ref[1]
    half = near_ref.shape[0]
    rows = w_ref.shape[1] // (2 * half)
    dim = gains_ref.shape[1]
    for p in range(2 * half):
        ref, q = (near_ref, p) if p < half else (far_ref, p - half)
        at = pl.multiple_of((b ^ relative(p, bits)) * rows, rows)
        for s in range(3):
            w_ref[s, pl.ds(at, rows), :] = ref[q, s * rows : (s + 1) * rows, :]
        rows_s[0, p : p + 1, :] = ref[q, 3 * rows : 3 * rows + 1, :].astype(F32)
        rows_s[1, p : p + 1, :] = other_ref[p, 0:1, :].astype(F32)
    lanes = rows_s.shape[2]
    count = 2 * half
    lane = lax.broadcasted_iota(jnp.int32, (lanes, dim), 0)
    col = lax.broadcasted_iota(jnp.int32, (lanes, dim), 1)
    block = lax.broadcasted_iota(jnp.int32, (count, dim), 1) // rows
    side = (lax.broadcasted_iota(jnp.int32, (count, dim), 1) // shard) & 1
    place = lax.broadcasted_iota(jnp.int32, (count, dim), 0)
    owner = sum(((place >> k) & 1) * bit for k, bit in enumerate(bits)) ^ b
    values = rows_s[...].astype(BF16)
    for g in range(2):
        start = g * 2 * shard + lax.rem(col, shard)
        pick = jnp.where((lane == start) | (lane == start + shard), 1.0, 0.0).astype(BF16)
        spread = jnp.where(side == h, dot(values[0], pick), dot(values[1], pick))
        gains_ref[g : g + 1, :] = jnp.sum(jnp.where(owner == block, spread, 0.0), 0, keepdims=True)


def pack_kernel(in_ref, proj_ref, out_ref, bulk_ref):
    rows, dim = in_ref.shape[0], bulk_ref.shape[1]
    blocks = in_ref.shape[1] // dim
    half, width = proj_ref.shape[0] // 2, proj_ref.shape[1]
    for k in range(blocks):
        bulk_ref[k * rows : (k + 1) * rows, :] = in_ref[:, k * dim : (k + 1) * dim]
    at = blocks * rows
    for k in range(2):
        bulk_ref[at : at + half, k * width : (k + 1) * width] = proj_ref[k * half : (k + 1) * half, :]
    bulk_ref[at + half :, :] = out_ref[...]


def pack_call(w_in, out_weight, w_out):
    args = [w_in, out_weight, w_out]
    dim = w_out.shape[1]
    out = jax.ShapeDtypeStruct((sum(x.size for x in args) // dim, dim), BF16)
    return pl.pallas_call(
        pack_kernel,
        grid=(1,),
        in_specs=[whole(x.shape) for x in args],
        out_specs=whole(out.shape),
        out_shape=out,
        name="pack",
    )(*args)


def attend_forward_kernel(
    info_ref, cnt_ref, atoms_ref, w_ref, gains_ref, pair_ref, *rest, hb, scale, carried, mol, bits, shard
):
    rest0, rest = rest, rest[carried + bool(bits) :]
    new_ref, exp_ref, mixed_ref, hid_t_ref, qkv_t_ref, inv_ref = rest[:6]
    if bits:
        near_ref, far_ref, other_ref, pair_ref = w_ref, gains_ref, pair_ref, rest0[0]
        w_ref, gains_ref = rest[6:8]
        rest = (*rest[:6], *rest[8:-1], rest[-1])
        rows_s = rest[-1]
        rest = rest[:-1]
    q_s, kz_s, va_s, valid_s, sum_s = rest[6:]
    mol_at, step = pl.program_id(0), pl.program_id(1)
    length = atoms_ref.shape[0]
    heads = qkv_t_ref.shape[1]
    lanes = 8 * hb
    count = cnt_ref[mol(info_ref) + mol_at]

    @pl.when((step == 0) & (mol_at == 0))
    def _():
        kz_s[...] = jnp.zeros_like(kz_s)
        if bits:
            unpack_shards(info_ref, near_ref, far_ref, other_ref, w_ref, gains_ref, rows_s, bits, shard)

    @pl.when(step == 0)
    def _():
        values = atoms_ref[...].astype(F32)
        center = values - jnp.mean(values, -1, keepdims=True)
        inverse = lax.rsqrt(jnp.mean(center * center, -1, keepdims=True) + 1e-05)
        hidden = (center * inverse * gains_ref[0:1, :]).astype(BF16)
        hid_t_ref[...] = hidden.T
        query = (dot(hidden, w_ref[0]) * scale).astype(BF16)
        key = dot(hidden, w_ref[1]).astype(BF16)
        value = dot(hidden, w_ref[2]).astype(BF16)
        qkv_t_ref[0] = query.T.reshape(heads, 8, length)
        qkv_t_ref[1] = key.T.reshape(heads, 8, length)
        value_t = value.T.reshape(heads, 8, length)
        qkv_t_ref[2] = value_t
        va_s[:, :8, :] = value_t
        top = lax.broadcasted_iota(jnp.int32, (8, length), 0) == 0
        first = jnp.where(top, 1.0, 0.0).astype(BF16)
        va_s[:, 8:, :] = jnp.broadcast_to(first[None], (heads, 8, length))
        at = lax.broadcasted_iota(jnp.int32, (8, length), 1)
        bias = jnp.where(top & (at >= count), NEG, 0.0).astype(BF16)
        kz_s[:, lanes : lanes + 8, :] = jnp.broadcast_to(bias[None], (hb, 8, length))
        first_lane = jnp.where(lax.broadcasted_iota(jnp.int32, (length, lanes), 1) == 0, 1.0, 0.0).astype(BF16)
        for g in range(heads // hb):
            q_s[g, :, :lanes] = query[:, g * lanes : (g + 1) * lanes]
            q_s[g, :, lanes:] = first_lane
        valid = (lax.broadcasted_iota(jnp.int32, (length, length), 0) < count) & (
            lax.broadcasted_iota(jnp.int32, (length, length), 1) < count
        )
        valid_s[...] = jnp.where(valid, 1.0, 0.0).astype(BF16)

    for i in range(hb):
        kz_s[i, i * 8 : (i + 1) * 8, :] = qkv_t_ref[1, step * hb + i]
    for i in range(hb):
        logits = dot(q_s[step], kz_s[i]) + pair_ref[0, i].astype(F32)
        new_ref[0, i] = logits.astype(BF16) * valid_s[...]
        soft = jnp.exp(logits - jnp.max(logits, -1, keepdims=True)).astype(BF16)
        exp_ref[0, i] = soft
        sum_s[i] = dot_nt(va_s[step * hb + i], exp_ref[0, i])
    inverse = 1.0 / sum_s[:, 8:9, :]
    rows_ok = lax.broadcasted_iota(jnp.int32, (1, 1, length), 2) < count
    mixed = jnp.where(rows_ok, sum_s[:, :8, :] * inverse, 0.0)
    at = pl.ds(pl.multiple_of(step * lanes, lanes), lanes)
    mixed_ref[:, at] = mixed.reshape(lanes, length).T.astype(BF16)
    inv_ref[:, at] = jnp.broadcast_to(inverse, (hb, 8, length)).reshape(lanes, length).T


ANY = pl.BlockSpec(memory_space=pl.ANY)


def pair_spec_of(mol, hb, length):
    return pl.BlockSpec((1, hb, length, length), lambda i, j, info, cnt: (mol(info) + i, j, 0, 0))


def rows_spec(length, cols, at=0):
    return pl.BlockSpec((length, cols), lambda i, *_: (at + i, 0))


def attend_forward_call(info, mol, n, counts, atoms, at, weights, pair, carried, bits=(), shard=0, hb=16):
    _, heads, length, _ = pair.shape
    dim = atoms.shape[1]
    width = 8 * heads
    lanes = 8 * hb
    pair_spec = pair_spec_of(mol, hb, length)
    args = [atoms, *weights, pair, *carried]
    shape = jax.ShapeDtypeStruct
    outs = [
        (shape(pair.shape, BF16), pair_spec),
        (shape(pair.shape, BF16), pair_spec),
        (shape((n * length, width), BF16), rows_spec(length, width)),
        (shape((dim, n * length), BF16), pl.BlockSpec((dim, length), lambda i, *_: (0, i))),
        (
            shape((3 * n, heads, 8, length), BF16),
            pl.BlockSpec((3, heads, 8, length), lambda i, *_: (i, 0, 0, 0)),
        ),
        (shape((n * length, width), F32), rows_spec(length, width)),
    ]
    scratch = [
        pltpu.VMEM((heads // hb, length, 2 * lanes), BF16),
        pltpu.VMEM((hb, 2 * lanes, length), BF16),
        pltpu.VMEM((heads, 16, length), BF16),
        pltpu.VMEM((length, length), BF16),
        pltpu.VMEM((hb, 16, length), F32),
    ]
    if bits:
        outs += [
            (shape((3, dim, width), BF16), whole((3, dim, width))),
            (shape((2, dim), F32), whole((2, dim))),
        ]
        scratch.append(pltpu.VMEM((2, 2 ** len(bits), width), F32))
    spec = pltpu.PrefetchScalarGridSpec(
        num_scalar_prefetch=2,
        grid=(n, heads // hb),
        in_specs=[rows_spec(length, dim, at), *[whole(x.shape) for x in weights], pair_spec]
        + [ANY] * len(carried),
        out_specs=[x[1] for x in outs],
        scratch_shapes=scratch,
    )
    return pl.pallas_call(
        partial(
            attend_forward_kernel,
            hb=hb,
            scale=8**-0.5,
            carried=len(carried),
            mol=mol,
            bits=bits,
            shard=shard,
        ),
        grid_spec=spec,
        out_shape=[x[0] for x in outs],
        input_output_aliases={4 + len(weights) + k: k for k in range(len(carried))},
        compiler_params=pltpu.CompilerParams(
            dimension_semantics=("arbitrary", "arbitrary"), vmem_limit_bytes=VMEM_LIMIT
        ),
        cost_estimate=pl.CostEstimate(
            flops=n * heads * 4 * length**3,
            transcendentals=n * heads * length**2,
            bytes_accessed=6 * n * heads * length**2,
        ),
        name="attend_forward",
    )(info, counts, *args)


def attend_backward_kernel(
    info_ref, cnt_ref, gm_ref, mixed_ref, inv_ref, qkv_t_ref, w_ref, mask_ref, exp_ref, cot_ref, *rest,
    hb, scale, carried, mol
):
    pg_ref, gh_ref, gp_ref, l_s, r_s, gt_s, valid_s, gq_s, gk_s, gv_s = rest[carried:]
    mol_at = pl.program_id(0)
    step, steps = pl.program_id(1), pl.num_programs(1)
    length, width = gm_ref.shape
    heads = qkv_t_ref.shape[1]
    lanes = 8 * hb
    count = cnt_ref[mol(info_ref) + mol_at]

    @pl.when(step == 0)
    def _():
        rows_ok = lax.broadcasted_iota(jnp.int32, (length, width), 0) < count
        scaled = jnp.where(rows_ok, gm_ref[...].astype(F32) * inv_ref[...], 0.0).astype(BF16)
        delta = (-(scaled.astype(F32) * mixed_ref[...].astype(F32))).astype(BF16)
        gt_s[...] = scaled.T.reshape(gt_s.shape)
        for g in range(heads // hb):
            part = slice(g * lanes, (g + 1) * lanes)
            l_s[g, :, :lanes] = scaled[:, part]
            l_s[g, :, lanes:] = delta[:, part]
            r_s[g, :lanes, :] = qkv_t_ref[2, g * hb : (g + 1) * hb].reshape(lanes, length)
            r_s[g, lanes:, :] = jnp.ones((lanes, length), BF16)
        valid = (lax.broadcasted_iota(jnp.int32, (length, length), 0) < count) & (
            lax.broadcasted_iota(jnp.int32, (length, length), 1) < count
        )
        valid_s[...] = jnp.where(valid, 1.0, 0.0).astype(BF16)

    for i in range(0, hb, 16):
        left = [l_s[step] * mask_ref[k : k + 1, :] for k in range(i, i + 16)]
        soft = dot(jnp.concatenate(left, 0), r_s[step])
        for k in range(16):
            part = soft[k * length : (k + 1) * length]
            cot = (cot_ref[0, i + k] * valid_s[...]).astype(F32)
            scores = (exp_ref[0, i + k].astype(F32) * part + cot).astype(BF16)
            pg_ref[0, i + k] = scores
            head = step * hb + i + k
            gq_s[head] = dot_nt(qkv_t_ref[1, head], pg_ref[0, i + k])
            gk_s[head] = dot(qkv_t_ref[0, head], pg_ref[0, i + k])
            gv_s[head] = dot(gt_s[head], exp_ref[0, i + k])

    @pl.when(step == steps - 1)
    def _():
        gp_ref[0] = (gq_s[...] * scale).reshape(width, length).astype(BF16).T
        gp_ref[1] = gk_s[...].reshape(width, length).astype(BF16).T
        gp_ref[2] = gv_s[...].reshape(width, length).astype(BF16).T
        gh_ref[...] = (
            dot_nt(gp_ref[0], w_ref[0]) + dot_nt(gp_ref[1], w_ref[1]) + dot_nt(gp_ref[2], w_ref[2])
        ).astype(BF16)


def attend_backward_call(info, mol, n, counts, gm, at, saved, weights, exps, cot, carried, hb=16):
    _, heads, length, _ = exps.shape
    dim, width = weights.shape[1], weights.shape[2]
    lanes = 8 * hb
    masks = jnp.asarray(np.tile(np.repeat(np.eye(hb, dtype=np.float32), 8, 1), 2), BF16)
    pair_spec = pair_spec_of(mol, hb, length)
    mixed, _, qkv_t, inverse = saved
    args = [gm, mixed, inverse, qkv_t, weights, masks, exps, cot, *carried]
    spec = pltpu.PrefetchScalarGridSpec(
        num_scalar_prefetch=2,
        grid=(n, heads // hb),
        in_specs=[
            rows_spec(length, width, at), rows_spec(length, width), rows_spec(length, width),
            pl.BlockSpec((3, heads, 8, length), lambda i, *_: (i, 0, 0, 0)),
            whole(weights.shape), whole(masks.shape), pair_spec, pair_spec,
        ] + [ANY] * len(carried),
        out_specs=[
            pair_spec,
            rows_spec(length, dim),
            pl.BlockSpec((3, length, width), lambda i, *_: (0, i, 0)),
        ],
        scratch_shapes=[
            pltpu.VMEM((heads // hb, length, 2 * lanes), BF16),
            pltpu.VMEM((heads // hb, 2 * lanes, length), BF16),
            pltpu.VMEM((heads, 8, length), BF16),
            pltpu.VMEM((length, length), BF16),
            pltpu.VMEM((heads, 8, length), F32),
            pltpu.VMEM((heads, 8, length), F32),
            pltpu.VMEM((heads, 8, length), F32),
        ],
    )
    shape = jax.ShapeDtypeStruct
    return pl.pallas_call(
        partial(attend_backward_kernel, hb=hb, scale=8**-0.5, carried=len(carried), mol=mol),
        grid_spec=spec,
        out_shape=[
            shape(exps.shape, BF16),
            shape((n * length, dim), BF16),
            shape((3, n * length, width), BF16),
        ],
        input_output_aliases={10 + k: k for k in range(len(carried))},
        compiler_params=pltpu.CompilerParams(
            dimension_semantics=("arbitrary", "arbitrary"), vmem_limit_bytes=VMEM_LIMIT
        ),
        cost_estimate=pl.CostEstimate(
            flops=n * heads * 6 * length**3,
            transcendentals=0,
            bytes_accessed=6 * n * heads * length**2,
        ),
        name="attend_backward",
    )(info, counts, *args)


ROOT = (2 / np.pi) ** 0.5


def layer_kernel(
    info_ref, atoms_ref, mine0_ref, mine1_ref, other_ref, cot_ref, gains_ref, *rest, bits_a, bits_b
):
    a_refs, b_refs = rest[:4], rest[4:8]
    out_ref, first_ref, gm_mine_ref, gm_other_ref = rest[8:12]
    ga_refs, gb_refs = rest[12:16], rest[16:20]
    win_s, wout_s, ow_s, sum_s, acc_s, gh_s, normed_s, inv_s, hid_s, hid_t_s, mixed_s = rest[20:]
    me = 2 * info_ref[0] + info_ref[1]
    c, steps = pl.program_id(0), pl.num_programs(0)
    part = a_refs[0].shape[0]
    dim = atoms_ref.shape[1]
    length, width = mine0_ref.shape
    rows = dim // (4 * part)
    ff_rows = b_refs[0].shape[1]
    e_rows = dim // (2 * part)

    def shards(bits, refs):
        for p in range(4 * part):
            yield p, me ^ relative(p, bits), (refs[p // part], p % part)

    @pl.when(c == 0)
    def _():
        for p, owner, (ref, q) in shards(bits_a, a_refs):
            for k in range(4):
                win_s[k, pl.ds(pl.multiple_of(owner * rows, rows), rows), :] = ref[q, k * rows : (k + 1) * rows, :]
            at = pl.multiple_of((owner // 2) * e_rows, e_rows)
            for k in range(2):
                ow_s[relative(p, bits_a) & 1, pl.ds(at + k * rows, rows), :] = ref[q, 4 * rows :, k * width : (k + 1) * width]
        for p, owner, (ref, q) in shards(bits_b, b_refs):
            wout_s[pl.ds(pl.multiple_of(owner * ff_rows, ff_rows), ff_rows), :] = ref[q]
        mixed_s[:length] = mine0_ref[...]
        mixed_s[length:] = mine1_ref[...]
        first_sum = (
            atoms_ref[...].astype(F32) + dot_nt(mixed_s[...], ow_s[0]) + dot_nt(other_ref[...], ow_s[1])
        )
        sum_s[...] = first_sum
        center = first_sum - jnp.mean(first_sum, -1, keepdims=True)
        inverse = lax.rsqrt(jnp.mean(center * center, -1, keepdims=True) + 1e-05)
        normed = center * inverse
        normed_s[...] = normed
        inv_s[...] = inverse
        hidden = (normed * gains_ref[1:2, :]).astype(BF16)
        hid_s[...] = hidden
        hid_t_s[...] = hidden.T
        acc_s[...] = jnp.zeros_like(acc_s)
        gh_s[...] = jnp.zeros_like(gh_s)

    win = win_s[c]
    wout = wout_s[pl.ds(pl.multiple_of(c * dim, dim), dim), :]
    inner = dot(hid_s[...], win)
    square = inner * inner
    tanh = jnp.tanh(ROOT * inner * (1.0 + 0.044715 * square))
    activated = (0.5 * inner * (1.0 + tanh)).astype(BF16)
    slope = 0.5 * (1.0 + tanh) + (0.5 * ROOT) * inner * (1.0 - tanh * tanh) * (1.0 + (3 * 0.044715) * square)
    acc_s[...] += dot(activated, wout)
    grad_inner = (dot_nt(cot_ref[...], wout) * slope).astype(BF16)
    gh_s[...] += dot_nt(grad_inner, win)
    grad_in = dot(hid_t_s[...], grad_inner).astype(BF16)
    win_s[c] = grad_in
    grad_out = dot_tn(activated, cot_ref[...]).astype(BF16)
    wout_s[pl.ds(pl.multiple_of(c * dim, dim), dim), :] = grad_out

    @pl.when(c == steps - 1)
    def _():
        out_ref[...] = (sum_s[...] + acc_s[...]).astype(BF16)
        normed = normed_s[...]
        grad_norm = gh_s[...] * gains_ref[1:2, :]
        grad_first = cot_ref[...].astype(F32) + inv_s[...] * (
            grad_norm
            - jnp.mean(grad_norm, -1, keepdims=True)
            - normed * jnp.mean(grad_norm * normed, -1, keepdims=True)
        )
        first_ref[...] = grad_first
        grad_attention = grad_first.astype(BF16)
        gm_mine_ref[...] = dot(grad_attention, ow_s[0]).astype(BF16)
        gm_other_ref[...] = dot(grad_attention, ow_s[1]).astype(BF16)
        ow_s[0] = dot_tn(grad_attention, mixed_s[...]).astype(BF16)
        ow_s[1] = dot_tn(grad_attention, other_ref[...]).astype(BF16)
        for p, owner, (ref, q) in shards(bits_a, ga_refs):
            for k in range(4):
                ref[q, k * rows : (k + 1) * rows, :] = win_s[k, pl.ds(pl.multiple_of(owner * rows, rows), rows), :]
            at = pl.multiple_of((owner // 2) * e_rows, e_rows)
            for k in range(2):
                ref[q, 4 * rows :, k * width : (k + 1) * width] = ow_s[relative(p, bits_a) & 1, pl.ds(at + k * rows, rows), :]
        for p, owner, (ref, q) in shards(bits_b, gb_refs):
            ref[q] = wout_s[pl.ds(pl.multiple_of(owner * ff_rows, ff_rows), ff_rows), :]


def layer_call(info, atoms, mine, other, cot, gains, a_parts, b_parts, bits_a, bits_b):
    own, dim = atoms.shape
    width = other.shape[1]
    ff = 4 * b_parts[0].shape[0] * b_parts[0].shape[1]
    args = [atoms, *mine, other, cot, gains, *a_parts, *b_parts]
    shape = jax.ShapeDtypeStruct
    outs = [
        shape((own, dim), BF16),
        shape((own, dim), F32),
        shape((own, width), BF16),
        shape((own, width), BF16),
        *[shape(x.shape, BF16) for x in (*a_parts, *b_parts)],
    ]
    spec = pltpu.PrefetchScalarGridSpec(
        num_scalar_prefetch=1,
        grid=(ff // dim,),
        in_specs=[whole(x.shape) for x in args],
        out_specs=[whole(x.shape) for x in outs],
        scratch_shapes=[
            pltpu.VMEM((ff // dim, dim, dim), BF16),
            pltpu.VMEM((ff, dim), BF16),
            pltpu.VMEM((2, dim, width), BF16),
            pltpu.VMEM((own, dim), F32),
            pltpu.VMEM((own, dim), F32),
            pltpu.VMEM((own, dim), F32),
            pltpu.VMEM((own, dim), F32),
            pltpu.VMEM((own, 1), F32),
            pltpu.VMEM((own, dim), BF16),
            pltpu.VMEM((dim, own), BF16),
            pltpu.VMEM((own, width), BF16),
        ],
    )
    return pl.pallas_call(
        partial(layer_kernel, bits_a=bits_a, bits_b=bits_b),
        grid_spec=spec,
        out_shape=outs,
        compiler_params=pltpu.CompilerParams(
            dimension_semantics=("arbitrary",), vmem_limit_bytes=VMEM_LIMIT
        ),
        cost_estimate=pl.CostEstimate(
            flops=12 * own * dim * ff, transcendentals=own * ff, bytes_accessed=8 * dim * ff
        ),
        name="layer",
    )(info, *args)


def project_grad_kernel(me_ref, *refs, bits, parts):
    b = me_ref[0]
    near_ref, far_ref, full_s = refs[2 * parts :]
    half = near_ref.shape[0]
    rows = full_s.shape[1] // (2 * half)
    for s in range(3):
        full_s[s] = sum(dot(refs[k][...], refs[parts + k][s]) for k in range(parts)).astype(BF16)
    for p in range(2 * half):
        ref, q = (near_ref, p) if p < half else (far_ref, p - half)
        at = pl.multiple_of((b ^ relative(p, bits)) * rows, rows)
        for s in range(3):
            ref[q, s * rows : (s + 1) * rows, :] = full_s[s, pl.ds(at, rows), :]


def project_grad_call(me, hid_ts, gps, bits):
    dim, width = hid_ts[0].shape[0], gps[0].shape[2]
    half = 2 ** (len(bits) - 1)
    rows = dim // (2 * half)
    args = [*hid_ts, *gps]
    outs = [jax.ShapeDtypeStruct((half, 3 * rows, width), BF16)] * 2
    return pl.pallas_call(
        partial(project_grad_kernel, bits=bits, parts=len(hid_ts)),
        grid_spec=pltpu.PrefetchScalarGridSpec(
            num_scalar_prefetch=1,
            grid=(1,),
            in_specs=[whole(x.shape) for x in args],
            out_specs=[whole(x.shape) for x in outs],
            scratch_shapes=[pltpu.VMEM((3, dim, width), BF16)],
        ),
        out_shape=outs,
        compiler_params=pltpu.CompilerParams(vmem_limit_bytes=32 << 20),
        name="project_grad",
    )(me, *args)


def last_kernel(atoms_ref, gains_ref, first_ref, ga_ref, gb_ref, recv_ref, out_ref):
    values = atoms_ref[...].astype(F32)
    center = values - jnp.mean(values, -1, keepdims=True)
    inverse = lax.rsqrt(jnp.mean(center * center, -1, keepdims=True) + 1e-05)
    normed = center * inverse
    part = ga_ref.shape[0]
    grads = jnp.concatenate([ga_ref[...], gb_ref[...]], 0).astype(F32) + recv_ref[...].astype(F32)
    grad_norm = grads * gains_ref[0:1, :]
    out_ref[...] = (
        first_ref[...]
        + inverse
        * (
            grad_norm
            - jnp.mean(grad_norm, -1, keepdims=True)
            - normed * jnp.mean(grad_norm * normed, -1, keepdims=True)
        )
    ).astype(BF16)


def last_call(atoms, gains, first, gh_a, gh_b, recv):
    args = [atoms, gains, first, gh_a, gh_b, recv]
    return pl.pallas_call(
        last_kernel,
        grid=(1,),
        in_specs=[whole(x.shape) for x in args],
        out_specs=whole(atoms.shape),
        out_shape=jax.ShapeDtypeStruct(atoms.shape, BF16),
        compiler_params=pltpu.CompilerParams(vmem_limit_bytes=32 << 20),
        name="last_norm",
    )(*args)


def join(values, received):
    return jnp.concatenate([values, received], 0)


def add(kept, received):
    return (kept.astype(F32) + received.astype(F32)).astype(BF16)


def halves(values):
    half = values.shape[0] // 2
    return values[:half], values[half:]


def body_pairs(
    atoms, pair, counts, qkv_weight, out_weight, ln1_gain, ln2_gain, w_in, w_out, out_cot, pair_cot,
    batch
):
    info = jnp.stack([lax.axis_index("batch"), lax.axis_index("head")])
    h = info[1]
    own, dim = atoms.shape
    length = pair.shape[2]
    width = qkv_weight.shape[2]
    shard = ln1_gain.shape[0]
    top = batch.bit_length() - 1
    far_bits = [1 << k for k in range(top - 1, 1, -1)]
    batch_bits = (*far_bits, 2, 1)
    bits_a = [2 * bit for bit in far_bits] + [4, 1, 2]
    bits_b = [2 * bit for bit in far_bits] + [1, 4, 2]
    nz = len(far_bits)
    over_batch = lambda x, bit: swap(x, "batch", batch, bit)
    over_head = lambda x: swap(x, "head", 2, 1)
    over_both = lambda x, bit: swap(x, BOTH, 2 * batch, bit)
    tie = lax.optimization_barrier

    def split_gain(gain):
        high = gain.astype(BF16)
        return [high, (gain - high.astype(F32)).astype(BF16)]

    gain_row = jnp.concatenate(split_gain(ln1_gain) + split_gain(ln2_gain))[None]
    tail = jnp.pad(gain_row, ((0, 7), (0, width - gain_row.shape[1])))
    gathered = jnp.concatenate([qkv_weight.reshape(-1, width), tail], 0)[None]
    gathered, late = tie((gathered, (w_in, out_weight, w_out)))
    bulk = pack_call(*late)[None]
    cut = bulk.shape[1] - w_out.shape[0]
    for k, bit in enumerate(batch_bits[:-1]):
        gathered = join(gathered, over_batch(gathered, bit))
        if k == 0:
            gathered, bulk = tie((gathered, bulk))
        elif k == nz - 1:
            gathered, atoms_late = tie((gathered, atoms))
    far = over_batch(gathered, 1)
    atoms_other = over_head(atoms_late)
    gain_at = 3 * qkv_weight.shape[1]
    gains_other = over_head(jnp.concatenate([gathered[:, gain_at:], far[:, gain_at:]], 0))

    per = own // length
    mine = lambda k: lambda info: info[1] * per + k
    theirs = lambda info: (1 - info[1]) * per
    plan = [(mine(0), 1, atoms, 0), (theirs, per, atoms_other, 0), (mine(1), per - 1, atoms, 1)]
    stage_bits = [(bit, bit) for bit in bits_a[:nz]] + list(zip(bits_a[nz:], bits_b[nz:]))
    last = len(stage_bits) - 1
    for bit in bits_a[:nz]:
        bulk = join(bulk, over_both(bulk, bit))
    parts = (bulk[:, :cut], bulk[:, cut:])

    def send_stage(parts, k):
        return tuple(over_both(x, bit) for x, bit in zip(parts, stage_bits[k]))

    received = ()
    cnt = counts
    carried = ()
    saved = []
    for k, (mol, n, rows, at) in enumerate(plan):
        stage = nz + k
        if stage < last:
            parts = tuple(map(join, parts, received)) if received else parts
            cnt, parts = tie((cnt, parts))
            received = send_stage(parts, stage)
        else:
            cnt, received = tie((cnt, received))
            a_parts, b_parts = (
                [x, y, over_both(x, bit), over_both(y, bit)]
                for x, y, bit in zip(parts, received, stage_bits[last])
            )
        if k == 0:
            results = attend_forward_call(
                info, mol, n, cnt, rows, at, (gathered, far, gains_other), pair, carried, batch_bits, shard
            )
            weights, gains = results[6:]
        else:
            results = attend_forward_call(
                info, mol, n, cnt, rows, at, (weights, gains), pair, carried
            )
        new_pair, exps, mixed, hid_t, qkv_t, inverse = results[:6]
        if stage < last:
            received, inverse = tie((received, inverse))
        carried = (new_pair, exps)
        saved.append((mixed, hid_t, qkv_t, inverse))
    mixed_other = over_head(saved[1][0])

    output, first, gm_mine, gm_other, *pieces = layer_call(
        info, atoms, (saved[0][0], saved[2][0]), mixed_other, out_cot, gains, a_parts, b_parts, bits_a, bits_b
    )
    gm_received = over_head(gm_other)

    parts = [p[:2] for p in (pieces[:4], pieces[4:])]
    received = [[over_both(x, bit) for x in p[2:]] for p, bit in zip((pieces[:4], pieces[4:]), stage_bits[last])]
    send_halves = lambda parts, k: [over_both(high, bit) for (_, high), bit in zip(parts, stage_bits[k])]
    add_halves = lambda parts, received: [add(low, r) for (low, _), r in zip(parts, received)]
    carried = ()
    grads = []
    cnt = counts
    gms = (gm_mine, gm_received, gm_mine)
    for k, (mol, n, _, at) in enumerate(plan):
        if k > 0:
            if k > 1:
                parts = [halves(x) for x in add_halves(parts, received)]
            else:
                parts = [[add(x, r) for x, r in zip(*pair)] for pair in zip(parts, received)]
            cnt, parts = tie((cnt, parts))
            received = send_halves(parts, last - k)
        pair_grad, gh, gp = attend_backward_call(
            info, mol, n, cnt, gms[k], at, saved[k], weights, exps, pair_cot, carried
        )
        received, gp = tie((received, gp))
        if k == 1:
            hidden_received = over_head(gh)
        elif k == 2:
            hidden_received, gp = tie((hidden_received, gp))
        carried = (pair_grad,)
        grads.append((gh, gp))
    bulk = jnp.concatenate(add_halves(parts, received), 1)
    gps, bulk = tie(([g[1] for g in grads], bulk))
    near, far = project_grad_call(info, [s[1] for s in saved], gps, batch_bits)
    near = add(near, over_batch(far, batch_bits[-1]))
    bulk_keep, bulk_send = halves(bulk)
    bulk_received = over_both(bulk_send, bits_a[nz - 1])
    for k, bit in enumerate(batch_bits[-2::-1]):
        keep, send = halves(near)
        received = over_batch(send, bit)
        near = add(keep, received)
        if k == 0:
            _, bulk_received = tie((received, bulk_received))
    bulk = add(bulk_keep, bulk_received)
    for bit in bits_a[: nz - 1][::-1]:
        keep, send = halves(bulk)
        bulk = add(keep, over_both(send, bit))
    qkv_grad = near[0].reshape(qkv_weight.shape).astype(F32)
    gain_part = jnp.sum(qkv_grad * qkv_weight.astype(F32), (0, 2)).reshape(2, shard)
    gain_mine = lax.dynamic_index_in_dim(gain_part, h, 0, False)
    gain_other = over_head(lax.dynamic_index_in_dim(gain_part, 1 - h, 0, False))
    gain_one_grad = (gain_mine + gain_other) / ln1_gain
    atoms_grad = last_call(atoms, gains, first, grads[0][0], grads[2][0], hidden_received)
    bulk = bulk[0].astype(F32)
    shard_rows = w_in.shape[0]
    blocks = w_in.shape[1] // dim
    in_grad = jnp.concatenate([bulk[k * shard_rows : (k + 1) * shard_rows] for k in range(blocks)], 1)
    out_grad = jnp.concatenate([bulk[blocks * shard_rows : cut, k * width : (k + 1) * width] for k in range(2)], 0)
    outer_grad = bulk[cut:]
    gain_two_grad = jnp.sum(in_grad * w_in.astype(F32), 1) / ln2_gain
    return (
        output, new_pair, atoms_grad, pair_grad, qkv_grad, out_grad,
        gain_one_grad, gain_two_grad, in_grad, outer_grad,
    )


def solution(mesh):
    rows = P(BOTH, None)
    heads = P("batch", "head", None, None)
    batch, head = mesh.shape["batch"], mesh.shape["head"]
    body = partial(body_pairs, batch=batch) if (batch, head) == (16, 2) else body_native
    return jax.shard_map(
        body,
        mesh=mesh,
        in_specs=(
            rows, heads, P("batch"), P(None, "batch", "head"), P("batch", "head"),
            P(BOTH), P(BOTH), rows, rows, rows, heads,
        ),
        out_specs=(
            rows, heads, rows, heads, P(None, "batch", "head"), P("batch", "head"),
            P(BOTH), P(BOTH), rows, rows,
        ),
        check_vma=False,
    )
```

```python
from functools import partial

import jax
import jax.numpy as jnp
import numpy as np
from jax import lax
from jax.experimental import pallas as pl
from jax.experimental.pallas import tpu as pltpu
from jax.sharding import PartitionSpec as P

F32 = jnp.float32
BF16 = jnp.bfloat16
NEG = -1e30
VMEM_LIMIT = 48 << 20
BOTH = ("batch", "head")


def layer_stats(values):
    center = values - jnp.mean(values, -1, keepdims=True)
    inverse = lax.rsqrt(jnp.mean(center * center, -1, keepdims=True) + 1e-05)
    return (center * inverse, inverse)


def norm_back(grad_norm, normed, inverse):
    return inverse * (
        grad_norm
        - jnp.mean(grad_norm, -1, keepdims=True)
        - normed * jnp.mean(grad_norm * normed, -1, keepdims=True)
    )


def times_transposed(left, right):
    return lax.dot_general(
        left, right, (((1,), (1,)), ((), ())), preferred_element_type=jnp.float32
    )


def transposed_times(left, right):
    return lax.dot_general(
        left, right, (((0,), (0,)), ((), ())), preferred_element_type=jnp.float32
    )


def block_masks(count_part, length):
    positions = jnp.arange(length, dtype=jnp.int32)
    valid_rows = positions[None, :] < count_part[:, None]
    both_valid = valid_rows[:, None, :, None] & valid_rows[:, None, None, :]
    return (valid_rows, both_valid)


def scores_of(query_part, key_part, pair_part, score_scale):
    raw = jnp.einsum("mqhd,mkhd->mhqk", query_part, key_part, preferred_element_type=jnp.float32)
    return raw * score_scale + pair_part.astype(jnp.float32)


def attend_forward(inputs, score_scale):
    query_part, key_part, value_part, pair_part, count_part = inputs
    valid_rows, both_valid = block_masks(count_part, query_part.shape[1])
    logits = scores_of(query_part, key_part, pair_part, score_scale)
    new_pair = jnp.where(both_valid, logits, 0.0).astype(jnp.bfloat16)
    masked = jnp.where(valid_rows[:, None, None, :], logits, -1e30)
    row_max = jnp.max(masked, -1, keepdims=True)
    exponent = jnp.exp(masked - row_max)
    row_total = jnp.sum(exponent, -1, keepdims=True)
    soft_weights = (exponent / row_total).astype(jnp.bfloat16)
    mixed = jnp.einsum(
        "mhqk,mkhd->mqhd", soft_weights, value_part, preferred_element_type=jnp.float32
    )
    mixed = jnp.where(valid_rows[:, :, None, None], mixed, 0.0).astype(jnp.bfloat16)
    return (new_pair, mixed, row_max[..., 0] + jnp.log(row_total[..., 0]))


def attend_backward(inputs, score_scale):
    query_part, key_part, value_part, pair_part, count_part, grad_mixed, log_total, cot_part = (
        inputs
    )
    valid_rows, both_valid = block_masks(count_part, query_part.shape[1])
    logits = scores_of(query_part, key_part, pair_part, score_scale)
    masked = jnp.where(valid_rows[:, None, None, :], logits, -1e30)
    soft = jnp.exp(masked - log_total[..., None])
    grad_masked = jnp.where(valid_rows[:, :, None, None], grad_mixed, jnp.zeros_like(grad_mixed))
    grad_soft = jnp.einsum(
        "mqhd,mkhd->mhqk", grad_masked, value_part, preferred_element_type=jnp.float32
    )
    grad_scores = soft * (grad_soft - jnp.sum(grad_soft * soft, -1, keepdims=True))
    grad_scores = (grad_scores + jnp.where(both_valid, cot_part.astype(jnp.float32), 0.0)).astype(
        jnp.bfloat16
    )
    grad_query = (
        jnp.einsum("mhqk,mkhd->mqhd", grad_scores, key_part, preferred_element_type=jnp.float32)
        * score_scale
    ).astype(jnp.bfloat16)
    grad_key = (
        jnp.einsum("mhqk,mqhd->mkhd", grad_scores, query_part, preferred_element_type=jnp.float32)
        * score_scale
    ).astype(jnp.bfloat16)
    grad_value = jnp.einsum(
        "mhqk,mqhd->mkhd",
        soft.astype(jnp.bfloat16),
        grad_masked,
        preferred_element_type=jnp.float32,
    ).astype(jnp.bfloat16)
    return (grad_scores, grad_query, grad_key, grad_value)


def body_native(
    atoms, pair, counts, qkv_weight, out_weight, ln1_gain, ln2_gain, w_in, w_out, out_cot, pair_cot
):
    mols_here, heads_here, length = (pair.shape[0], pair.shape[1], pair.shape[2])
    qkv_full, out_full = (
        lax.all_gather(qkv_weight, "batch", axis=1, tiled=True),
        lax.all_gather(out_weight, "batch", axis=0, tiled=True),
    )
    gain_one, gain_two, inner_weight, outer_weight = (
        lax.all_gather(ln1_gain.astype(jnp.bfloat16), ("batch", "head"), axis=0, tiled=True).astype(
            ln1_gain.dtype
        ),
        lax.all_gather(ln2_gain.astype(jnp.bfloat16), ("batch", "head"), axis=0, tiled=True).astype(
            ln2_gain.dtype
        ),
        lax.all_gather(w_in, ("batch", "head"), axis=0, tiled=True),
        lax.all_gather(w_out, ("batch", "head"), axis=0, tiled=True),
    )
    width_here = qkv_full.shape[2]
    head_size = width_here // heads_here
    score_scale = head_size ** (-0.5)
    blocks = mols_here // 2
    group_total = mols_here * length
    atoms_f = atoms.astype(jnp.float32)
    normed_one, inverse_one = layer_stats(atoms_f)
    hidden_one = (normed_one * gain_one).astype(jnp.bfloat16)
    group_rows = lax.all_gather(hidden_one, "head", axis=0, tiled=True)
    projected = jnp.einsum(
        "rd,sde->sre", group_rows, qkv_full, preferred_element_type=jnp.float32
    ).astype(jnp.bfloat16)

    def to_blocks(values):
        return values.reshape(blocks, 2, length, heads_here, head_size)

    query_all, key_all, value_all = (
        to_blocks(projected[0]),
        to_blocks(projected[1]),
        to_blocks(projected[2]),
    )
    pair_blocks = pair.reshape(blocks, 2, heads_here, length, length)
    count_blocks = counts.reshape(blocks, 2)
    new_pair, mixed, log_total = lax.map(
        partial(attend_forward, score_scale=score_scale),
        (query_all, key_all, value_all, pair_blocks, count_blocks),
    )
    mixed_flat = mixed.reshape(group_total, width_here)
    slab_rows = mixed_flat
    attention = lax.psum_scatter(
        times_transposed(slab_rows, out_full).astype(jnp.bfloat16),
        "head",
        scatter_dimension=0,
        tiled=True,
    ).astype(jnp.float32)
    first_sum = atoms_f + attention
    normed_two, inverse_two = layer_stats(first_sum)
    hidden_two = (normed_two * gain_two).astype(jnp.bfloat16)
    inner = jnp.dot(hidden_two, inner_weight, preferred_element_type=jnp.float32)
    gelu_value, gelu_pull = jax.vjp(jax.nn.gelu, inner)
    activated = gelu_value.astype(jnp.bfloat16)
    output = first_sum + jnp.dot(activated, outer_weight, preferred_element_type=jnp.float32)
    grad_outer_w = transposed_times(activated, out_cot)
    grad_act = times_transposed(out_cot, outer_weight)
    grad_inner = gelu_pull(grad_act)[0].astype(jnp.bfloat16)
    grad_inner_w = transposed_times(hidden_two, grad_inner)
    grad_hidden_two = times_transposed(grad_inner, inner_weight)
    grad_gain_two = jnp.sum(grad_hidden_two * normed_two, 0)
    grad_first = out_cot.astype(jnp.float32) + norm_back(
        grad_hidden_two * gain_two, normed_two, inverse_two
    )
    grad_attention = grad_first.astype(jnp.bfloat16)
    group_grad = lax.all_gather(grad_attention, "head", axis=0, tiled=True)
    grad_out_full = transposed_times(group_grad, mixed_flat)
    grad_mixed = jnp.dot(group_grad, out_full, preferred_element_type=jnp.float32).astype(
        jnp.bfloat16
    )
    cot_blocks = pair_cot.reshape(blocks, 2, heads_here, length, length)
    grad_scores, grad_query, grad_key, grad_value = lax.map(
        partial(attend_backward, score_scale=score_scale),
        (
            query_all,
            key_all,
            value_all,
            pair_blocks,
            count_blocks,
            to_blocks(grad_mixed),
            log_total,
            cot_blocks,
        ),
    )
    grad_projected = jnp.stack(
        [
            grad_query.reshape(group_total, width_here),
            grad_key.reshape(group_total, width_here),
            grad_value.reshape(group_total, width_here),
        ]
    )
    grad_qkv_full = jnp.einsum(
        "rd,sre->sde", group_rows, grad_projected, preferred_element_type=jnp.float32
    )
    slab_rows = grad_projected
    grad_hidden_one = lax.psum_scatter(
        jnp.einsum("sre,sde->rd", slab_rows, qkv_full, preferred_element_type=jnp.float32).astype(
            jnp.bfloat16
        ),
        "head",
        scatter_dimension=0,
        tiled=True,
    ).astype(jnp.float32)
    grad_gain_one = jnp.sum(grad_hidden_one * normed_one, 0)
    atoms_grad = grad_first + norm_back(grad_hidden_one * gain_one, normed_one, inverse_one)
    qkv_grad, out_grad = (
        lax.psum_scatter(
            grad_qkv_full.astype(jnp.bfloat16), "batch", scatter_dimension=1, tiled=True
        ).astype(jnp.float32),
        lax.psum_scatter(
            grad_out_full.astype(jnp.bfloat16), "batch", scatter_dimension=0, tiled=True
        ).astype(jnp.float32),
    )
    gain_one_grad, gain_two_grad, inner_grad, outer_grad = (
        lax.psum_scatter(grad_gain_one, ("batch", "head"), scatter_dimension=0, tiled=True),
        lax.psum_scatter(grad_gain_two, ("batch", "head"), scatter_dimension=0, tiled=True),
        lax.psum_scatter(grad_inner_w, ("batch", "head"), scatter_dimension=0, tiled=True),
        lax.psum_scatter(grad_outer_w, ("batch", "head"), scatter_dimension=0, tiled=True),
    )
    return (
        output.astype(jnp.bfloat16),
        new_pair.reshape(mols_here, heads_here, length, length),
        atoms_grad.astype(jnp.bfloat16),
        grad_scores.reshape(mols_here, heads_here, length, length),
        qkv_grad,
        out_grad,
        gain_one_grad,
        gain_two_grad,
        inner_grad,
        outer_grad,
    )


def dot(left, right):
    return jnp.dot(left, right, preferred_element_type=F32)


def dot_nt(left, right):
    return lax.dot_general(left, right, (((1,), (1,)), ((), ())), preferred_element_type=F32)


def dot_tn(left, right):
    return lax.dot_general(left, right, (((0,), (0,)), ((), ())), preferred_element_type=F32)


def swap(values, axes, count, bit):
    return lax.ppermute(values, axes, [(i, i ^ bit) for i in range(count)])


def relative(position, bits):
    return sum(((position >> k) & 1) * bit for k, bit in enumerate(bits))


def whole(shape):
    return pl.BlockSpec(shape, lambda *_: (0,) * len(shape))


def unpack_shards(info_ref, near_ref, far_ref, other_ref, w_ref, gains_ref, rows_s, bits, shard):
    b, h = info_ref[0], info_ref[1]
    half = near_ref.shape[0]
    rows = w_ref.shape[1] // (2 * half)
    dim = gains_ref.shape[1]
    for p in range(2 * half):
        ref, q = (near_ref, p) if p < half else (far_ref, p - half)
        at = pl.multiple_of((b ^ relative(p, bits)) * rows, rows)
        for s in range(3):
            w_ref[s, pl.ds(at, rows), :] = ref[q, s * rows : (s + 1) * rows, :]
        rows_s[0, p : p + 1, :] = ref[q, 3 * rows : 3 * rows + 1, :].astype(F32)
        rows_s[1, p : p + 1, :] = other_ref[p, 0:1, :].astype(F32)
    lanes = rows_s.shape[2]
    count = 2 * half
    lane = lax.broadcasted_iota(jnp.int32, (lanes, dim), 0)
    col = lax.broadcasted_iota(jnp.int32, (lanes, dim), 1)
    block = lax.broadcasted_iota(jnp.int32, (count, dim), 1) // rows
    side = (lax.broadcasted_iota(jnp.int32, (count, dim), 1) // shard) & 1
    place = lax.broadcasted_iota(jnp.int32, (count, dim), 0)
    owner = sum(((place >> k) & 1) * bit for k, bit in enumerate(bits)) ^ b
    values = rows_s[...].astype(BF16)
    for g in range(2):
        start = g * 2 * shard + lax.rem(col, shard)
        pick = jnp.where((lane == start) | (lane == start + shard), 1.0, 0.0).astype(BF16)
        spread = jnp.where(side == h, dot(values[0], pick), dot(values[1], pick))
        gains_ref[g : g + 1, :] = jnp.sum(jnp.where(owner == block, spread, 0.0), 0, keepdims=True)


def pack_kernel(in_ref, proj_ref, out_ref, bulk_ref):
    rows, dim = in_ref.shape[0], bulk_ref.shape[1]
    blocks = in_ref.shape[1] // dim
    half, width = proj_ref.shape[0] // 2, proj_ref.shape[1]
    for k in range(blocks):
        bulk_ref[k * rows : (k + 1) * rows, :] = in_ref[:, k * dim : (k + 1) * dim]
    at = blocks * rows
    for k in range(2):
        bulk_ref[at : at + half, k * width : (k + 1) * width] = proj_ref[k * half : (k + 1) * half, :]
    bulk_ref[at + half :, :] = out_ref[...]


def pack_call(w_in, out_weight, w_out):
    args = [w_in, out_weight, w_out]
    dim = w_out.shape[1]
    out = jax.ShapeDtypeStruct((sum(x.size for x in args) // dim, dim), BF16)
    return pl.pallas_call(
        pack_kernel,
        grid=(1,),
        in_specs=[whole(x.shape) for x in args],
        out_specs=whole(out.shape),
        out_shape=out,
        name="pack",
    )(*args)


def attend_forward_kernel(
    info_ref, cnt_ref, atoms_ref, w_ref, gains_ref, pair_ref, *rest, hb, scale, carried, mol, bits, shard
):
    rest0, rest = rest, rest[carried + bool(bits) :]
    new_ref, exp_ref, mixed_ref, hid_t_ref, qkv_t_ref, inv_ref = rest[:6]
    if bits:
        near_ref, far_ref, other_ref, pair_ref = w_ref, gains_ref, pair_ref, rest0[0]
        w_ref, gains_ref = rest[6:8]
        rest = (*rest[:6], *rest[8:-1], rest[-1])
        rows_s = rest[-1]
        rest = rest[:-1]
    q_s, kz_s, va_s, valid_s, sum_s = rest[6:]
    mol_at, step = pl.program_id(0), pl.program_id(1)
    length = atoms_ref.shape[0]
    heads = qkv_t_ref.shape[1]
    lanes = 8 * hb
    count = cnt_ref[mol(info_ref) + mol_at]

    @pl.when((step == 0) & (mol_at == 0))
    def _():
        kz_s[...] = jnp.zeros_like(kz_s)
        if bits:
            unpack_shards(info_ref, near_ref, far_ref, other_ref, w_ref, gains_ref, rows_s, bits, shard)

    @pl.when(step == 0)
    def _():
        values = atoms_ref[...].astype(F32)
        center = values - jnp.mean(values, -1, keepdims=True)
        inverse = lax.rsqrt(jnp.mean(center * center, -1, keepdims=True) + 1e-05)
        hidden = (center * inverse * gains_ref[0:1, :]).astype(BF16)
        hid_t_ref[...] = hidden.T
        query = (dot(hidden, w_ref[0]) * scale).astype(BF16)
        key = dot(hidden, w_ref[1]).astype(BF16)
        value = dot(hidden, w_ref[2]).astype(BF16)
        qkv_t_ref[0] = query.T.reshape(heads, 8, length)
        qkv_t_ref[1] = key.T.reshape(heads, 8, length)
        value_t = value.T.reshape(heads, 8, length)
        qkv_t_ref[2] = value_t
        va_s[:, :8, :] = value_t
        top = lax.broadcasted_iota(jnp.int32, (8, length), 0) == 0
        first = jnp.where(top, 1.0, 0.0).astype(BF16)
        va_s[:, 8:, :] = jnp.broadcast_to(first[None], (heads, 8, length))
        at = lax.broadcasted_iota(jnp.int32, (8, length), 1)
        bias = jnp.where(top & (at >= count), NEG, 0.0).astype(BF16)
        kz_s[:, lanes : lanes + 8, :] = jnp.broadcast_to(bias[None], (hb, 8, length))
        first_lane = jnp.where(lax.broadcasted_iota(jnp.int32, (length, lanes), 1) == 0, 1.0, 0.0).astype(BF16)
        for g in range(heads // hb):
            q_s[g, :, :lanes] = query[:, g * lanes : (g + 1) * lanes]
            q_s[g, :, lanes:] = first_lane
        valid = (lax.broadcasted_iota(jnp.int32, (length, length), 0) < count) & (
            lax.broadcasted_iota(jnp.int32, (length, length), 1) < count
        )
        valid_s[...] = jnp.where(valid, 1.0, 0.0).astype(BF16)

    for i in range(hb):
        kz_s[i, i * 8 : (i + 1) * 8, :] = qkv_t_ref[1, step * hb + i]
    for i in range(hb):
        logits = dot(q_s[step], kz_s[i]) + pair_ref[0, i].astype(F32)
        new_ref[0, i] = logits.astype(BF16) * valid_s[...]
        soft = jnp.exp(logits - jnp.max(logits, -1, keepdims=True)).astype(BF16)
        exp_ref[0, i] = soft
        sum_s[i] = dot_nt(va_s[step * hb + i], exp_ref[0, i])
    inverse = 1.0 / sum_s[:, 8:9, :]
    rows_ok = lax.broadcasted_iota(jnp.int32, (1, 1, length), 2) < count
    mixed = jnp.where(rows_ok, sum_s[:, :8, :] * inverse, 0.0)
    at = pl.ds(pl.multiple_of(step * lanes, lanes), lanes)
    mixed_ref[:, at] = mixed.reshape(lanes, length).T.astype(BF16)
    inv_ref[:, at] = jnp.broadcast_to(inverse, (hb, 8, length)).reshape(lanes, length).T


ANY = pl.BlockSpec(memory_space=pl.ANY)


def pair_spec_of(mol, hb, length):
    return pl.BlockSpec((1, hb, length, length), lambda i, j, info, cnt: (mol(info) + i, j, 0, 0))


def rows_spec(length, cols, at=0):
    return pl.BlockSpec((length, cols), lambda i, *_: (at + i, 0))


def attend_forward_call(info, mol, n, counts, atoms, at, weights, pair, carried, bits=(), shard=0, hb=16):
    _, heads, length, _ = pair.shape
    dim = atoms.shape[1]
    width = 8 * heads
    lanes = 8 * hb
    pair_spec = pair_spec_of(mol, hb, length)
    args = [atoms, *weights, pair, *carried]
    shape = jax.ShapeDtypeStruct
    outs = [
        (shape(pair.shape, BF16), pair_spec),
        (shape(pair.shape, BF16), pair_spec),
        (shape((n * length, width), BF16), rows_spec(length, width)),
        (shape((dim, n * length), BF16), pl.BlockSpec((dim, length), lambda i, *_: (0, i))),
        (
            shape((3 * n, heads, 8, length), BF16),
            pl.BlockSpec((3, heads, 8, length), lambda i, *_: (i, 0, 0, 0)),
        ),
        (shape((n * length, width), F32), rows_spec(length, width)),
    ]
    scratch = [
        pltpu.VMEM((heads // hb, length, 2 * lanes), BF16),
        pltpu.VMEM((hb, 2 * lanes, length), BF16),
        pltpu.VMEM((heads, 16, length), BF16),
        pltpu.VMEM((length, length), BF16),
        pltpu.VMEM((hb, 16, length), F32),
    ]
    if bits:
        outs += [
            (shape((3, dim, width), BF16), whole((3, dim, width))),
            (shape((2, dim), F32), whole((2, dim))),
        ]
        scratch.append(pltpu.VMEM((2, 2 ** len(bits), width), F32))
    spec = pltpu.PrefetchScalarGridSpec(
        num_scalar_prefetch=2,
        grid=(n, heads // hb),
        in_specs=[rows_spec(length, dim, at), *[whole(x.shape) for x in weights], pair_spec]
        + [ANY] * len(carried),
        out_specs=[x[1] for x in outs],
        scratch_shapes=scratch,
    )
    return pl.pallas_call(
        partial(
            attend_forward_kernel,
            hb=hb,
            scale=8**-0.5,
            carried=len(carried),
            mol=mol,
            bits=bits,
            shard=shard,
        ),
        grid_spec=spec,
        out_shape=[x[0] for x in outs],
        input_output_aliases={4 + len(weights) + k: k for k in range(len(carried))},
        compiler_params=pltpu.CompilerParams(
            dimension_semantics=("arbitrary", "arbitrary"), vmem_limit_bytes=VMEM_LIMIT
        ),
        cost_estimate=pl.CostEstimate(
            flops=n * heads * 4 * length**3,
            transcendentals=n * heads * length**2,
            bytes_accessed=6 * n * heads * length**2,
        ),
        name="attend_forward",
    )(info, counts, *args)


def attend_backward_kernel(
    info_ref, cnt_ref, gm_ref, mixed_ref, inv_ref, qkv_t_ref, w_ref, mask_ref, exp_ref, cot_ref, *rest,
    hb, scale, carried, mol
):
    pg_ref, gh_ref, gp_ref, l_s, r_s, gt_s, valid_s, gq_s, gk_s, gv_s = rest[carried:]
    mol_at = pl.program_id(0)
    step, steps = pl.program_id(1), pl.num_programs(1)
    length, width = gm_ref.shape
    heads = qkv_t_ref.shape[1]
    lanes = 8 * hb
    count = cnt_ref[mol(info_ref) + mol_at]

    @pl.when(step == 0)
    def _():
        rows_ok = lax.broadcasted_iota(jnp.int32, (length, width), 0) < count
        scaled = jnp.where(rows_ok, gm_ref[...].astype(F32) * inv_ref[...], 0.0).astype(BF16)
        delta = (-(scaled.astype(F32) * mixed_ref[...].astype(F32))).astype(BF16)
        gt_s[...] = scaled.T.reshape(gt_s.shape)
        for g in range(heads // hb):
            part = slice(g * lanes, (g + 1) * lanes)
            l_s[g, :, :lanes] = scaled[:, part]
            l_s[g, :, lanes:] = delta[:, part]
            r_s[g, :lanes, :] = qkv_t_ref[2, g * hb : (g + 1) * hb].reshape(lanes, length)
            r_s[g, lanes:, :] = jnp.ones((lanes, length), BF16)
        valid = (lax.broadcasted_iota(jnp.int32, (length, length), 0) < count) & (
            lax.broadcasted_iota(jnp.int32, (length, length), 1) < count
        )
        valid_s[...] = jnp.where(valid, 1.0, 0.0).astype(BF16)

    for i in range(0, hb, 16):
        left = [l_s[step] * mask_ref[k : k + 1, :] for k in range(i, i + 16)]
        soft = dot(jnp.concatenate(left, 0), r_s[step])
        for k in range(16):
            part = soft[k * length : (k + 1) * length]
            cot = (cot_ref[0, i + k] * valid_s[...]).astype(F32)
            scores = (exp_ref[0, i + k].astype(F32) * part + cot).astype(BF16)
            pg_ref[0, i + k] = scores
            head = step * hb + i + k
            gq_s[head] = dot_nt(qkv_t_ref[1, head], pg_ref[0, i + k])
            gk_s[head] = dot(qkv_t_ref[0, head], pg_ref[0, i + k])
            gv_s[head] = dot(gt_s[head], exp_ref[0, i + k])

    @pl.when(step == steps - 1)
    def _():
        gp_ref[0] = (gq_s[...] * scale).reshape(width, length).astype(BF16).T
        gp_ref[1] = gk_s[...].reshape(width, length).astype(BF16).T
        gp_ref[2] = gv_s[...].reshape(width, length).astype(BF16).T
        gh_ref[...] = (
            dot_nt(gp_ref[0], w_ref[0]) + dot_nt(gp_ref[1], w_ref[1]) + dot_nt(gp_ref[2], w_ref[2])
        ).astype(BF16)


def attend_backward_call(info, mol, n, counts, gm, at, saved, weights, exps, cot, carried, hb=16):
    _, heads, length, _ = exps.shape
    dim, width = weights.shape[1], weights.shape[2]
    lanes = 8 * hb
    masks = jnp.asarray(np.tile(np.repeat(np.eye(hb, dtype=np.float32), 8, 1), 2), BF16)
    pair_spec = pair_spec_of(mol, hb, length)
    mixed, _, qkv_t, inverse = saved
    args = [gm, mixed, inverse, qkv_t, weights, masks, exps, cot, *carried]
    spec = pltpu.PrefetchScalarGridSpec(
        num_scalar_prefetch=2,
        grid=(n, heads // hb),
        in_specs=[
            rows_spec(length, width, at), rows_spec(length, width), rows_spec(length, width),
            pl.BlockSpec((3, heads, 8, length), lambda i, *_: (i, 0, 0, 0)),
            whole(weights.shape), whole(masks.shape), pair_spec, pair_spec,
        ] + [ANY] * len(carried),
        out_specs=[
            pair_spec,
            rows_spec(length, dim),
            pl.BlockSpec((3, length, width), lambda i, *_: (0, i, 0)),
        ],
        scratch_shapes=[
            pltpu.VMEM((heads // hb, length, 2 * lanes), BF16),
            pltpu.VMEM((heads // hb, 2 * lanes, length), BF16),
            pltpu.VMEM((heads, 8, length), BF16),
            pltpu.VMEM((length, length), BF16),
            pltpu.VMEM((heads, 8, length), F32),
            pltpu.VMEM((heads, 8, length), F32),
            pltpu.VMEM((heads, 8, length), F32),
        ],
    )
    shape = jax.ShapeDtypeStruct
    return pl.pallas_call(
        partial(attend_backward_kernel, hb=hb, scale=8**-0.5, carried=len(carried), mol=mol),
        grid_spec=spec,
        out_shape=[
            shape(exps.shape, BF16),
            shape((n * length, dim), BF16),
            shape((3, n * length, width), BF16),
        ],
        input_output_aliases={10 + k: k for k in range(len(carried))},
        compiler_params=pltpu.CompilerParams(
            dimension_semantics=("arbitrary", "arbitrary"), vmem_limit_bytes=VMEM_LIMIT
        ),
        cost_estimate=pl.CostEstimate(
            flops=n * heads * 6 * length**3,
            transcendentals=0,
            bytes_accessed=6 * n * heads * length**2,
        ),
        name="attend_backward",
    )(info, counts, *args)


ROOT = (2 / np.pi) ** 0.5


def layer_kernel(
    info_ref, atoms_ref, mine0_ref, mine1_ref, other_ref, cot_ref, gains_ref, *rest, bits_a, bits_b
):
    a_refs, b_refs = rest[:4], rest[4:8]
    out_ref, first_ref, gm_mine_ref, gm_other_ref = rest[8:12]
    ga_refs, gb_refs = rest[12:16], rest[16:20]
    win_s, wout_s, ow_s, sum_s, acc_s, gh_s, normed_s, inv_s, hid_s, hid_t_s, mixed_s = rest[20:]
    me = 2 * info_ref[0] + info_ref[1]
    c, steps = pl.program_id(0), pl.num_programs(0)
    part = a_refs[0].shape[0]
    dim = atoms_ref.shape[1]
    length, width = mine0_ref.shape
    rows = dim // (4 * part)
    ff_rows = b_refs[0].shape[1]
    e_rows = dim // (2 * part)

    def shards(bits, refs):
        for p in range(4 * part):
            yield p, me ^ relative(p, bits), (refs[p // part], p % part)

    @pl.when(c == 0)
    def _():
        for p, owner, (ref, q) in shards(bits_a, a_refs):
            for k in range(4):
                win_s[k, pl.ds(pl.multiple_of(owner * rows, rows), rows), :] = ref[q, k * rows : (k + 1) * rows, :]
            at = pl.multiple_of((owner // 2) * e_rows, e_rows)
            for k in range(2):
                ow_s[relative(p, bits_a) & 1, pl.ds(at + k * rows, rows), :] = ref[q, 4 * rows :, k * width : (k + 1) * width]
        for p, owner, (ref, q) in shards(bits_b, b_refs):
            wout_s[pl.ds(pl.multiple_of(owner * ff_rows, ff_rows), ff_rows), :] = ref[q]
        mixed_s[:length] = mine0_ref[...]
        mixed_s[length:] = mine1_ref[...]
        first_sum = (
            atoms_ref[...].astype(F32) + dot_nt(mixed_s[...], ow_s[0]) + dot_nt(other_ref[...], ow_s[1])
        )
        sum_s[...] = first_sum
        center = first_sum - jnp.mean(first_sum, -1, keepdims=True)
        inverse = lax.rsqrt(jnp.mean(center * center, -1, keepdims=True) + 1e-05)
        normed = center * inverse
        normed_s[...] = normed
        inv_s[...] = inverse
        hidden = (normed * gains_ref[1:2, :]).astype(BF16)
        hid_s[...] = hidden
        hid_t_s[...] = hidden.T
        acc_s[...] = jnp.zeros_like(acc_s)
        gh_s[...] = jnp.zeros_like(gh_s)

    win = win_s[c]
    wout = wout_s[pl.ds(pl.multiple_of(c * dim, dim), dim), :]
    inner = dot(hid_s[...], win)
    square = inner * inner
    tanh = jnp.tanh(ROOT * inner * (1.0 + 0.044715 * square))
    activated = (0.5 * inner * (1.0 + tanh)).astype(BF16)
    slope = 0.5 * (1.0 + tanh) + (0.5 * ROOT) * inner * (1.0 - tanh * tanh) * (1.0 + (3 * 0.044715) * square)
    acc_s[...] += dot(activated, wout)
    grad_inner = (dot_nt(cot_ref[...], wout) * slope).astype(BF16)
    gh_s[...] += dot_nt(grad_inner, win)
    grad_in = dot(hid_t_s[...], grad_inner).astype(BF16)
    win_s[c] = grad_in
    grad_out = dot_tn(activated, cot_ref[...]).astype(BF16)
    wout_s[pl.ds(pl.multiple_of(c * dim, dim), dim), :] = grad_out

    @pl.when(c == steps - 1)
    def _():
        out_ref[...] = (sum_s[...] + acc_s[...]).astype(BF16)
        normed = normed_s[...]
        grad_norm = gh_s[...] * gains_ref[1:2, :]
        grad_first = cot_ref[...].astype(F32) + inv_s[...] * (
            grad_norm
            - jnp.mean(grad_norm, -1, keepdims=True)
            - normed * jnp.mean(grad_norm * normed, -1, keepdims=True)
        )
        first_ref[...] = grad_first
        grad_attention = grad_first.astype(BF16)
        gm_mine_ref[...] = dot(grad_attention, ow_s[0]).astype(BF16)
        gm_other_ref[...] = dot(grad_attention, ow_s[1]).astype(BF16)
        ow_s[0] = dot_tn(grad_attention, mixed_s[...]).astype(BF16)
        ow_s[1] = dot_tn(grad_attention, other_ref[...]).astype(BF16)
        for p, owner, (ref, q) in shards(bits_a, ga_refs):
            for k in range(4):
                ref[q, k * rows : (k + 1) * rows, :] = win_s[k, pl.ds(pl.multiple_of(owner * rows, rows), rows), :]
            at = pl.multiple_of((owner // 2) * e_rows, e_rows)
            for k in range(2):
                ref[q, 4 * rows :, k * width : (k + 1) * width] = ow_s[relative(p, bits_a) & 1, pl.ds(at + k * rows, rows), :]
        for p, owner, (ref, q) in shards(bits_b, gb_refs):
            ref[q] = wout_s[pl.ds(pl.multiple_of(owner * ff_rows, ff_rows), ff_rows), :]


def layer_call(info, atoms, mine, other, cot, gains, a_parts, b_parts, bits_a, bits_b):
    own, dim = atoms.shape
    width = other.shape[1]
    ff = 4 * b_parts[0].shape[0] * b_parts[0].shape[1]
    args = [atoms, *mine, other, cot, gains, *a_parts, *b_parts]
    shape = jax.ShapeDtypeStruct
    outs = [
        shape((own, dim), BF16),
        shape((own, dim), F32),
        shape((own, width), BF16),
        shape((own, width), BF16),
        *[shape(x.shape, BF16) for x in (*a_parts, *b_parts)],
    ]
    spec = pltpu.PrefetchScalarGridSpec(
        num_scalar_prefetch=1,
        grid=(ff // dim,),
        in_specs=[whole(x.shape) for x in args],
        out_specs=[whole(x.shape) for x in outs],
        scratch_shapes=[
            pltpu.VMEM((ff // dim, dim, dim), BF16),
            pltpu.VMEM((ff, dim), BF16),
            pltpu.VMEM((2, dim, width), BF16),
            pltpu.VMEM((own, dim), F32),
            pltpu.VMEM((own, dim), F32),
            pltpu.VMEM((own, dim), F32),
            pltpu.VMEM((own, dim), F32),
            pltpu.VMEM((own, 1), F32),
            pltpu.VMEM((own, dim), BF16),
            pltpu.VMEM((dim, own), BF16),
            pltpu.VMEM((own, width), BF16),
        ],
    )
    return pl.pallas_call(
        partial(layer_kernel, bits_a=bits_a, bits_b=bits_b),
        grid_spec=spec,
        out_shape=outs,
        compiler_params=pltpu.CompilerParams(
            dimension_semantics=("arbitrary",), vmem_limit_bytes=VMEM_LIMIT
        ),
        cost_estimate=pl.CostEstimate(
            flops=12 * own * dim * ff, transcendentals=own * ff, bytes_accessed=8 * dim * ff
        ),
        name="layer",
    )(info, *args)


def project_grad_kernel(me_ref, *refs, bits, parts):
    b = me_ref[0]
    near_ref, far_ref, full_s = refs[2 * parts :]
    half = near_ref.shape[0]
    rows = full_s.shape[1] // (2 * half)
    for s in range(3):
        full_s[s] = sum(dot(refs[k][...], refs[parts + k][s]) for k in range(parts)).astype(BF16)
    for p in range(2 * half):
        ref, q = (near_ref, p) if p < half else (far_ref, p - half)
        at = pl.multiple_of((b ^ relative(p, bits)) * rows, rows)
        for s in range(3):
            ref[q, s * rows : (s + 1) * rows, :] = full_s[s, pl.ds(at, rows), :]


def project_grad_call(me, hid_ts, gps, bits):
    dim, width = hid_ts[0].shape[0], gps[0].shape[2]
    half = 2 ** (len(bits) - 1)
    rows = dim // (2 * half)
    args = [*hid_ts, *gps]
    outs = [jax.ShapeDtypeStruct((half, 3 * rows, width), BF16)] * 2
    return pl.pallas_call(
        partial(project_grad_kernel, bits=bits, parts=len(hid_ts)),
        grid_spec=pltpu.PrefetchScalarGridSpec(
            num_scalar_prefetch=1,
            grid=(1,),
            in_specs=[whole(x.shape) for x in args],
            out_specs=[whole(x.shape) for x in outs],
            scratch_shapes=[pltpu.VMEM((3, dim, width), BF16)],
        ),
        out_shape=outs,
        compiler_params=pltpu.CompilerParams(vmem_limit_bytes=32 << 20),
        cost_estimate=pl.CostEstimate(flops=1000, transcendentals=0, bytes_accessed=1000),
        name="project_grad",
    )(me, *args)


def last_kernel(atoms_ref, gains_ref, first_ref, ga_ref, gb_ref, recv_ref, out_ref):
    values = atoms_ref[...].astype(F32)
    center = values - jnp.mean(values, -1, keepdims=True)
    inverse = lax.rsqrt(jnp.mean(center * center, -1, keepdims=True) + 1e-05)
    normed = center * inverse
    part = ga_ref.shape[0]
    grads = jnp.concatenate([ga_ref[...], gb_ref[...]], 0).astype(F32) + recv_ref[...].astype(F32)
    grad_norm = grads * gains_ref[0:1, :]
    out_ref[...] = (
        first_ref[...]
        + inverse
        * (
            grad_norm
            - jnp.mean(grad_norm, -1, keepdims=True)
            - normed * jnp.mean(grad_norm * normed, -1, keepdims=True)
        )
    ).astype(BF16)


def last_call(atoms, gains, first, gh_a, gh_b, recv):
    args = [atoms, gains, first, gh_a, gh_b, recv]
    return pl.pallas_call(
        last_kernel,
        grid=(1,),
        in_specs=[whole(x.shape) for x in args],
        out_specs=whole(atoms.shape),
        out_shape=jax.ShapeDtypeStruct(atoms.shape, BF16),
        compiler_params=pltpu.CompilerParams(vmem_limit_bytes=32 << 20),
        cost_estimate=pl.CostEstimate(flops=1000, transcendentals=0, bytes_accessed=1000),
        name="last_norm",
    )(*args)


def join(values, received):
    return jnp.concatenate([values, received], 0)


def add(kept, received):
    return (kept.astype(F32) + received.astype(F32)).astype(BF16)


def halves(values):
    half = values.shape[0] // 2
    return values[:half], values[half:]


def body_pairs(
    atoms, pair, counts, qkv_weight, out_weight, ln1_gain, ln2_gain, w_in, w_out, out_cot, pair_cot,
    batch
):
    info = jnp.stack([lax.axis_index("batch"), lax.axis_index("head")])
    h = info[1]
    own, dim = atoms.shape
    length = pair.shape[2]
    width = qkv_weight.shape[2]
    shard = ln1_gain.shape[0]
    top = batch.bit_length() - 1
    far_bits = [1 << k for k in range(top - 1, 1, -1)]
    batch_bits = (*far_bits, 2, 1)
    bits_a = [2 * bit for bit in far_bits] + [4, 1, 2]
    bits_b = [2 * bit for bit in far_bits] + [1, 4, 2]
    nz = len(far_bits)
    over_batch = lambda x, bit: swap(x, "batch", batch, bit)
    over_head = lambda x: swap(x, "head", 2, 1)
    over_both = lambda x, bit: swap(x, BOTH, 2 * batch, bit)
    tie = lax.optimization_barrier

    def split_gain(gain):
        high = gain.astype(BF16)
        return [high, (gain - high.astype(F32)).astype(BF16)]

    gain_row = jnp.concatenate(split_gain(ln1_gain) + split_gain(ln2_gain))[None]
    tail = jnp.pad(gain_row, ((0, 7), (0, width - gain_row.shape[1])))
    gathered = jnp.concatenate([qkv_weight.reshape(-1, width), tail], 0)[None]
    gathered, late, atoms_late = tie((gathered, (w_in, out_weight, w_out), atoms))
    bulk = pack_call(*late)[None]
    cut = bulk.shape[1] - w_out.shape[0]
    for k, bit in enumerate(batch_bits[:-1]):
        gathered = join(gathered, over_batch(gathered, bit))
        if k == 0:
            gathered, bulk = tie((gathered, bulk))
    far = over_batch(gathered, 1)
    atoms_other = over_head(atoms_late)
    gain_at = 3 * qkv_weight.shape[1]
    gains_other = over_head(jnp.concatenate([gathered[:, gain_at:], far[:, gain_at:]], 0))

    per = own // length
    mine = lambda k: lambda info: info[1] * per + k
    theirs = lambda info: (1 - info[1]) * per
    stage_bits = [(bit, bit) for bit in bits_a[:nz]] + list(zip(bits_a[nz:], bits_b[nz:]))
    last = len(stage_bits) - 1
    for bit in bits_a[:nz]:
        bulk = join(bulk, over_both(bulk, bit))
    bulk, gains_other, atoms_other = tie((bulk, gains_other, atoms_other))
    parts = (bulk[:, :cut], bulk[:, cut:])

    def send_stage(parts, k):
        return tuple(over_both(x, bit) for x, bit in zip(parts, stage_bits[k]))

    plan = [(mine(0), 1, atoms, 0), (theirs, per, atoms_other, 0), (mine(1), per - 1, atoms, 1)]
    received = ()
    cnt = counts
    carried = ()
    saved = []
    for k, (mol, n, rows, at) in enumerate(plan):
        stage = nz + k
        if stage < last:
            parts = tuple(map(join, parts, received)) if received else parts
            cnt, parts = tie((cnt, parts))
            received = send_stage(parts, stage)
        else:
            cnt, received = tie((cnt, received))
            a_parts, b_parts = (
                [x, y, over_both(x, bit), over_both(y, bit)]
                for x, y, bit in zip(parts, received, stage_bits[last])
            )
        if k == 0:
            results = attend_forward_call(
                info, mol, n, cnt, rows, at, (gathered, far, gains_other), pair, carried, batch_bits, shard
            )
            weights, gains = results[6:]
        else:
            results = attend_forward_call(
                info, mol, n, cnt, rows, at, (weights, gains), pair, carried
            )
        new_pair, exps, mixed, hid_t, qkv_t, inverse = results[:6]
        if stage < last:
            received, inverse = tie((received, inverse))
        carried = (new_pair, exps)
        saved.append((mixed, hid_t, qkv_t, inverse))
    mixed_other = over_head(saved[1][0])

    output, first, gm_mine, gm_other, *pieces = layer_call(
        info, atoms, (saved[0][0], saved[2][0]), mixed_other, out_cot, gains, a_parts, b_parts, bits_a, bits_b
    )
    gm_received = over_head(gm_other)

    parts = [p[:2] for p in (pieces[:4], pieces[4:])]
    received = [[over_both(x, bit) for x in p[2:]] for p, bit in zip((pieces[:4], pieces[4:]), stage_bits[last])]
    send_halves = lambda parts, k: [over_both(high, bit) for (_, high), bit in zip(parts, stage_bits[k])]
    add_halves = lambda parts, received: [add(low, r) for (low, _), r in zip(parts, received)]
    carried = ()
    grads = []
    cnt = counts
    gms = (gm_mine, gm_received, gm_mine)
    for k, (mol, n, _, at) in enumerate(plan):
        if k > 0:
            if k > 1:
                parts = [halves(x) for x in add_halves(parts, received)]
            else:
                parts = [[add(x, r) for x, r in zip(*pair)] for pair in zip(parts, received)]
            cnt, parts = tie((cnt, parts))
            received = send_halves(parts, last - k)
        pair_grad, gh, gp = attend_backward_call(
            info, mol, n, cnt, gms[k], at, saved[k], weights, exps, pair_cot, carried
        )
        received, gp = tie((received, gp))
        carried = (pair_grad,)
        grads.append((gh, gp))
    bulk_keep, bulk_send = halves(jnp.concatenate(add_halves(parts, received), 1))
    gps, bulk_keep, bulk_send, gh = tie(([g[1] for g in grads], bulk_keep, bulk_send, grads[1][0]))
    hidden_received = over_head(gh)
    near, far = project_grad_call(info, [s[1] for s in saved], gps, batch_bits)
    near = add(near, over_batch(far, batch_bits[-1]))
    bulk_received = over_both(bulk_send, bits_a[nz - 1])
    for k, bit in enumerate(batch_bits[-2::-1]):
        keep, send = halves(near)
        received = over_batch(send, bit)
        near = add(keep, received)
        if k == 0:
            _, bulk_received = tie((received, bulk_received))
        elif k == 1:
            _, hidden_received = tie((received, hidden_received))
    bulk = add(bulk_keep, bulk_received)
    for bit in bits_a[: nz - 1][::-1]:
        keep, send = halves(bulk)
        bulk = add(keep, over_both(send, bit))
    qkv_grad = near[0].reshape(qkv_weight.shape).astype(F32)
    gain_part = jnp.sum(qkv_grad * qkv_weight.astype(F32), (0, 2)).reshape(2, shard)
    gain_mine = lax.dynamic_index_in_dim(gain_part, h, 0, False)
    gain_other = over_head(lax.dynamic_index_in_dim(gain_part, 1 - h, 0, False))
    gain_one_grad = (gain_mine + gain_other) / ln1_gain
    atoms_grad = last_call(atoms, gains, first, grads[0][0], grads[2][0], hidden_received)
    bulk = bulk[0].astype(F32)
    shard_rows = w_in.shape[0]
    blocks = w_in.shape[1] // dim
    in_grad = jnp.concatenate([bulk[k * shard_rows : (k + 1) * shard_rows] for k in range(blocks)], 1)
    out_grad = jnp.concatenate([bulk[blocks * shard_rows : cut, k * width : (k + 1) * width] for k in range(2)], 0)
    outer_grad = bulk[cut:]
    gain_two_grad = jnp.sum(in_grad * w_in.astype(F32), 1) / ln2_gain
    return (
        output, new_pair, atoms_grad, pair_grad, qkv_grad, out_grad,
        gain_one_grad, gain_two_grad, in_grad, outer_grad,
    )


def solution(mesh):
    rows = P(BOTH, None)
    heads = P("batch", "head", None, None)
    batch, head = mesh.shape["batch"], mesh.shape["head"]
    body = partial(body_pairs, batch=batch) if (batch, head) == (16, 2) else body_native
    return jax.shard_map(
        body,
        mesh=mesh,
        in_specs=(
            rows, heads, P("batch"), P(None, "batch", "head"), P("batch", "head"),
            P(BOTH), P(BOTH), rows, rows, rows, heads,
        ),
        out_specs=(
            rows, heads, rows, heads, P(None, "batch", "head"), P("batch", "head"),
            P(BOTH), P(BOTH), rows, rows,
        ),
        check_vma=False,
    )
```
